256 devices in a mesh: section: 8 (over z), dp: 32 (over y, x, core).
Axes of the slice: x: 4, y: 4, z: 8, core: 2. Of those that a mesh axis runs over, the one named last changes fastest.
Arguments:
- layer_input_states: bfloat16 [8, 32, 128, 8192], P('section', 'dp'), may hold values from -11 to 11, as said below
- frozen_reference_states: bfloat16 [8, 32, 128, 8192], P('section', None, None, 'dp'), may hold values from -11 to 11
- adapter_down_weight: bfloat16 [8, 16, 8192], P('section'), may hold values from -0.0625 to 0.0625
- adapter_up_weight: bfloat16 [8, 16, 8192], P('section'), may hold values from -0.1796875 to 0.1796875
- layer_norm_gain: float32 [8, 8192], P('section'), may hold values from 0.5 to 1.5
- tile_reference_position: int32 [32], replicated, may hold values from 0 to 31, each once
- tile_harmful_flag: int32 [32], P('dp'), may hold values from 0 to 1, as said below
- tile_valid_count: int32 [32], P('dp'), may hold values from 32 to 128
Outputs:
- grad_down: float32 [8, 16, 8192], P('section')
- grad_up: float32 [8, 16, 8192], P('section')
The draws below stay inside these ranges and needn't reach their ends.
Inputs may be any that keep to these rules, and one draw needn't show every extreme that they name: layer_input_states and frozen_reference_states are bounded. `tile_harmful_flag`: both harmful and retain tiles occur.
All inputs are finite; a program needn't handle non-finite values.
Results may differ from the reference program's by a relative error of at most 0.0012.
Values may be sent and summed in bfloat16 or wider, within the bound.
No kernel may reach another device: no remote copies, remote signals or barrier semaphores. Data moves between devices by JAX's collectives and lax.ppermute only.
A program may use at most 64 MiB of HBM per device.

```python
import jax
import jax.numpy as jnp
from jax import lax

MODEL_WIDTH = 8192
ADAPTER_RANK = 16
TILE = 128
ADAPTED_LAYERS = 8
TILES = 32


def shared_direction(key):
    return jax.random.truncated_normal(jax.random.fold_in(key, 11), -4.0, 4.0, (ADAPTED_LAYERS, 1, 1, MODEL_WIDTH), jnp.float32)


def residual_draw(key, salt_value):
    direction = shared_direction(key)
    sign_key = jax.random.fold_in(key, salt_value)
    noise_key = jax.random.fold_in(key, salt_value + 1)
    signs = jnp.where(jax.random.bernoulli(sign_key, 0.5, (ADAPTED_LAYERS, TILES, TILE, 1)), 1.0, -1.0)
    noise = jax.random.truncated_normal(noise_key, -4.0, 4.0, (ADAPTED_LAYERS, TILES, TILE, MODEL_WIDTH), jnp.float32)
    spread = jnp.full((ADAPTED_LAYERS, TILES, TILE, 1), 0.8, jnp.float32)
    return (signs * direction + spread * noise).astype(jnp.bfloat16)


def draw_layer_input_states(key, part):
    return residual_draw(key, 21)


def draw_frozen_reference_states(key, part):
    return residual_draw(key, 31)


def draw_tile_harmful_flag(key, part):
    labels = jax.random.randint(jax.random.fold_in(key, 41), (TILES,), 0, 2, jnp.int32)
    return labels.at[0].set(1).at[1].set(0)


def place_ends(result, rng, smallest, top_value):
    longest = result.shape.index(max(result.shape))
    spots = []
    for shift in (0, 1):
        where = [jax.random.randint(jax.random.fold_in(rng, axis), (), 0, length) for axis, length in enumerate(result.shape)]
        where[longest] = (where[longest] + shift) % result.shape[longest]
        spots.append(tuple(where))
    return result.at[spots[0]].set(smallest).at[spots[1]].set(top_value)


def shard_levels(stream_key, extent, cuts, low, largest):
    level, own = 1.0, jax.random.fold_in(stream_key, 6)
    for position, blocks in cuts:
        steps = jnp.exp(jax.random.uniform(jax.random.fold_in(own, position), (blocks,), jnp.float32, low / len(cuts), largest / len(cuts)))
        level = level * jnp.repeat(steps, extent[position] // blocks).reshape([-1 if axis == position else 1 for axis in range(len(extent))])
    return level


def centred(stream_key, extent, scale, limit, pieces=(), kind=jnp.bfloat16):
    entries = scale * jax.random.normal(stream_key, extent, jnp.float32)
    if pieces:
        entries = entries * shard_levels(stream_key, extent, pieces, -0.22, 0.18)
    return jnp.clip(entries, -limit, limit).astype(kind)


def setup_inputs(seed: int = 0) -> dict:
    streams_of = jax.random.split(jax.random.key(seed), 9)
    return {
        "layer_input_states": draw_layer_input_states(jax.random.fold_in(streams_of[8], 71), 0),
        "frozen_reference_states": draw_frozen_reference_states(jax.random.fold_in(streams_of[8], 71), 0),
        "adapter_down_weight": centred(streams_of[2], (ADAPTED_LAYERS, ADAPTER_RANK, MODEL_WIDTH), MODEL_WIDTH ** -0.5, 0.0625, ((0, 8),)),
        "adapter_up_weight": centred(streams_of[3], (ADAPTED_LAYERS, ADAPTER_RANK, MODEL_WIDTH), 0.03, 0.1796875, ((0, 8),)),
        "layer_norm_gain": jnp.clip(1.0 + 0.1 * jax.random.normal(streams_of[4], (ADAPTED_LAYERS, MODEL_WIDTH), jnp.float32), 0.5, 1.5),
        "tile_reference_position": jax.random.permutation(streams_of[5], TILES).astype(jnp.int32),
        "tile_harmful_flag": draw_tile_harmful_flag(jax.random.fold_in(streams_of[8], 71), 0),
        "tile_valid_count": place_ends(jax.random.randint(streams_of[7], (TILES,), TILE // 4, TILE + 1), jax.random.fold_in(streams_of[7], 1), TILE // 4, TILE).astype(jnp.int32),
    }


norm_eps = 1e-05
stat_eps = 1e-06
coef_reroute = 64.0
coef_retain = 1.0
loss_scale = 2048.0

def section_forward(inputs, down_projection_rows, up_projection_rows, gains):
    stream = inputs.astype(jnp.float32)
    inverse_rms = lax.rsqrt(lax.optimization_barrier(jnp.mean(stream * stream, axis=-1, keepdims=True)) + norm_eps)
    normed = (stream * inverse_rms * gains).astype(jnp.bfloat16)
    low_rank = jnp.dot(normed, down_projection_rows.T, preferred_element_type=jnp.float32).astype(jnp.bfloat16)
    output = stream + jnp.dot(low_rank, up_projection_rows, preferred_element_type=jnp.float32)
    return (stream, inverse_rms, normed, low_rank, output)

def token_stats(output, references):
    difference = output - references
    out_sq = lax.optimization_barrier(jnp.sum(output * output, axis=-1, keepdims=True))
    ref_sq = lax.optimization_barrier(jnp.sum(references * references, axis=-1, keepdims=True))
    cross_sum = lax.optimization_barrier(jnp.sum(output * references, axis=-1, keepdims=True))
    diff_sq = lax.optimization_barrier(jnp.sum(difference * difference, axis=-1, keepdims=True))
    return (out_sq, ref_sq, cross_sum, diff_sq)

def loss_grad(output, references, out_sq, ref_sq, cross_sum, diff_sq, is_harm, is_valid, weight_harm, weight_keep):
    out_norm = jnp.sqrt(out_sq + stat_eps)
    ref_norm = jnp.sqrt(ref_sq + stat_eps)
    diff_norm = jnp.sqrt(diff_sq + stat_eps)
    cosine = cross_sum / (out_norm * ref_norm)
    reroute = jnp.where(cosine > 0, references / (out_norm * ref_norm) - cosine * output / (out_sq + stat_eps), 0.0)
    retain = (output - references) / diff_norm
    return is_valid * (is_harm * weight_harm * reroute + (1.0 - is_harm) * weight_keep * retain)

def reference(layer_input_states, frozen_reference_states, adapter_down_weight, adapter_up_weight, layer_norm_gain, tile_reference_position, tile_harmful_flag, tile_valid_count):
    tokens = TILES * TILE
    positions = jnp.arange(TILE, dtype=jnp.int32)
    is_valid = (positions[None, :] < tile_valid_count[:, None]).astype(jnp.float32).reshape(tokens, 1)
    is_harm = jnp.broadcast_to(tile_harmful_flag.astype(jnp.float32)[:, None], (TILES, TILE)).reshape(tokens, 1)
    count_harm = jnp.sum(is_valid * is_harm)
    count_keep = jnp.sum(is_valid * (1.0 - is_harm))
    weight_harm = loss_scale * coef_reroute / count_harm
    weight_keep = loss_scale * coef_retain / count_keep
    incoming = jnp.zeros((tokens, MODEL_WIDTH), jnp.float32)
    grads_down = []
    grads_up = []
    for layer_position in range(ADAPTED_LAYERS - 1, -1, -1):
        down_projection_rows = adapter_down_weight[layer_position]
        up_projection_rows = adapter_up_weight[layer_position]
        gains = layer_norm_gain[layer_position]
        stream, inverse_rms, normed, low_rank, output = section_forward(layer_input_states[layer_position].reshape(tokens, MODEL_WIDTH), down_projection_rows, up_projection_rows, gains)
        references = jnp.take(frozen_reference_states[layer_position], tile_reference_position, axis=0).reshape(tokens, MODEL_WIDTH).astype(jnp.float32)
        out_sq, ref_sq, cross_sum, diff_sq = token_stats(output, references)
        gradient = loss_grad(output, references, out_sq, ref_sq, cross_sum, diff_sq, is_harm, is_valid, weight_harm, weight_keep) + incoming
        grad_bf = gradient.astype(jnp.bfloat16)
        low_grad = jnp.dot(grad_bf, up_projection_rows.T, preferred_element_type=jnp.float32).astype(jnp.bfloat16)
        grads_up.append(jnp.dot(low_rank.T, grad_bf, preferred_element_type=jnp.float32))
        grads_down.append(jnp.dot(low_grad.T, normed, preferred_element_type=jnp.float32))
        norm_grad = jnp.dot(low_grad, down_projection_rows, preferred_element_type=jnp.float32) * gains
        scaled = stream * inverse_rms
        passed = gradient + inverse_rms * (norm_grad - scaled * lax.optimization_barrier(jnp.mean(norm_grad * scaled, axis=-1, keepdims=True)))
        incoming = lax.optimization_barrier(passed.astype(jnp.bfloat16)).astype(jnp.float32)
    return (jnp.stack(grads_down[::-1]), jnp.stack(grads_up[::-1]))
```

```python
import functools

import jax
import jax.numpy as jnp
from jax import lax
from jax.experimental import pallas as pl
from jax.experimental.pallas import tpu as pltpu
from jax.sharding import Mesh
from jax.sharding import PartitionSpec as P

norm_eps = 1e-05
stat_eps = 1e-06
coef_reroute = 64.0
coef_retain = 1.0
loss_scale = 2048.0

SEC = "section"
CHIPS = ("y", "x")
DP = ("y", "x", "core")
f32 = jnp.float32
bf16 = jnp.bfloat16


def nt(left, right):
    return lax.dot_general(left, right, (((1,), (1,)), ((), ())), preferred_element_type=f32)


def tn(left, right):
    return lax.dot_general(left, right, (((0,), (0,)), ((), ())), preferred_element_type=f32)


def nn(left, right):
    return lax.dot_general(left, right, (((1,), (0,)), ((), ())), preferred_element_type=f32)


def split2(value):
    hi = value.astype(bf16)
    lo = (value - hi.astype(f32)).astype(bf16)
    return hi, lo


def ring_gather(block, axis):
    n = lax.axis_size(axis)
    up = [(i, (i + 1) % n) for i in range(n)]
    down = [(i, (i - 1) % n) for i in range(n)]
    found = [None] * n
    found[0] = block
    fwd = bwd = block
    for k in range(1, n // 2 + 1):
        fwd = lax.ppermute(fwd, axis, up)
        found[k] = fwd
        if k < n - n // 2:
            bwd = lax.ppermute(bwd, axis, down)
            found[n - k] = bwd
    return found


def total_over_dp(value):
    for axis in ("core", "x", "y"):
        n = lax.axis_size(axis)
        step = 1
        while step < n:
            pairs = [(i, (i + step) % n) for i in range(n)]
            value = value + lax.ppermute(value, axis, pairs)
            step *= 2
    return value


def solve_kernel(layers, rank, width, own_ref, *refs):
    packs = refs[: layers - 1]
    lrt_ref, irms_ref, out_ref, acc = refs[layers - 1 :]
    lanes = own_ref.shape[1]
    rows = layers * rank
    acc[...] = jnp.zeros_like(acc)
    acc[0:rank, :] = own_ref[rows - rank : rows, :]
    for j in range(1, layers):
        low = rank * (layers - 1 - j)
        acc[0 : rank * (j + 1), :] += packs[j - 1][low:rows, 0:lanes].astype(f32)
    for j in range(layers - 1, 0, -1):
        low = rank * (layers - 1 - j)
        grad = acc[rank * j : rank * (j + 1), :].astype(bf16)
        k = layers - j
        lrt = lrt_ref[rank * k : rank * (k + 1), :].astype(f32)
        mean = jnp.sum(grad.astype(f32) * lrt, axis=0, keepdims=True) * (1.0 / width)
        irms = irms_ref[k : k + 1, :]
        w_hi = packs[j - 1][rows : rows + rank, 0:rows][:, low : rows - rank]
        w_lo = packs[j - 1][rows : rows + rank, rows : 2 * rows][:, low : rows - rank]
        term = tn(w_hi, grad) + tn(w_lo, grad)
        scaled_up = packs[j - 1][low : rows - rank, lanes : 2 * lanes].astype(f32)
        acc[0 : rank * j, :] += irms * (term - mean * scaled_up)
    out_ref[...] = acc[0:rank, :]


def solve(width, rank, own, packs, lrt, irms):
    layers = len(packs) + 1
    return pl.pallas_call(
        functools.partial(solve_kernel, layers, rank, width),
        out_shape=jax.ShapeDtypeStruct((rank, own.shape[1]), f32),
        scratch_shapes=[pltpu.VMEM((layers * rank, own.shape[1]), f32)],
        name="solve",
    )(own, *packs, lrt, irms)


def shards(
    layer_input_states,
    frozen_reference_states,
    adapter_down_weight,
    adapter_up_weight,
    layer_norm_gain,
    tile_reference_position,
    tile_harmful_flag,
    tile_valid_count,
):
    stream_bf = layer_input_states[0, 0]
    tokens, width = stream_bf.shape
    down = adapter_down_weight[0]
    up = adapter_up_weight[0]
    gains = layer_norm_gain[0]
    rank = up.shape[0]
    layers = lax.axis_size(SEC)
    core = lax.axis_index("core")
    cores = lax.axis_size("core")
    chips = lax.axis_size("y") * lax.axis_size("x")
    half = width // cores
    swap = [(i, (i + 1) % cores) for i in range(cores)]

    ordered = frozen_reference_states[0].at[tile_reference_position].get(mode="promise_in_bounds", unique_indices=True)
    fetched = lax.all_to_all(ordered, DP, split_axis=0, concat_axis=2, tiled=True)
    refs = fetched.reshape(tokens, width).astype(f32)

    flag = tile_harmful_flag[0].astype(f32)
    valid = tile_valid_count[0].astype(f32)
    lane = lax.broadcasted_iota(jnp.int32, (8, 128), 1)
    counts = jnp.where(lane == 0, flag * valid, jnp.where(lane == 1, (1.0 - flag) * valid, 0.0))
    counts = total_over_dp(counts)
    weight_harm = loss_scale * coef_reroute / counts[0, 0]
    weight_keep = loss_scale * coef_retain / counts[0, 1]

    stream = stream_bf.astype(f32)
    inverse_rms = lax.rsqrt(jnp.mean(stream * stream, axis=-1, keepdims=True) + norm_eps)
    normed = (stream * inverse_rms * gains).astype(bf16)
    lrt_own = nt(down, normed).astype(bf16)
    low_rank = nt(normed, down).astype(bf16)
    output = stream + nn(low_rank, up)
    irms_row = inverse_rms.reshape(1, tokens)
    dg = down.astype(f32) * gains
    dg_hi, dg_lo = split2(dg)

    up_half = lax.dynamic_slice_in_dim(up, core * half, half, axis=1)
    gathered = ring_gather(up_half, SEC)
    up_mine = jnp.concatenate(gathered[::-1], axis=0)
    up_other = lax.ppermute(up_mine, "core", swap)
    up_all = jnp.concatenate(
        [jnp.where(core == 0, up_mine, up_other), jnp.where(core == 0, up_other, up_mine)], axis=1
    )
    side = jnp.concatenate([lrt_own.astype(f32), jnp.broadcast_to(irms_row, (8, tokens))], axis=0)
    sides = ring_gather(side, SEC)
    lrt = jnp.concatenate([s[:rank] for s in sides], axis=0).astype(bf16)
    irms_all = jnp.concatenate([s[rank : rank + 1] for s in sides], axis=0)

    scaled_up = nt(up_all, stream_bf) * irms_row
    w_hi, w_lo = split2(nt(dg_hi, up_all) + nt(dg_lo, up_all))

    difference = output - refs
    out_sq = jnp.sum(output * output, axis=-1, keepdims=True)
    ref_sq = jnp.sum(refs * refs, axis=-1, keepdims=True)
    cross_sum = jnp.sum(output * refs, axis=-1, keepdims=True)
    diff_sq = jnp.sum(difference * difference, axis=-1, keepdims=True)
    out_norm = jnp.sqrt(out_sq + stat_eps)
    ref_norm = jnp.sqrt(ref_sq + stat_eps)
    diff_norm = jnp.sqrt(diff_sq + stat_eps)
    cosine = cross_sum / (out_norm * ref_norm)
    is_valid = lax.broadcasted_iota(jnp.int32, (tokens, 1), 0) < tile_valid_count[0]
    harm = tile_harmful_flag[0] == 1
    on_harm = jnp.where(is_valid & harm & (cosine > 0), weight_harm, 0.0)
    on_keep = jnp.where(is_valid & jnp.logical_not(harm), weight_keep, 0.0)
    coef_ref = on_harm / (out_norm * ref_norm)
    coef_out = -on_harm * cosine / (out_sq + stat_eps)
    coef_diff = on_keep / diff_norm
    own = (coef_ref * refs + coef_out * output + coef_diff * difference).astype(bf16)

    own_up = nt(up_all, own)
    pack = jnp.concatenate(
        [
            jnp.concatenate([own_up.astype(bf16), scaled_up.astype(bf16)], axis=1),
            jnp.concatenate([w_hi, w_lo], axis=1),
        ],
        axis=0,
    )
    packs = [lax.ppermute(pack, SEC, [(t, t - j) for t in range(j, layers)]) for j in range(1, layers)]
    low_grad_t = solve(width, rank, own_up, packs, lrt, irms_all).astype(bf16)

    low_grad_f = low_grad_t.astype(f32)
    mean = jnp.sum(low_grad_f * lrt[:rank].astype(f32), axis=0, keepdims=True) * (1.0 / width)
    below = (lax.broadcasted_iota(jnp.int32, (layers * rank, 1), 0) >= rank).astype(f32)
    lrt_f = lrt.astype(f32) * below
    coef_stream = (lrt_f * (-irms_row * irms_row * mean)).astype(bf16)
    k_hi, k_lo = split2(nt(lrt_f.astype(bf16), (low_grad_f * irms_row).astype(bf16)))
    part_up = (
        nn(lrt, own) + nn(coef_stream, stream_bf) + nn(k_hi, dg_hi) + nn(k_hi, dg_lo) + nn(k_lo, dg_hi)
    )
    part_down = nn(low_grad_t, normed)
    part = jnp.concatenate([part_up, part_down], axis=0)

    lower, upper = part[:, :half], part[:, half:]
    kept = jnp.where(core == 0, lower, upper)
    given = jnp.where(core == 0, upper, lower)
    chip = (kept + lax.ppermute(given, "core", swap)).astype(bf16)
    rows = part.shape[0]
    blocks = chip.reshape(rows, chips, half // chips).transpose(1, 0, 2)
    blocks = lax.all_to_all(blocks, CHIPS, 0, 0, tiled=True)
    summed = jnp.sum(blocks.astype(f32), axis=0)

    grad_up = summed[:rank]
    for k in range(1, layers):
        grad_up = grad_up + lax.ppermute(
            summed[rank * k : rank * (k + 1)], SEC, [(t, t - k) for t in range(k, layers)]
        )
    final = jnp.concatenate([summed[layers * rank :], grad_up], axis=0)

    wide = lax.all_to_all(jnp.broadcast_to(final, (chips,) + final.shape), CHIPS, 0, 0, tiled=True)
    mine = wide.transpose(1, 0, 2).reshape(2 * rank, half)
    other = lax.ppermute(mine, "core", swap)
    full = jnp.concatenate([jnp.where(core == 0, mine, other), jnp.where(core == 0, other, mine)], axis=1)
    return (full[None, :rank], full[None, rank:])


def solution(mesh):
    layers, dp = mesh.devices.shape
    cores = 2
    side = round((dp // cores) ** 0.5)
    mesh4 = Mesh(mesh.devices.reshape(layers, side, side, cores), (SEC,) + DP)
    return jax.shard_map(
        shards,
        mesh=mesh4,
        in_specs=(
            P(SEC, DP, None, None),
            P(SEC, None, None, DP),
            P(SEC, None, None),
            P(SEC, None, None),
            P(SEC, None),
            P(),
            P(DP),
            P(DP),
        ),
        out_specs=(P(SEC, None, None), P(SEC, None, None)),
        check_vma=False,
    )
```

```python
import functools

import jax
import jax.numpy as jnp
from jax import lax
from jax.experimental import pallas as pl
from jax.experimental.pallas import tpu as pltpu
from jax.sharding import Mesh
from jax.sharding import PartitionSpec as P

norm_eps = 1e-05
stat_eps = 1e-06
coef_reroute = 64.0
coef_retain = 1.0
loss_scale = 2048.0

SEC = "section"
CHIPS = ("y", "x")
DP = ("y", "x", "core")
f32 = jnp.float32
bf16 = jnp.bfloat16


def nt(left, right):
    return lax.dot_general(left, right, (((1,), (1,)), ((), ())), preferred_element_type=f32)


def tn(left, right):
    return lax.dot_general(left, right, (((0,), (0,)), ((), ())), preferred_element_type=f32)


def nn(left, right):
    return lax.dot_general(left, right, (((1,), (0,)), ((), ())), preferred_element_type=f32)


def split2(value):
    hi = value.astype(bf16)
    lo = (value - hi.astype(f32)).astype(bf16)
    return hi, lo


def ring_gather(block, axis):
    n = lax.axis_size(axis)
    up = [(i, (i + 1) % n) for i in range(n)]
    down = [(i, (i - 1) % n) for i in range(n)]
    found = [None] * n
    found[0] = block
    fwd = bwd = block
    for k in range(1, n // 2 + 1):
        fwd = lax.ppermute(fwd, axis, up)
        found[k] = fwd
        if k < n - n // 2:
            bwd = lax.ppermute(bwd, axis, down)
            found[n - k] = bwd
    return found

def vmem():
    return pl.BlockSpec(memory_space=pltpu.VMEM)


def smem():
    return pl.BlockSpec(memory_space=pltpu.SMEM)


def hbm():
    return pl.BlockSpec(memory_space=pl.ANY)


def params(mib=48):
    return pltpu.CompilerParams(vmem_limit_bytes=mib << 20)


INFO = 8


def order_kernel(position_ref, info_ref, held_ref, out_ref, tile_sem, info_sem):
    tiles, tokens = held_ref.shape[0], held_ref.shape[1]
    copies = []
    for i in range(tiles):
        copies.append(
            pltpu.make_async_copy(held_ref.at[position_ref[i]], out_ref.at[i, pl.ds(0, tokens)], tile_sem.at[i])
        )
        copies.append(pltpu.make_async_copy(info_ref, out_ref.at[i, pl.ds(tokens, INFO)], info_sem.at[i]))
    for copy in copies:
        copy.start()
    for copy in copies:
        copy.wait()


def order(position, info, held):
    tiles, tokens, width = held.shape
    return pl.pallas_call(
        order_kernel,
        out_shape=jax.ShapeDtypeStruct((tiles, tokens + INFO, width), held.dtype),
        in_specs=[smem(), vmem(), hbm()],
        out_specs=hbm(),
        scratch_shapes=[pltpu.SemaphoreType.DMA((tiles,)), pltpu.SemaphoreType.DMA((tiles,))],
        name="order",
    )(position, info, held)


def fold(value):
    lanes = 128
    total = value[:, :lanes]
    for i in range(1, value.shape[1] // lanes):
        total = total + value[:, i * lanes : (i + 1) * lanes]
    return total


def own_kernel(meta_ref, refs_ref, output_ref, mine_ref, other_ref, own_ref, proj_ref):
    core, flag, valid = meta_ref[0], meta_ref[1], meta_ref[2]
    tiles, padded, chunk = refs_ref.shape
    tokens = padded - INFO
    half = mine_ref.shape[1]
    per_half = half // chunk
    rows = 32

    info = refs_ref[0, tokens:, :128].astype(f32)
    for i in range(1, tiles):
        info = info + refs_ref[i, tokens:, :128].astype(f32)
    weight_harm = (loss_scale * coef_reroute) / info[0:1, 0:1]
    weight_keep = (loss_scale * coef_retain) / info[1:2, 0:1]

    def stats(terms, count):
        found = []
        for low in range(0, tokens, rows):

            def step(i, acc, low=low):
                out = output_ref[low : low + rows, pl.ds(pl.multiple_of(i * chunk, chunk), chunk)]
                ref = refs_ref[i, low : low + rows, :].astype(f32)
                return tuple(a + fold(v) for a, v in zip(acc, terms(out, ref)))

            zero = jnp.zeros((rows, 128), f32)
            acc = lax.fori_loop(0, tiles, step, (zero,) * count, unroll=4)
            found.append([jnp.sum(a, axis=1, keepdims=True) for a in acc])
        return [jnp.concatenate([f[i] for f in found], axis=0) for i in range(count)]

    is_valid = lax.broadcasted_iota(jnp.int32, (tokens, 1), 0) < valid

    def finish(make):
        total = jnp.zeros(proj_ref.shape[1:], f32)
        for base, weights in ((core, mine_ref), (1 - core, other_ref)):

            def step(i, acc, base=base, weights=weights):
                j = base * per_half + i
                columns = pl.ds(pl.multiple_of(j * chunk, chunk), chunk)
                own = make(output_ref[:, columns], refs_ref[j, :tokens, :].astype(f32)).astype(bf16)
                own_ref[:, columns] = own
                return acc + nt(weights[:, pl.ds(pl.multiple_of(i * chunk, chunk), chunk)], own)

            total = lax.fori_loop(0, per_half, step, total, unroll=2)
        total = total.astype(bf16)
        for i in range(proj_ref.shape[0]):
            proj_ref[i] = total

    @pl.when(flag == 1)
    def _():
        out_sq, ref_sq, cross = stats(lambda o, r: (o * o, r * r, o * r), 3)
        out_norm = jnp.sqrt(out_sq + stat_eps)
        ref_norm = jnp.sqrt(ref_sq + stat_eps)
        cosine = cross / (out_norm * ref_norm)
        weight = jnp.where(is_valid & (cosine > 0), weight_harm, 0.0)
        coef_ref = weight / (out_norm * ref_norm)
        coef_out = weight * cosine / (out_sq + stat_eps)
        finish(lambda o, r: coef_ref * r - coef_out * o)

    @pl.when(flag != 1)
    def _():
        (diff_sq,) = stats(lambda o, r: ((o - r) * (o - r),), 1)
        coef = jnp.where(is_valid, weight_keep, 0.0) / jnp.sqrt(diff_sq + stat_eps)
        finish(lambda o, r: coef * (o - r))


def own_gradient(meta, refs, output, mine, other, layers):
    tokens = output.shape[0]
    return pl.pallas_call(
        own_kernel,
        out_shape=(
            jax.ShapeDtypeStruct(output.shape, bf16),
            jax.ShapeDtypeStruct((layers, mine.shape[0], tokens), bf16),
        ),
        in_specs=[smem()] + [vmem()] * 4,
        out_specs=(vmem(), vmem()),
        compiler_params=params(),
        name="own",
    )(meta, refs, output, mine, other)


def solve_kernel(width, rank, me_ref, own_ref, side_ref, low_ref, lrt_ref, coef_ref, k_ref, acc):
    me = me_ref[0]
    layers, rows, _ = own_ref.shape
    acc[...] = jnp.zeros_like(acc)
    for j in range(layers):

        @pl.when(me + j < layers)
        def _(j=j):
            low = rank * (layers - 1 - j)
            acc[0 : rank * (j + 1), :] += own_ref[me + j, low:rows, :].astype(f32)

    def inverse_rms(t):
        return side_ref[t, rows + 3 * rank : rows + 3 * rank + 1, :].astype(f32) + side_ref[
            t, rows + 3 * rank + 1 : rows + 3 * rank + 2, :
        ].astype(f32)

    def mean_of(grad, t):
        lrt = side_ref[t, rows : rows + rank, :].astype(f32)
        return jnp.sum(grad.astype(f32) * lrt, axis=0, keepdims=True) * (1.0 / width)

    for j in range(layers - 1, 0, -1):

        @pl.when(me + j < layers)
        def _(j=j):
            t = me + j
            low = rank * (layers - 1 - j)
            grad = acc[rank * j : rank * (j + 1), :].astype(bf16)
            mean = mean_of(grad, t)
            w_hi = side_ref[t, rows + rank : rows + 2 * rank, :]
            w_lo = side_ref[t, rows + 2 * rank : rows + 3 * rank, :]
            term = tn(w_hi, grad) + tn(w_lo, grad)
            scaled_up = side_ref[t, low : rows - rank, :].astype(f32)
            acc[0 : rank * j, :] += inverse_rms(t) * (term[low : rows - rank, :] - mean * scaled_up)

    grad = acc[0:rank, :].astype(bf16)
    low_ref[...] = grad
    irms = inverse_rms(me)
    mean = mean_of(grad, me)
    lrt = side_ref[:, rows : rows + rank, :].reshape(layers * rank, -1)
    layer = lax.broadcasted_iota(jnp.int32, lrt.shape, 0) // rank
    lrt_f = lrt.astype(f32)
    lrt_ref[...] = jnp.where(layer <= me, lrt_f, 0.0).astype(bf16)
    below = jnp.where(layer < me, lrt_f, 0.0)
    coef_ref[...] = (below * (-irms * irms * mean)).astype(bf16)
    k_hi, k_lo = split2(nt(below.astype(bf16), (grad.astype(f32) * irms).astype(bf16)))
    k_ref[0] = k_hi
    k_ref[1] = k_lo


def solve(width, rank, me, own, side):
    layers, rows, tokens = own.shape
    return pl.pallas_call(
        functools.partial(solve_kernel, width, rank),
        out_shape=(
            jax.ShapeDtypeStruct((rank, tokens), bf16),
            jax.ShapeDtypeStruct((rows, tokens), bf16),
            jax.ShapeDtypeStruct((rows, tokens), bf16),
            jax.ShapeDtypeStruct((2, rows, rank), bf16),
        ),
        in_specs=[smem(), vmem(), vmem()],
        out_specs=(vmem(),) * 4,
        scratch_shapes=[pltpu.VMEM((rows, tokens), f32)],
        compiler_params=params(),
        name="solve",
    )(me, own, side)


def part_kernel(start_ref, low_ref, lrt_ref, coef_ref, k_ref, own_ref, stream_ref, normed_ref, dg_ref, out_ref):
    start = start_ref[0]
    chunks, _, chunk = out_ref.shape
    rows = lrt_ref.shape[0]

    def step(i, carry):
        columns = pl.ds(pl.multiple_of(start + i * chunk, chunk), chunk)
        dg_hi, dg_lo = dg_ref[0, :, columns], dg_ref[1, :, columns]
        out_ref[i, :rows, :] = (
            nn(lrt_ref[...], own_ref[:, columns])
            + nn(coef_ref[...], stream_ref[:, columns])
            + nn(k_ref[0], dg_hi)
            + nn(k_ref[0], dg_lo)
            + nn(k_ref[1], dg_hi)
        )
        out_ref[i, rows:, :] = nn(low_ref[...], normed_ref[:, columns])
        return carry

    lax.fori_loop(0, chunks, step, 0)


def part(start, chunks, chunk, low, lrt, coef, k, own, stream, normed, dg):
    return pl.pallas_call(
        part_kernel,
        out_shape=jax.ShapeDtypeStruct((chunks, lrt.shape[0] + low.shape[0], chunk), f32),
        in_specs=[smem()] + [vmem()] * 8,
        out_specs=vmem(),
        compiler_params=params(),
        name="part",
    )(start, low, lrt, coef, k, own, stream, normed, dg)


def shards(
    layer_input_states,
    frozen_reference_states,
    adapter_down_weight,
    adapter_up_weight,
    layer_norm_gain,
    tile_reference_position,
    tile_harmful_flag,
    tile_valid_count,
):
    tokens, width = layer_input_states.shape[2:]
    rank = adapter_up_weight.shape[1]
    layers = lax.axis_size(SEC)
    me = lax.axis_index(SEC)
    core = lax.axis_index("core")
    cores = lax.axis_size("core")
    chips = lax.axis_size("y") * lax.axis_size("x")
    half = width // cores
    chunk = half // chips
    swap = [(i, (i + 1) % cores) for i in range(cores)]

    flag, valid = tile_harmful_flag[0], tile_valid_count[0]
    row = lax.broadcasted_iota(jnp.int32, (INFO, chunk), 0)
    info = jnp.where((row == 0) & (flag == 1), valid, jnp.where((row == 1) & (flag != 1), valid, 0))
    ordered = order(tile_reference_position, info.astype(bf16), frozen_reference_states[0])
    refs = lax.all_to_all(ordered, DP, split_axis=0, concat_axis=0, tiled=True)
    ordered, stream_bf, down, up, gains = lax.optimization_barrier(
        (ordered, layer_input_states[0, 0], adapter_down_weight[0], adapter_up_weight[0], layer_norm_gain[0])
    )

    up_half = lax.dynamic_slice_in_dim(up, core * half, half, axis=1)
    up_mine = jnp.concatenate(ring_gather(up_half, SEC)[::-1], axis=0)
    up_other = lax.ppermute(up_mine, "core", swap)

    stream = stream_bf.astype(f32)
    inverse_rms = lax.rsqrt(jnp.mean(stream * stream, axis=-1, keepdims=True) + norm_eps)
    normed = (stream * inverse_rms * gains).astype(bf16)
    lrt = nt(down, normed).astype(bf16)
    output = stream + tn(lrt, up)
    irms_row = inverse_rms.reshape(1, tokens)
    dg = jnp.stack(split2(down.astype(f32) * gains))

    def halves(value):
        return (
            lax.dynamic_slice_in_dim(value, core * half, half, axis=1),
            lax.dynamic_slice_in_dim(value, (1 - core) * half, half, axis=1),
        )

    stream_mine, stream_other = halves(stream_bf)
    hi_mine, hi_other = halves(dg[0])
    lo_mine, lo_other = halves(dg[1])
    scaled_up = (nt(up_mine, stream_mine) + nt(up_other, stream_other)) * irms_row
    w = nt(hi_mine, up_mine) + nt(lo_mine, up_mine) + nt(hi_other, up_other) + nt(lo_other, up_other)
    w_hi, w_lo = split2(w)
    irms_hi, irms_lo = split2(irms_row)
    side = jnp.concatenate(
        [scaled_up.astype(bf16), lrt, w_hi, w_lo, irms_hi, irms_lo, jnp.zeros((14, tokens), bf16)], axis=0
    )
    sides = lax.all_to_all(jnp.broadcast_to(side, (layers,) + side.shape), SEC, 0, 0, tiled=True)

    meta = jnp.stack([core, flag, valid]).astype(jnp.int32)
    own, own_up = own_gradient(meta, refs, output, up_mine, up_other, layers)
    own_up = lax.all_to_all(own_up, SEC, 0, 0, tiled=True)
    low, lrt_all, coef, k = solve(width, rank, me[None], own_up, sides)

    given = part(((1 - core) * half)[None], chips, chunk, low, lrt_all, coef, k, own, stream_bf, normed, dg)
    received = lax.ppermute(given, "core", swap)
    kept = part((core * half)[None], chips, chunk, low, lrt_all, coef, k, own, stream_bf, normed, dg)
    blocks = lax.all_to_all((kept + received).astype(bf16), CHIPS, 0, 0, tiled=True)
    summed = jnp.sum(blocks.astype(f32), axis=0)

    by_layer = lax.all_to_all(summed[: layers * rank].reshape(layers, rank, chunk), SEC, 0, 0, tiled=True)
    final = jnp.concatenate([summed[layers * rank :], jnp.sum(by_layer, axis=0)], axis=0)

    wide = lax.all_to_all(jnp.broadcast_to(final, (chips,) + final.shape), CHIPS, 0, 0, tiled=True)
    mine = wide.transpose(1, 0, 2).reshape(2 * rank, half)
    other = lax.ppermute(mine, "core", swap)
    full = jnp.concatenate([jnp.where(core == 0, mine, other), jnp.where(core == 0, other, mine)], axis=1)
    return (full[None, :rank], full[None, rank:])


def solution(mesh):
    layers, dp = mesh.devices.shape
    cores = 2
    side = round((dp // cores) ** 0.5)
    mesh4 = Mesh(mesh.devices.reshape(layers, side, side, cores), (SEC,) + DP)
    return jax.shard_map(
        shards,
        mesh=mesh4,
        in_specs=(
            P(SEC, DP, None, None),
            P(SEC, None, None, DP),
            P(SEC, None, None),
            P(SEC, None, None),
            P(SEC, None),
            P(),
            P(DP),
            P(DP),
        ),
        out_specs=(P(SEC, None, None), P(SEC, None, None)),
        check_vma=False,
    )
```

```python
import functools

import jax
import jax.numpy as jnp
from jax import lax
from jax.experimental import pallas as pl
from jax.experimental.pallas import tpu as pltpu
from jax.sharding import Mesh
from jax.sharding import PartitionSpec as P

norm_eps = 1e-05
stat_eps = 1e-06
coef_reroute = 64.0
coef_retain = 1.0
loss_scale = 2048.0

SEC = "section"
CHIPS = ("y", "x")
DP = ("y", "x", "core")
f32 = jnp.float32
bf16 = jnp.bfloat16


def nt(left, right):
    return lax.dot_general(left, right, (((1,), (1,)), ((), ())), preferred_element_type=f32)


def tn(left, right):
    return lax.dot_general(left, right, (((0,), (0,)), ((), ())), preferred_element_type=f32)


def nn(left, right):
    return lax.dot_general(left, right, (((1,), (0,)), ((), ())), preferred_element_type=f32)


def split2(value):
    hi = value.astype(bf16)
    lo = (value - hi.astype(f32)).astype(bf16)
    return hi, lo


def ring_gather(block, axis, gate):
    n = lax.axis_size(axis)
    up = [(i, (i + 1) % n) for i in range(n)]
    down = [(i, (i - 1) % n) for i in range(n)]
    found = [None] * n
    found[0] = block
    fwd = bwd = block
    for k in range(1, n // 2 + 1):
        fwd = lax.ppermute(fwd, axis, up)
        found[k] = fwd
        if k < n - n // 2:
            bwd = lax.ppermute(bwd, axis, down)
            found[n - k] = bwd
        if k == 1:
            fwd, bwd, _ = lax.optimization_barrier((fwd, bwd, gate))
            found[1], found[n - 1] = fwd, bwd
    return found


def params(mib=63):
    return pltpu.CompilerParams(vmem_limit_bytes=mib << 20)


def smem():
    return pl.BlockSpec(memory_space=pltpu.SMEM)


def in_place():
    return pl.BlockSpec(memory_space=pl.ANY)


def vmem():
    return pl.BlockSpec(memory_space=pltpu.VMEM)


def call(kernel, name, out_shape, scalars, arrays, scratch=()):
    count, total = len(scalars), len(arrays)
    outs = len(out_shape)

    def body(*refs):
        held = refs[count : count + total]
        first = count + total + outs
        buffers, sems = refs[first : first + total], refs[first + total : first + 2 * total]
        kernel(*refs[:count], *zip(held, buffers, sems), *refs[count + total : first], *refs[first + 2 * total :])

    return pl.pallas_call(
        body,
        out_shape=out_shape,
        in_specs=[smem()] * count + [in_place()] * total,
        out_specs=[vmem()] * outs,
        scratch_shapes=[pltpu.VMEM(a.shape, a.dtype) for a in arrays]
        + [pltpu.SemaphoreType.DMA((PIECES,)) for _ in arrays]
        + list(scratch),
        compiler_params=params(),
        name=name,
    )(*scalars, *arrays)


PIECES = 8


def whole(item):
    held, buffer, sem = item
    return pltpu.make_async_copy(held, buffer, sem.at[0])


def columns_piece(item, i, start, width):
    held, buffer, sem = item
    where = (slice(None),) * (len(held.shape) - 1) + (pl.ds(start, width),)
    return pltpu.make_async_copy(held.at[where], buffer.at[where], sem.at[i])


def leading_piece(item, i, start, count):
    held, buffer, sem = item
    return pltpu.make_async_copy(held.at[pl.ds(start, count)], buffer.at[pl.ds(start, count)], sem.at[i])


INFO = 8


def order_kernel(position_ref, meta_ref, held_ref, out_ref, buffer, in_sem, out_sem):
    tiles, tokens, width = held_ref.shape
    loads = [
        pltpu.make_async_copy(held_ref.at[position_ref[i]], buffer.at[i, pl.ds(0, tokens)], in_sem.at[i])
        for i in range(tiles)
    ]
    for load in loads:
        load.start()
    flag, valid = meta_ref[1], meta_ref[2]
    row = lax.broadcasted_iota(jnp.int32, (INFO, width), 0)
    here = ((row == 0) & (flag == 1)) | ((row == 1) & (flag != 1))
    info = jnp.where(here, valid, 0).astype(f32).astype(bf16)
    stores = []
    for i in range(tiles):
        buffer[i, tokens:, :] = info
        loads[i].wait()
        stores.append(pltpu.make_async_copy(buffer.at[i], out_ref.at[i], out_sem.at[i]))
        stores[-1].start()
    for store in stores:
        store.wait()


def order(position, meta, held):
    tiles, tokens, width = held.shape
    shape = (tiles, tokens + INFO, width)
    return pl.pallas_call(
        order_kernel,
        out_shape=jax.ShapeDtypeStruct(shape, held.dtype),
        in_specs=[smem(), smem(), in_place()],
        out_specs=in_place(),
        scratch_shapes=[
            pltpu.VMEM(shape, held.dtype),
            pltpu.SemaphoreType.DMA((tiles,)),
            pltpu.SemaphoreType.DMA((tiles,)),
        ],
        compiler_params=params(),
        name="order",
    )(position, meta, held)


def fold(value):
    lanes = 128
    total = value[:, :lanes]
    for i in range(1, value.shape[1] // lanes):
        total = total + value[:, i * lanes : (i + 1) * lanes]
    return total


def forward_kernel(stream_in, down_in, gain_in, normed_ref, lrt_ref, irms_ref, dg_ref):
    stream_ref, down_ref, gain_ref = stream_in[1], down_in[1], gain_in[1]
    tokens, width = stream_ref.shape
    piece = width // PIECES
    loads = [columns_piece(stream_in, i, i * piece, piece) for i in range(PIECES)]
    for load in loads:
        load.start()
    whole(down_in).start()
    whole(gain_in).start()
    total = jnp.zeros((tokens, 128), f32)
    for i in range(PIECES):
        loads[i].wait()
        for low in range(i * piece, (i + 1) * piece, 256):
            x = stream_ref[:, low : low + 256].astype(f32)
            total = total + fold(x * x)
    irms = lax.rsqrt(jnp.sum(total, axis=1, keepdims=True) * (1.0 / width) + norm_eps)
    irms_ref[...] = jnp.broadcast_to(irms, (tokens, 128)).T[:8, :]
    whole(down_in).wait()
    whole(gain_in).wait()
    chunk = min(512, piece)

    def norm(i, acc):
        columns = pl.ds(pl.multiple_of(i * chunk, chunk), chunk)
        gain = gain_ref[:, columns]
        normed = (stream_ref[:, columns].astype(f32) * irms * gain).astype(bf16)
        normed_ref[:, columns] = normed
        down = down_ref[:, columns]
        hi, lo = split2(down.astype(f32) * gain)
        dg_ref[0, :, columns] = hi
        dg_ref[1, :, columns] = lo
        return acc + nt(down, normed)

    rank = down_ref.shape[0]
    low_rank = lax.fori_loop(0, width // chunk, norm, jnp.zeros((rank, tokens), f32), unroll=2)
    lrt_ref[...] = low_rank.astype(bf16)


def forward(stream, down, gain):
    rank = down.shape[0]
    tokens, width = stream.shape
    return call(
        forward_kernel,
        "forward",
        (
            jax.ShapeDtypeStruct((tokens, width), bf16),
            jax.ShapeDtypeStruct((rank, tokens), bf16),
            jax.ShapeDtypeStruct((8, tokens), f32),
            jax.ShapeDtypeStruct((2, rank, width), bf16),
        ),
        (),
        (stream, down, gain),
    )


def side_kernel(count, meta_ref, stream_in, dg_in, lrt_in, irms_in, *refs):
    mine, other, out_ref = refs[:count], refs[count : 2 * count], refs[2 * count]
    core = meta_ref[0]
    rank, half = mine[0][1].shape
    tokens = stream_in[1].shape[0]
    rows = count * rank
    chunk = min(1024, half)
    for item in (*mine, stream_in, dg_in, *other, lrt_in, irms_in):
        whole(item).start()
    for item in (*mine, stream_in, dg_in):
        whole(item).wait()
    stream_ref, dg_ref = stream_in[1], dg_in[1]
    total = jnp.zeros((rows, tokens + 2 * rank), f32)
    for base, blocks in ((core, mine), (1 - core, other)):
        if blocks is other:
            for item in other:
                whole(item).wait()

        def step(i, acc, base=base, blocks=blocks):
            local = pl.ds(pl.multiple_of(i * chunk, chunk), chunk)
            columns = pl.ds(pl.multiple_of(base * half + i * chunk, chunk), chunk)
            up = jnp.concatenate([b[1][:, local] for b in blocks], axis=0)
            right = jnp.concatenate([stream_ref[:, columns], dg_ref[0, :, columns], dg_ref[1, :, columns]], axis=0)
            return acc + nt(up, right)

        total = lax.fori_loop(0, half // chunk, step, total, unroll=2)
    whole(lrt_in).wait()
    whole(irms_in).wait()
    irms = irms_in[1][0:1, :]
    scaled_up = (total[:, :tokens] * irms).astype(bf16)
    w = total[:, tokens : tokens + rank] + total[:, tokens + rank :]
    w = jnp.concatenate([w, jnp.zeros((rows, 128 - rank), f32)], axis=1).T[:rank, :]
    w_hi, w_lo = split2(w)
    irms_hi = irms.astype(bf16).astype(f32)
    row = lax.broadcasted_iota(jnp.int32, (rank, tokens), 0)
    last = jnp.where(row == 0, irms_hi, jnp.where(row == 1, irms - irms_hi, 0.0)).astype(bf16)
    for i in range(out_ref.shape[0]):
        out_ref[i, :rows, :] = scaled_up
        out_ref[i, rows : rows + rank, :] = lrt_in[1][...]
        out_ref[i, rows + rank : rows + 2 * rank, :] = w_hi
        out_ref[i, rows + 2 * rank : rows + 3 * rank, :] = w_lo
        out_ref[i, rows + 3 * rank :, :] = last


def side_of(meta, stream, dg, lrt, irms, mine, other):
    layers = len(mine)
    rank = lrt.shape[0]
    (side,) = call(
        functools.partial(side_kernel, layers),
        "side",
        (jax.ShapeDtypeStruct((layers, (layers + 4) * rank, stream.shape[0]), bf16),),
        (meta,),
        (stream, dg, lrt, irms, *mine, *other),
    )
    return side


def own_kernel(count, meta_ref, refs_in, stream_in, up_in, lrt_in, *refs):
    mine, other, own_ref, proj_ref, output_ref = (
        refs[:count],
        refs[count : 2 * count],
        refs[2 * count],
        refs[2 * count + 1],
        refs[2 * count + 2],
    )
    core, flag, valid = meta_ref[0], meta_ref[1], meta_ref[2]
    refs_ref, stream_ref, up_ref = refs_in[1], stream_in[1], up_in[1]
    tiles, padded, chunk = refs_ref.shape
    tokens = padded - INFO
    half = mine[0][1].shape[1]
    per_half = half // chunk
    per_piece = tiles // PIECES
    width = per_piece * chunk

    whole(lrt_in).start()
    whole(up_in).start()
    stream_loads = [columns_piece(stream_in, i, i * width, width) for i in range(PIECES)]
    ref_loads = [leading_piece(refs_in, i, i * per_piece, per_piece) for i in range(PIECES)]
    for i in range(PIECES):
        stream_loads[i].start()
        ref_loads[i].start()
    for item in (*mine, *other):
        whole(item).start()
    whole(lrt_in).wait()
    whole(up_in).wait()
    low_rank = lrt_in[1][...].astype(f32).T.astype(bf16)
    is_valid = lax.broadcasted_iota(jnp.int32, (tokens, 1), 0) < valid

    def weight(row):
        info = refs_ref[0, tokens:, :128].astype(f32)
        for i in range(1, tiles):
            info = info + refs_ref[i, tokens:, :128].astype(f32)
        return loss_scale / info[row : row + 1, 0:1]

    def stats(terms, number):
        acc = [jnp.zeros((tokens, 128), f32) for _ in range(number)]
        for i in range(PIECES):
            stream_loads[i].wait()
            ref_loads[i].wait()
            for j in range(i * per_piece, (i + 1) * per_piece):
                columns = slice(j * chunk, (j + 1) * chunk)
                out = stream_ref[:, columns].astype(f32) + nn(low_rank, up_ref[:, columns])
                output_ref[:, columns] = out
                ref = refs_ref[j, :tokens, :].astype(f32)
                acc = [a + fold(v) for a, v in zip(acc, terms(out, ref))]
        return [jnp.sum(a, axis=1, keepdims=True) for a in acc]

    group = min(4, per_half)

    def finish(make):
        for item in (*mine, *other):
            whole(item).wait()
        total = jnp.zeros(proj_ref.shape[1:], f32)
        for base, blocks in ((core, mine), (1 - core, other)):

            def step(i, acc, base=base, blocks=blocks):
                parts = []
                for g in range(group):
                    j = base * per_half + i * group + g
                    columns = pl.ds(pl.multiple_of(j * chunk, chunk), chunk)
                    own = make(output_ref[:, columns], refs_ref[j, :tokens, :].astype(f32)).astype(bf16)
                    own_ref[:, columns] = own
                    parts.append(own)
                local = pl.ds(pl.multiple_of(i * group * chunk, group * chunk), group * chunk)
                up = jnp.concatenate([b[1][:, local] for b in blocks], axis=0)
                return acc + nt(up, jnp.concatenate(parts, axis=1))

            total = lax.fori_loop(0, per_half // group, step, total, unroll=2)
        total = total.astype(bf16)
        for i in range(proj_ref.shape[0]):
            proj_ref[i] = total

    @pl.when(flag == 1)
    def _():
        out_sq, ref_sq, cross = stats(lambda o, r: (o * o, r * r, o * r), 3)
        out_norm = jnp.sqrt(out_sq + stat_eps)
        ref_norm = jnp.sqrt(ref_sq + stat_eps)
        cosine = cross / (out_norm * ref_norm)
        on = jnp.where(is_valid & (cosine > 0), coef_reroute * weight(0), 0.0)
        coef_ref = on / (out_norm * ref_norm)
        coef_out = on * cosine / (out_sq + stat_eps)
        finish(lambda o, r: coef_ref * r - coef_out * o)

    @pl.when(flag != 1)
    def _():
        (diff_sq,) = stats(lambda o, r: ((o - r) * (o - r),), 1)
        coef = jnp.where(is_valid, coef_retain * weight(1), 0.0) / jnp.sqrt(diff_sq + stat_eps)
        finish(lambda o, r: coef * (o - r))


def own_gradient(meta, refs, stream, up, lrt, mine, other):
    layers = len(mine)
    return call(
        functools.partial(own_kernel, layers),
        "own",
        (
            jax.ShapeDtypeStruct(stream.shape, bf16),
            jax.ShapeDtypeStruct((layers, layers * up.shape[0], stream.shape[0]), bf16),
        ),
        (meta,),
        (refs, stream, up, lrt, *mine, *other),
        (pltpu.VMEM(stream.shape, f32),),
    )


def solve_kernel(width, rank, me_ref, own_ref, side_ref, low_ref, lrt_ref, coef_ref, k_ref, acc):
    me = me_ref[0]
    layers, rows, _ = own_ref.shape
    acc[...] = jnp.zeros_like(acc)
    for j in range(layers):

        @pl.when(me + j < layers)
        def _(j=j):
            low = rank * (layers - 1 - j)
            acc[0 : rank * (j + 1), :] += own_ref[me + j, low:rows, :].astype(f32)

    def inverse_rms(t):
        return side_ref[t, rows + 3 * rank : rows + 3 * rank + 1, :].astype(f32) + side_ref[
            t, rows + 3 * rank + 1 : rows + 3 * rank + 2, :
        ].astype(f32)

    def mean_of(grad, t):
        lrt = side_ref[t, rows : rows + rank, :].astype(f32)
        return jnp.sum(grad.astype(f32) * lrt, axis=0, keepdims=True) * (1.0 / width)

    for j in range(layers - 1, 0, -1):

        @pl.when(me + j < layers)
        def _(j=j):
            t = me + j
            low = rank * (layers - 1 - j)
            grad = acc[rank * j : rank * (j + 1), :].astype(bf16)
            mean = mean_of(grad, t)
            w_hi = side_ref[t, rows + rank : rows + 2 * rank, :]
            w_lo = side_ref[t, rows + 2 * rank : rows + 3 * rank, :]
            term = tn(w_hi, grad) + tn(w_lo, grad)
            scaled_up = side_ref[t, low : rows - rank, :].astype(f32)
            acc[0 : rank * j, :] += inverse_rms(t) * (term[low : rows - rank, :] - mean * scaled_up)

    grad = acc[0:rank, :].astype(bf16)
    low_ref[...] = grad
    irms = inverse_rms(me)
    mean = mean_of(grad, me)
    lrt = side_ref[:, rows : rows + rank, :].reshape(layers * rank, -1)
    layer = lax.broadcasted_iota(jnp.int32, lrt.shape, 0) // rank
    lrt_f = lrt.astype(f32)
    lrt_ref[...] = jnp.where(layer <= me, lrt_f, 0.0).astype(bf16)
    below = jnp.where(layer < me, lrt_f, 0.0)
    coef_ref[...] = (below * (-irms * irms * mean)).astype(bf16)
    k_hi, k_lo = split2(nt(below.astype(bf16), (grad.astype(f32) * irms).astype(bf16)))
    k_ref[0] = k_hi
    k_ref[1] = k_lo


def solve(width, rank, me, own, side):
    layers, rows, tokens = own.shape
    return pl.pallas_call(
        functools.partial(solve_kernel, width, rank),
        out_shape=(
            jax.ShapeDtypeStruct((rank, tokens), bf16),
            jax.ShapeDtypeStruct((rows, tokens), bf16),
            jax.ShapeDtypeStruct((rows, tokens), bf16),
            jax.ShapeDtypeStruct((2, rows, rank), bf16),
        ),
        in_specs=[smem(), vmem(), vmem()],
        out_specs=(vmem(),) * 4,
        scratch_shapes=[pltpu.VMEM((rows, tokens), f32)],
        compiler_params=params(8),
        name="solve",
    )(me, own, side)


def part_kernel(start_ref, low_in, lrt_in, coef_in, k_in, own_in, stream_in, normed_in, dg_in, out_ref):
    start = start_ref[0]
    chunks, _, chunk = out_ref.shape
    rows = lrt_in[1].shape[0]
    group = min(4, chunks)
    width = group * chunk
    small = (low_in, lrt_in, coef_in, k_in)
    large = (own_in, stream_in, normed_in, dg_in)
    for item in small:
        whole(item).start()
    loads = [
        [columns_piece(item, i, pl.multiple_of(start + i * width, width), width) for item in large]
        for i in range(chunks // group)
    ]
    for piece in loads:
        for load in piece:
            load.start()
    for item in small:
        whole(item).wait()
    left = jnp.concatenate([lrt_in[1][...], coef_in[1][...]], axis=1)
    k_hi, k_lo = k_in[1][0].astype(f32), k_in[1][1].astype(f32)
    k = jnp.concatenate([k_hi, k_hi, k_lo], axis=1).astype(bf16)
    low = low_in[1][...]
    for i, piece in enumerate(loads):
        for load in piece:
            load.wait()
        columns = pl.ds(pl.multiple_of(start + i * width, width), width)
        right = jnp.concatenate([own_in[1][:, columns], stream_in[1][:, columns]], axis=0)
        dg_hi = dg_in[1][0, :, columns]
        dg = jnp.concatenate([dg_hi, dg_in[1][1, :, columns], dg_hi], axis=0)
        up = nn(left, right) + nn(k, dg)
        down = nn(low, normed_in[1][:, columns])
        for j in range(group):
            out_ref[i * group + j, :rows, :] = up[:, j * chunk : (j + 1) * chunk]
            out_ref[i * group + j, rows:, :] = down[:, j * chunk : (j + 1) * chunk]


def part(start, chunks, chunk, *arrays):
    low, lrt = arrays[:2]
    (found,) = call(
        part_kernel,
        "part",
        (jax.ShapeDtypeStruct((chunks, lrt.shape[0] + low.shape[0], chunk), f32),),
        (start,),
        arrays,
    )
    return found


def shards(
    layer_input_states,
    frozen_reference_states,
    adapter_down_weight,
    adapter_up_weight,
    layer_norm_gain,
    tile_reference_position,
    tile_harmful_flag,
    tile_valid_count,
):
    tokens, width = layer_input_states.shape[2:]
    rank = adapter_up_weight.shape[1]
    layers = lax.axis_size(SEC)
    me = lax.axis_index(SEC)
    core = lax.axis_index("core")
    cores = lax.axis_size("core")
    chips = lax.axis_size("y") * lax.axis_size("x")
    half = width // cores
    chunk = half // chips
    swap = [(i, (i + 1) % cores) for i in range(cores)]

    meta = jnp.stack([core, tile_harmful_flag[0], tile_valid_count[0]]).astype(jnp.int32)
    ordered = order(tile_reference_position, meta, frozen_reference_states[0])
    refs = lax.all_to_all(ordered, DP, split_axis=0, concat_axis=0, tiled=True)
    gate, stream, down, up, gains = lax.optimization_barrier(
        (ordered, layer_input_states[0, 0], adapter_down_weight[0], adapter_up_weight[0], layer_norm_gain)
    )

    up_half = lax.dynamic_slice_in_dim(adapter_up_weight[0], core * half, half, axis=1)
    mine = ring_gather(up_half, SEC, gate)[::-1]
    other = [lax.ppermute(block, "core", swap) for block in mine]

    normed, lrt, irms, dg = forward(stream, down, gains)
    side = side_of(meta, stream, dg, lrt, irms, mine, other)
    sides = lax.all_to_all(side, SEC, 0, 0, tiled=True)

    own, own_up = own_gradient(meta, refs, stream, up, lrt, mine, other)
    own_up = lax.all_to_all(own_up, SEC, 0, 0, tiled=True)
    low, lrt_all, coef, k = solve(width, rank, me[None], own_up, sides)

    given = part(((1 - core) * half)[None], chips, chunk, low, lrt_all, coef, k, own, stream, normed, dg)
    received = lax.ppermute(given, "core", swap)
    kept = part((core * half)[None], chips, chunk, low, lrt_all, coef, k, own, stream, normed, dg)
    blocks = lax.all_to_all((kept + received).astype(bf16), CHIPS, 0, 0, tiled=True)
    summed = jnp.sum(blocks.astype(f32), axis=0)

    by_layer = lax.all_to_all(summed[: layers * rank].reshape(layers, rank, chunk), SEC, 0, 0, tiled=True)
    final = jnp.concatenate([summed[layers * rank :], jnp.sum(by_layer, axis=0)], axis=0)

    wide = lax.all_to_all(jnp.broadcast_to(final, (chips,) + final.shape), CHIPS, 0, 0, tiled=True)
    mine = wide.transpose(1, 0, 2).reshape(2 * rank, half)
    other = lax.ppermute(mine, "core", swap)
    full = jnp.concatenate([jnp.where(core == 0, mine, other), jnp.where(core == 0, other, mine)], axis=1)
    return (full[None, :rank], full[None, rank:])


def solution(mesh):
    layers, dp = mesh.devices.shape
    cores = 2
    side = round((dp // cores) ** 0.5)
    mesh4 = Mesh(mesh.devices.reshape(layers, side, side, cores), (SEC,) + DP)
    return jax.shard_map(
        shards,
        mesh=mesh4,
        in_specs=(
            P(SEC, DP, None, None),
            P(SEC, None, None, DP),
            P(SEC, None, None),
            P(SEC, None, None),
            P(SEC, None),
            P(),
            P(DP),
            P(DP),
        ),
        out_specs=(P(SEC, None, None), P(SEC, None, None)),
        check_vma=False,
    )
```

```python
import functools

import jax
import jax.numpy as jnp
from jax import lax
from jax.experimental import pallas as pl
from jax.experimental.pallas import tpu as pltpu
from jax.sharding import Mesh
from jax.sharding import PartitionSpec as P

norm_eps = 1e-05
stat_eps = 1e-06
coef_reroute = 64.0
coef_retain = 1.0
loss_scale = 2048.0

SEC = "section"
CHIPS = ("y", "x")
DP = ("y", "x", "core")
f32 = jnp.float32
bf16 = jnp.bfloat16


def nt(left, right):
    return lax.dot_general(left, right, (((1,), (1,)), ((), ())), preferred_element_type=f32)


def tn(left, right):
    return lax.dot_general(left, right, (((0,), (0,)), ((), ())), preferred_element_type=f32)


def nn(left, right):
    return lax.dot_general(left, right, (((1,), (0,)), ((), ())), preferred_element_type=f32)


def split2(value):
    hi = value.astype(bf16)
    lo = (value - hi.astype(f32)).astype(bf16)
    return hi, lo


def ring_gather(block, axis, gate):
    n = lax.axis_size(axis)
    up = [(i, (i + 1) % n) for i in range(n)]
    down = [(i, (i - 1) % n) for i in range(n)]
    found = [None] * n
    found[0] = block
    fwd = bwd = block
    for k in range(1, n // 2 + 1):
        fwd = lax.ppermute(fwd, axis, up)
        found[k] = fwd
        if k < n - n // 2:
            bwd = lax.ppermute(bwd, axis, down)
            found[n - k] = bwd
        if k == 1:
            fwd, bwd, _ = lax.optimization_barrier((fwd, bwd, gate))
            found[1], found[n - 1] = fwd, bwd
    return found


def params(mib=63):
    return pltpu.CompilerParams(vmem_limit_bytes=mib << 20)


def smem():
    return pl.BlockSpec(memory_space=pltpu.SMEM)


def in_place():
    return pl.BlockSpec(memory_space=pl.ANY)


def vmem():
    return pl.BlockSpec(memory_space=pltpu.VMEM)


def call(kernel, name, out_shape, scalars, arrays, scratch=(), in_place_outs=0):
    count, total = len(scalars), len(arrays)
    outs = len(out_shape)

    def body(*refs):
        held = refs[count : count + total]
        first = count + total + outs
        buffers, sems = refs[first : first + total], refs[first + total : first + 2 * total]
        kernel(*refs[:count], *zip(held, buffers, sems), *refs[count + total : first], *refs[first + 2 * total :])

    return pl.pallas_call(
        body,
        out_shape=out_shape,
        in_specs=[smem()] * count + [in_place()] * total,
        out_specs=[in_place()] * in_place_outs + [vmem()] * (outs - in_place_outs),
        scratch_shapes=[pltpu.VMEM(a.shape, a.dtype) for a in arrays]
        + [pltpu.SemaphoreType.DMA((PIECES,)) for _ in arrays]
        + list(scratch),
        compiler_params=params(),
        name=name,
    )(*scalars, *arrays)


PIECES = 8
AHEAD = 2


def whole(item):
    held, buffer, sem = item
    return pltpu.make_async_copy(held, buffer, sem.at[0])


def columns_piece(item, i, start, width):
    held, buffer, sem = item
    where = (slice(None),) * (len(held.shape) - 1) + (pl.ds(start, width),)
    return pltpu.make_async_copy(held.at[where], buffer.at[where], sem.at[i])


def leading_piece(item, i, start, count):
    held, buffer, sem = item
    return pltpu.make_async_copy(held.at[pl.ds(start, count)], buffer.at[pl.ds(start, count)], sem.at[i])


INFO = 8


def order_kernel(position_ref, meta_ref, held_ref, out_ref, buffer, in_sem, out_sem):
    tiles, tokens, width = held_ref.shape
    loads = [
        pltpu.make_async_copy(held_ref.at[position_ref[i]], buffer.at[i, pl.ds(0, tokens)], in_sem.at[i])
        for i in range(tiles)
    ]
    for load in loads:
        load.start()
    flag, valid = meta_ref[1], meta_ref[2]
    row = lax.broadcasted_iota(jnp.int32, (INFO, width), 0)
    here = ((row == 0) & (flag == 1)) | ((row == 1) & (flag != 1))
    info = jnp.where(here, valid, 0).astype(f32).astype(bf16)
    stores = []
    for i in range(tiles):
        buffer[i, tokens:, :] = info
        loads[i].wait()
        stores.append(pltpu.make_async_copy(buffer.at[i], out_ref.at[i], out_sem.at[i]))
        stores[-1].start()
    for store in stores:
        store.wait()


def order(position, meta, held):
    tiles, tokens, width = held.shape
    shape = (tiles, tokens + INFO, width)
    return pl.pallas_call(
        order_kernel,
        out_shape=jax.ShapeDtypeStruct(shape, held.dtype),
        in_specs=[smem(), smem(), in_place()],
        out_specs=in_place(),
        scratch_shapes=[
            pltpu.VMEM(shape, held.dtype),
            pltpu.SemaphoreType.DMA((tiles,)),
            pltpu.SemaphoreType.DMA((tiles,)),
        ],
        compiler_params=params(),
        name="order",
    )(position, meta, held)


def fold(value):
    lanes = 128
    total = value[:, :lanes]
    for i in range(1, value.shape[1] // lanes):
        total = total + value[:, i * lanes : (i + 1) * lanes]
    return total


def forward_kernel(stream_in, down_in, gain_in, normed_ref, lrt_ref, irms_ref, dg_ref):
    stream_ref, down_ref, gain_ref = stream_in[1], down_in[1], gain_in[1]
    tokens, width = stream_ref.shape
    piece = width // PIECES
    loads = [columns_piece(stream_in, i, i * piece, piece) for i in range(PIECES)]
    for load in loads:
        load.start()
    whole(down_in).start()
    whole(gain_in).start()
    total = jnp.zeros((tokens, 128), f32)
    for i in range(PIECES):
        loads[i].wait()
        for low in range(i * piece, (i + 1) * piece, 256):
            x = stream_ref[:, low : low + 256].astype(f32)
            total = total + fold(x * x)
    irms = lax.rsqrt(jnp.sum(total, axis=1, keepdims=True) * (1.0 / width) + norm_eps)
    irms_ref[...] = jnp.broadcast_to(irms, (tokens, 128)).T[:8, :]
    whole(down_in).wait()
    whole(gain_in).wait()
    chunk = min(512, piece)

    def norm(i, acc):
        columns = pl.ds(pl.multiple_of(i * chunk, chunk), chunk)
        gain = gain_ref[:, columns]
        normed = (stream_ref[:, columns].astype(f32) * irms * gain).astype(bf16)
        normed_ref[:, columns] = normed
        down = down_ref[:, columns]
        hi, lo = split2(down.astype(f32) * gain)
        dg_ref[0, :, columns] = hi
        dg_ref[1, :, columns] = lo
        return acc + nt(down, normed)

    rank = down_ref.shape[0]
    low_rank = lax.fori_loop(0, width // chunk, norm, jnp.zeros((rank, tokens), f32), unroll=2)
    lrt_ref[...] = low_rank.astype(bf16)


def forward(stream, down, gain):
    rank = down.shape[0]
    tokens, width = stream.shape
    return call(
        forward_kernel,
        "forward",
        (
            jax.ShapeDtypeStruct((tokens, width), bf16),
            jax.ShapeDtypeStruct((rank, tokens), bf16),
            jax.ShapeDtypeStruct((8, tokens), f32),
            jax.ShapeDtypeStruct((2, rank, width), bf16),
        ),
        (),
        (stream, down, gain),
    )


def side_kernel(count, meta_ref, stream_in, dg_in, lrt_in, irms_in, *refs):
    mine, other, out_ref = refs[:count], refs[count : 2 * count], refs[2 * count]
    core = meta_ref[0]
    rank, half = mine[0][1].shape
    tokens = stream_in[1].shape[0]
    rows = count * rank
    chunk = min(1024, half)
    for item in (*mine, stream_in, dg_in, *other, lrt_in, irms_in):
        whole(item).start()
    for item in (*mine, stream_in, dg_in):
        whole(item).wait()
    stream_ref, dg_ref = stream_in[1], dg_in[1]
    total = jnp.zeros((rows, tokens + 2 * rank), f32)
    for base, blocks in ((core, mine), (1 - core, other)):
        if blocks is other:
            for item in other:
                whole(item).wait()

        def step(i, acc, base=base, blocks=blocks):
            local = pl.ds(pl.multiple_of(i * chunk, chunk), chunk)
            columns = pl.ds(pl.multiple_of(base * half + i * chunk, chunk), chunk)
            up = jnp.concatenate([b[1][:, local] for b in blocks], axis=0)
            right = jnp.concatenate([stream_ref[:, columns], dg_ref[0, :, columns], dg_ref[1, :, columns]], axis=0)
            return acc + nt(up, right)

        total = lax.fori_loop(0, half // chunk, step, total, unroll=2)
    whole(lrt_in).wait()
    whole(irms_in).wait()
    irms = irms_in[1][0:1, :]
    scaled_up = (total[:, :tokens] * irms).astype(bf16)
    w = total[:, tokens : tokens + rank] + total[:, tokens + rank :]
    w = jnp.concatenate([w, jnp.zeros((rows, 128 - rank), f32)], axis=1).T[:rank, :]
    w_hi, w_lo = split2(w)
    irms_hi = irms.astype(bf16).astype(f32)
    row = lax.broadcasted_iota(jnp.int32, (rank, tokens), 0)
    last = jnp.where(row == 0, irms_hi, jnp.where(row == 1, irms - irms_hi, 0.0)).astype(bf16)
    for i in range(out_ref.shape[0]):
        out_ref[i, :rows, :] = scaled_up
        out_ref[i, rows : rows + rank, :] = lrt_in[1][...]
        out_ref[i, rows + rank : rows + 2 * rank, :] = w_hi
        out_ref[i, rows + 2 * rank : rows + 3 * rank, :] = w_lo
        out_ref[i, rows + 3 * rank :, :] = last


def side_of(meta, stream, dg, lrt, irms, mine, other):
    layers = len(mine)
    rank = lrt.shape[0]
    (side,) = call(
        functools.partial(side_kernel, layers),
        "side",
        (jax.ShapeDtypeStruct((layers, (layers + 4) * rank, stream.shape[0]), bf16),),
        (meta,),
        (stream, dg, lrt, irms, *mine, *other),
    )
    return side


def own_kernel(count, meta_ref, refs_in, stream_in, up_in, lrt_in, *refs):
    mine, other, own_ref, proj_ref, output_ref = (
        refs[:count],
        refs[count : 2 * count],
        refs[2 * count],
        refs[2 * count + 1],
        refs[2 * count + 2],
    )
    core, flag, valid = meta_ref[0], meta_ref[1], meta_ref[2]
    refs_ref, stream_ref, up_ref = refs_in[1], stream_in[1], up_in[1]
    tiles, padded, chunk = refs_ref.shape
    tokens = padded - INFO
    half = mine[0][1].shape[1]
    per_half = half // chunk
    per_piece = tiles // PIECES
    width = per_piece * chunk

    whole(lrt_in).start()
    whole(up_in).start()
    stream_loads = [columns_piece(stream_in, i, i * width, width) for i in range(PIECES)]
    ref_loads = [leading_piece(refs_in, i, i * per_piece, per_piece) for i in range(PIECES)]

    def start(i):
        if i < PIECES:
            stream_loads[i].start()
            ref_loads[i].start()
        else:
            for item in (*mine, *other)[2 * count * (i - PIECES) // AHEAD : 2 * count * (i - PIECES + 1) // AHEAD]:
                whole(item).start()

    for i in range(AHEAD):
        start(i)
    whole(lrt_in).wait()
    whole(up_in).wait()
    low_rank = lrt_in[1][...].astype(f32).T.astype(bf16)
    is_valid = lax.broadcasted_iota(jnp.int32, (tokens, 1), 0) < valid

    def weight(row):
        info = refs_ref[0, tokens:, :128].astype(f32)
        for i in range(1, tiles):
            info = info + refs_ref[i, tokens:, :128].astype(f32)
        return loss_scale / info[row : row + 1, 0:1]

    def stats(terms, number):
        acc = [jnp.zeros((tokens, 128), f32) for _ in range(number)]
        for i in range(PIECES):
            stream_loads[i].wait()
            ref_loads[i].wait()
            start(i + AHEAD)
            for j in range(i * per_piece, (i + 1) * per_piece):
                columns = slice(j * chunk, (j + 1) * chunk)
                out = stream_ref[:, columns].astype(f32) + nn(low_rank, up_ref[:, columns])
                output_ref[:, columns] = out
                ref = refs_ref[j, :tokens, :].astype(f32)
                acc = [a + fold(v) for a, v in zip(acc, terms(out, ref))]
        return [jnp.sum(a, axis=1, keepdims=True) for a in acc]

    group = min(4, per_half)

    def finish(make):
        for item in (*mine, *other):
            whole(item).wait()
        total = jnp.zeros(proj_ref.shape[1:], f32)
        for base, blocks in ((core, mine), (1 - core, other)):

            def step(i, acc, base=base, blocks=blocks):
                parts = []
                for g in range(group):
                    j = base * per_half + i * group + g
                    columns = pl.ds(pl.multiple_of(j * chunk, chunk), chunk)
                    own = make(output_ref[:, columns], refs_ref[j, :tokens, :].astype(f32)).astype(bf16)
                    own_ref[:, columns] = own
                    parts.append(own)
                local = pl.ds(pl.multiple_of(i * group * chunk, group * chunk), group * chunk)
                up = jnp.concatenate([b[1][:, local] for b in blocks], axis=0)
                return acc + nt(up, jnp.concatenate(parts, axis=1))

            total = lax.fori_loop(0, per_half // group, step, total, unroll=2)
        total = total.astype(bf16)
        for i in range(proj_ref.shape[0]):
            proj_ref[i] = total

    @pl.when(flag == 1)
    def _():
        out_sq, ref_sq, cross = stats(lambda o, r: (o * o, r * r, o * r), 3)
        out_norm = jnp.sqrt(out_sq + stat_eps)
        ref_norm = jnp.sqrt(ref_sq + stat_eps)
        cosine = cross / (out_norm * ref_norm)
        on = jnp.where(is_valid & (cosine > 0), coef_reroute * weight(0), 0.0)
        coef_ref = on / (out_norm * ref_norm)
        coef_out = on * cosine / (out_sq + stat_eps)
        finish(lambda o, r: coef_ref * r - coef_out * o)

    @pl.when(flag != 1)
    def _():
        (diff_sq,) = stats(lambda o, r: ((o - r) * (o - r),), 1)
        coef = jnp.where(is_valid, coef_retain * weight(1), 0.0) / jnp.sqrt(diff_sq + stat_eps)
        finish(lambda o, r: coef * (o - r))


def own_gradient(meta, refs, stream, up, lrt, mine, other):
    layers = len(mine)
    return call(
        functools.partial(own_kernel, layers),
        "own",
        (
            jax.ShapeDtypeStruct(stream.shape, bf16),
            jax.ShapeDtypeStruct((layers, layers * up.shape[0], stream.shape[0]), bf16),
        ),
        (meta,),
        (refs, stream, up, lrt, *mine, *other),
        (pltpu.VMEM(stream.shape, f32),),
    )


def solve(width, rank, me, own_ref, side_ref, low_ref, lrt_ref, coef_ref, k_ref, acc):
    layers, rows, _ = own_ref.shape
    acc[...] = jnp.zeros_like(acc)
    for j in range(layers):

        @pl.when(me + j < layers)
        def _(j=j):
            low = rank * (layers - 1 - j)
            acc[0 : rank * (j + 1), :] += own_ref[me + j, low:rows, :].astype(f32)

    def inverse_rms(t):
        return side_ref[t, rows + 3 * rank : rows + 3 * rank + 1, :].astype(f32) + side_ref[
            t, rows + 3 * rank + 1 : rows + 3 * rank + 2, :
        ].astype(f32)

    def mean_of(grad, t):
        lrt = side_ref[t, rows : rows + rank, :].astype(f32)
        return jnp.sum(grad.astype(f32) * lrt, axis=0, keepdims=True) * (1.0 / width)

    for j in range(layers - 1, 0, -1):

        @pl.when(me + j < layers)
        def _(j=j):
            t = me + j
            low = rank * (layers - 1 - j)
            grad = acc[rank * j : rank * (j + 1), :].astype(bf16)
            mean = mean_of(grad, t)
            w_hi = side_ref[t, rows + rank : rows + 2 * rank, :]
            w_lo = side_ref[t, rows + 2 * rank : rows + 3 * rank, :]
            term = tn(w_hi, grad) + tn(w_lo, grad)
            scaled_up = side_ref[t, low : rows - rank, :].astype(f32)
            acc[0 : rank * j, :] += inverse_rms(t) * (term[low : rows - rank, :] - mean * scaled_up)

    grad = acc[0:rank, :].astype(bf16)
    low_ref[...] = grad
    irms = inverse_rms(me)
    mean = mean_of(grad, me)
    lrt = side_ref[:, rows : rows + rank, :].reshape(layers * rank, -1)
    layer = lax.broadcasted_iota(jnp.int32, lrt.shape, 0) // rank
    lrt_f = lrt.astype(f32)
    lrt_ref[...] = jnp.where(layer <= me, lrt_f, 0.0).astype(bf16)
    below = jnp.where(layer < me, lrt_f, 0.0)
    coef_ref[...] = (below * (-irms * irms * mean)).astype(bf16)
    k_hi, k_lo = split2(nt(below.astype(bf16), (grad.astype(f32) * irms).astype(bf16)))
    k_ref[0] = k_hi
    k_ref[1] = k_lo


def part(start, loads, low, lrt, coef, k, own_in, stream_in, normed_in, dg_in, out_ref, buffer, out_sem):
    chunks, _, chunk = buffer.shape
    rows = lrt.shape[0]
    group = chunks // len(loads)
    width = group * chunk
    left = jnp.concatenate([lrt, coef], axis=1)
    k_hi, k_lo = k[0].astype(f32), k[1].astype(f32)
    k = jnp.concatenate([k_hi, k_hi, k_lo], axis=1).astype(bf16)
    stores = []
    for i, piece in enumerate(loads):
        for load in piece:
            load.wait()
        columns = pl.ds(pl.multiple_of(start + i * width, width), width)
        right = jnp.concatenate([own_in[1][:, columns], stream_in[1][:, columns]], axis=0)
        dg_hi = dg_in[1][0, :, columns]
        dg = jnp.concatenate([dg_hi, dg_in[1][1, :, columns], dg_hi], axis=0)
        up = nn(left, right) + nn(k, dg)
        down = nn(low, normed_in[1][:, columns])
        for j in range(group):
            buffer[i * group + j, :rows, :] = up[:, j * chunk : (j + 1) * chunk]
            buffer[i * group + j, rows:, :] = down[:, j * chunk : (j + 1) * chunk]
        here = pl.ds(i * group, group)
        stores.append(pltpu.make_async_copy(buffer.at[here], out_ref.at[here], out_sem.at[i]))
        stores[-1].start()
    for store in stores:
        store.wait()


def part_loads(start, large, chunks, chunk):
    pieces = min(4, chunks)
    width = chunks // pieces * chunk
    return [
        [columns_piece(item, i, pl.multiple_of(start + i * width, width), width) for item in large]
        for i in range(pieces)
    ]


def given_kernel(rank, meta_ref, own_up_in, side_in, *refs):
    large, (out_ref, low_ref, lrt_ref, coef_ref, k_ref, acc, buffer, out_sem) = refs[:4], refs[4:]
    start, me = meta_ref[0], meta_ref[1]
    loads = part_loads(start, large, buffer.shape[0], buffer.shape[2])
    whole(own_up_in).start()
    whole(side_in).start()
    for load in loads:
        for item in load:
            item.start()
    whole(own_up_in).wait()
    whole(side_in).wait()
    solve(large[0][0].shape[1], rank, me, own_up_in[1], side_in[1], low_ref, lrt_ref, coef_ref, k_ref, acc)
    part(start, loads, low_ref[...], lrt_ref[...], coef_ref[...], k_ref, *large, out_ref, buffer, out_sem)


def kept_kernel(meta_ref, low_in, lrt_in, coef_in, k_in, *refs):
    large, (out_ref, buffer, out_sem) = refs[:4], refs[4:]
    start = meta_ref[0]
    loads = part_loads(start, large, buffer.shape[0], buffer.shape[2])
    for item in (low_in, lrt_in, coef_in, k_in):
        whole(item).start()
    for load in loads:
        for item in load:
            item.start()
    for item in (low_in, lrt_in, coef_in, k_in):
        whole(item).wait()
    part(start, loads, low_in[1][...], lrt_in[1][...], coef_in[1][...], k_in[1], *large, out_ref, buffer, out_sem)


def part_shapes(chunks, chunk, rows, rank):
    shape = (chunks, rows + rank, chunk)
    return jax.ShapeDtypeStruct(shape, f32), (pltpu.VMEM(shape, f32), pltpu.SemaphoreType.DMA((PIECES,)))


def given_part(meta, chunks, chunk, rank, own_up, side, *large):
    _, rows, tokens = own_up.shape
    shape, scratch = part_shapes(chunks, chunk, rows, rank)
    return call(
        functools.partial(given_kernel, rank),
        "given",
        (
            shape,
            jax.ShapeDtypeStruct((rank, tokens), bf16),
            jax.ShapeDtypeStruct((rows, tokens), bf16),
            jax.ShapeDtypeStruct((rows, tokens), bf16),
            jax.ShapeDtypeStruct((2, rows, rank), bf16),
        ),
        (meta,),
        (own_up, side, *large),
        (pltpu.VMEM((rows, tokens), f32),) + scratch,
        in_place_outs=1,
    )


def kept_part(meta, chunks, chunk, low, lrt, coef, k, *large):
    shape, scratch = part_shapes(chunks, chunk, lrt.shape[0], low.shape[0])
    (found,) = call(kept_kernel, "kept", (shape,), (meta,), (low, lrt, coef, k, *large), scratch, in_place_outs=1)
    return found


def shards(
    layer_input_states,
    frozen_reference_states,
    adapter_down_weight,
    adapter_up_weight,
    layer_norm_gain,
    tile_reference_position,
    tile_harmful_flag,
    tile_valid_count,
):
    tokens, width = layer_input_states.shape[2:]
    rank = adapter_up_weight.shape[1]
    layers = lax.axis_size(SEC)
    me = lax.axis_index(SEC)
    core = lax.axis_index("core")
    cores = lax.axis_size("core")
    chips = lax.axis_size("y") * lax.axis_size("x")
    half = width // cores
    chunk = half // chips
    swap = [(i, (i + 1) % cores) for i in range(cores)]

    meta = jnp.stack([core, tile_harmful_flag[0], tile_valid_count[0]]).astype(jnp.int32)
    ordered = order(tile_reference_position, meta, frozen_reference_states[0])
    refs = lax.all_to_all(ordered, DP, split_axis=0, concat_axis=0, tiled=True)
    _, stream, down, up, gains = lax.optimization_barrier(
        (ordered, layer_input_states[0, 0], adapter_down_weight[0], adapter_up_weight[0], layer_norm_gain)
    )

    up_half = lax.dynamic_slice_in_dim(adapter_up_weight[0], core * half, half, axis=1)
    normed, lrt, irms, dg = forward(stream, down, gains)
    mine = ring_gather(up_half, SEC, lrt)[::-1]
    other = [lax.ppermute(block, "core", swap) for block in mine]

    side = side_of(meta, stream, dg, lrt, irms, mine, other)
    sides = lax.all_to_all(side, SEC, 0, 0, tiled=True)

    own, own_up = own_gradient(meta, refs, stream, up, lrt, mine, other)
    own_up = lax.all_to_all(own_up, SEC, 0, 0, tiled=True)

    large = (own, stream, normed, dg)
    away = jnp.stack([(1 - core) * half, me]).astype(jnp.int32)
    here = (core * half)[None].astype(jnp.int32)
    given, *coefs = given_part(away, chips, chunk, rank, own_up, sides, *large)
    received = lax.ppermute(given, "core", swap)
    kept = kept_part(here, chips, chunk, *coefs, *large)
    blocks = lax.all_to_all((kept + received).astype(bf16), CHIPS, 0, 0, tiled=True)
    grad_up = jnp.sum(blocks[:, : layers * rank].astype(f32), axis=0)
    grad_down = jnp.sum(blocks[:, layers * rank :].astype(f32), axis=0)

    by_layer = lax.all_to_all(grad_up.reshape(layers, rank, chunk), SEC, 0, 0, tiled=True)
    final = jnp.concatenate([grad_down, jnp.sum(by_layer, axis=0)], axis=0)
    wide = lax.all_to_all(jnp.broadcast_to(final, (chips,) + final.shape), CHIPS, 0, 0, tiled=True)
    mine = wide.transpose(1, 0, 2).reshape(2 * rank, half)
    other = lax.ppermute(mine, "core", swap)
    full = jnp.concatenate([jnp.where(core == 0, mine, other), jnp.where(core == 0, other, mine)], axis=1)
    return (full[None, :rank], full[None, rank:])


def solution(mesh):
    layers, dp = mesh.devices.shape
    cores = 2
    side = round((dp // cores) ** 0.5)
    mesh4 = Mesh(mesh.devices.reshape(layers, side, side, cores), (SEC,) + DP)
    return jax.shard_map(
        shards,
        mesh=mesh4,
        in_specs=(
            P(SEC, DP, None, None),
            P(SEC, None, None, DP),
            P(SEC, None, None),
            P(SEC, None, None),
            P(SEC, None),
            P(),
            P(DP),
            P(DP),
        ),
        out_specs=(P(SEC, None, None), P(SEC, None, None)),
        check_vma=False,
    )
```

```python
import functools

import jax
import jax.numpy as jnp
from jax import lax
from jax.experimental import pallas as pl
from jax.experimental.pallas import tpu as pltpu
from jax.sharding import Mesh
from jax.sharding import PartitionSpec as P

norm_eps = 1e-05
stat_eps = 1e-06
coef_reroute = 64.0
coef_retain = 1.0
loss_scale = 2048.0

SEC = "section"
CHIPS = ("y", "x")
DP = ("y", "x", "core")
f32 = jnp.float32
bf16 = jnp.bfloat16


def nt(left, right):
    return lax.dot_general(left, right, (((1,), (1,)), ((), ())), preferred_element_type=f32)


def tn(left, right):
    return lax.dot_general(left, right, (((0,), (0,)), ((), ())), preferred_element_type=f32)


def nn(left, right):
    return lax.dot_general(left, right, (((1,), (0,)), ((), ())), preferred_element_type=f32)


def split2(value):
    hi = value.astype(bf16)
    lo = (value - hi.astype(f32)).astype(bf16)
    return hi, lo


def ring_gather(block, axis, gate):
    n = lax.axis_size(axis)
    up = [(i, (i + 1) % n) for i in range(n)]
    down = [(i, (i - 1) % n) for i in range(n)]
    found = [None] * n
    found[0] = block
    fwd = bwd = block
    for k in range(1, n // 2 + 1):
        fwd = lax.ppermute(fwd, axis, up)
        found[k] = fwd
        if k < n - n // 2:
            bwd = lax.ppermute(bwd, axis, down)
            found[n - k] = bwd
        if k == 1:
            fwd, bwd, _ = lax.optimization_barrier((fwd, bwd, gate))
            found[1], found[n - 1] = fwd, bwd
    return found


def params(mib=63):
    return pltpu.CompilerParams(vmem_limit_bytes=mib << 20)


def smem():
    return pl.BlockSpec(memory_space=pltpu.SMEM)


def in_place():
    return pl.BlockSpec(memory_space=pl.ANY)


def vmem():
    return pl.BlockSpec(memory_space=pltpu.VMEM)


def call(kernel, name, out_shape, scalars, arrays, pieces, scratch=(), in_place_outs=0):
    count, total = len(scalars), len(arrays)
    outs = len(out_shape)
    buffered = [(a, n) for a, n in zip(arrays, pieces, strict=True) if n]

    def body(*refs):
        held = refs[count : count + total]
        first = count + total + outs
        buffers = iter(refs[first : first + len(buffered)])
        sems = iter(refs[first + len(buffered) : first + 2 * len(buffered)])
        inputs = [(h, next(buffers), next(sems)) if n else h for h, n in zip(held, pieces)]
        kernel(*refs[:count], *inputs, *refs[count + total : first], *refs[first + 2 * len(buffered) :])

    return pl.pallas_call(
        body,
        out_shape=out_shape,
        in_specs=[smem()] * count + [in_place()] * total,
        out_specs=[in_place()] * in_place_outs + [vmem()] * (outs - in_place_outs),
        scratch_shapes=[pltpu.VMEM(a.shape, a.dtype) for a, _ in buffered]
        + [pltpu.SemaphoreType.DMA((n,)) for _, n in buffered]
        + list(scratch),
        compiler_params=params(),
        cost_estimate=pl.CostEstimate(flops=COST[name] * 10**9, bytes_accessed=COST[name] * 3 * 10**6, transcendentals=0),
        name=name,
    )(*scalars, *arrays)


PIECES = 8
COST = dict(forward=4, side=5, own=8, given=5, kept=4)


def gather_into(blocks, buffer, sem):
    rows = blocks[0].shape[0]
    for i, block in enumerate(blocks):
        pltpu.make_async_copy(block, buffer.at[pl.ds(i * rows, rows)], sem).start()
    return pltpu.make_async_copy(buffer, buffer, sem)


def whole(item):
    held, buffer, sem = item
    return pltpu.make_async_copy(held, buffer, sem.at[0])


def columns_piece(item, i, start, width):
    held, buffer, sem = item
    where = (slice(None),) * (len(held.shape) - 1) + (pl.ds(start, width),)
    return pltpu.make_async_copy(held.at[where], buffer.at[where], sem.at[i])


def leading_piece(item, i, start, count):
    held, buffer, sem = item
    return pltpu.make_async_copy(held.at[pl.ds(start, count)], buffer.at[pl.ds(start, count)], sem.at[i])


INFO = 8


def order_kernel(position_ref, meta_ref, held_ref, out_ref, buffer, in_sem, out_sem):
    tiles, tokens, width = held_ref.shape
    groups = in_sem.shape[0]
    group = tiles // groups
    for i in range(tiles):
        pltpu.make_async_copy(
            held_ref.at[position_ref[i]], buffer.at[i, pl.ds(0, tokens)], in_sem.at[i // group]
        ).start()
    flag, valid = meta_ref[1], meta_ref[2]
    row = lax.broadcasted_iota(jnp.int32, (INFO, width), 0)
    here = ((row == 0) & (flag == 1)) | ((row == 1) & (flag != 1))
    info = jnp.where(here, valid, 0).astype(f32).astype(bf16)
    for i in range(tiles):
        buffer[i, tokens:, :] = info
    stores = []
    for i in range(groups):
        part = pl.ds(i * group, group)
        landed = buffer.at[part, pl.ds(0, tokens)]
        pltpu.make_async_copy(landed, landed, in_sem.at[i]).wait()
        stores.append(pltpu.make_async_copy(buffer.at[part], out_ref.at[part], out_sem.at[i]))
        stores[-1].start()
    for store in stores:
        store.wait()


def order(position, meta, held):
    tiles, tokens, width = held.shape
    shape = (tiles, tokens + INFO, width)
    return pl.pallas_call(
        order_kernel,
        out_shape=jax.ShapeDtypeStruct(shape, held.dtype),
        in_specs=[smem(), smem(), in_place()],
        out_specs=in_place(),
        scratch_shapes=[
            pltpu.VMEM(shape, held.dtype),
            pltpu.SemaphoreType.DMA((4,)),
            pltpu.SemaphoreType.DMA((4,)),
        ],
        compiler_params=params(),
        name="order",
    )(position, meta, held)


def fold(value):
    lanes = 128
    total = value[:, :lanes]
    for i in range(1, value.shape[1] // lanes):
        total = total + value[:, i * lanes : (i + 1) * lanes]
    return total


def forward_kernel(stream_in, down_in, gain_in, normed_ref, lrt_ref, irms_ref, dg_ref):
    stream_ref, down_ref, gain_ref = stream_in[1], down_in[1], gain_in[1]
    tokens, width = stream_ref.shape
    piece = width // PIECES
    loads = [columns_piece(stream_in, i, i * piece, piece) for i in range(PIECES)]
    for load in loads:
        load.start()
    whole(down_in).start()
    whole(gain_in).start()
    total = jnp.zeros((tokens, 128), f32)
    for i in range(PIECES):
        loads[i].wait()
        for low in range(i * piece, (i + 1) * piece, 256):
            x = stream_ref[:, low : low + 256].astype(f32)
            total = total + fold(x * x)
    irms = lax.rsqrt(jnp.sum(total, axis=1, keepdims=True) * (1.0 / width) + norm_eps)
    irms_ref[...] = jnp.broadcast_to(irms, (tokens, 128)).T[:8, :]
    whole(down_in).wait()
    whole(gain_in).wait()
    chunk = min(512, piece)

    def norm(i, acc):
        columns = pl.ds(pl.multiple_of(i * chunk, chunk), chunk)
        gain = gain_ref[:, columns]
        normed = (stream_ref[:, columns].astype(f32) * irms * gain).astype(bf16)
        normed_ref[:, columns] = normed
        down = down_ref[:, columns]
        hi, lo = split2(down.astype(f32) * gain)
        dg_ref[0, :, columns] = hi
        dg_ref[1, :, columns] = lo
        return acc + nt(down, normed)

    rank = down_ref.shape[0]
    low_rank = lax.fori_loop(0, width // chunk, norm, jnp.zeros((rank, tokens), f32), unroll=2)
    lrt_ref[...] = low_rank.astype(bf16)


def forward(stream, down, gain):
    rank = down.shape[0]
    tokens, width = stream.shape
    return call(
        forward_kernel,
        "forward",
        (
            jax.ShapeDtypeStruct((tokens, width), bf16),
            jax.ShapeDtypeStruct((rank, tokens), bf16),
            jax.ShapeDtypeStruct((8, tokens), f32),
            jax.ShapeDtypeStruct((2, rank, width), bf16),
        ),
        (),
        (stream, down, gain),
        (PIECES, 1, 1),
    )


def side_kernel(count, meta_ref, stream_in, dg_in, lrt_in, irms_in, *refs):
    mine, other, (out_ref, up_ref, up_sem) = refs[:count], refs[count : 2 * count], refs[2 * count :]
    core = meta_ref[0]
    rank, half = mine[0].shape
    tokens = stream_in[1].shape[0]
    rows = count * rank
    chunk = min(1024, half)
    ready = [gather_into(mine, up_ref.at[0], up_sem.at[0])]
    for item in (stream_in, dg_in):
        whole(item).start()
    ready.append(gather_into(other, up_ref.at[1], up_sem.at[1]))
    for item in (lrt_in, irms_in):
        whole(item).start()
    for item in (stream_in, dg_in):
        whole(item).wait()
    stream_ref, dg_ref = stream_in[1], dg_in[1]
    total = jnp.zeros((rows, tokens + 2 * rank), f32)
    for which, base in enumerate((core, 1 - core)):
        ready[which].wait()

        def step(i, acc, which=which, base=base):
            local = pl.ds(pl.multiple_of(i * chunk, chunk), chunk)
            columns = pl.ds(pl.multiple_of(base * half + i * chunk, chunk), chunk)
            right = jnp.concatenate([stream_ref[:, columns], dg_ref[0, :, columns], dg_ref[1, :, columns]], axis=0)
            return acc + nt(up_ref[which, :, local], right)

        total = lax.fori_loop(0, half // chunk, step, total, unroll=2)
    whole(lrt_in).wait()
    whole(irms_in).wait()
    irms = irms_in[1][0:1, :]
    w = total[:, tokens : tokens + rank] + total[:, tokens + rank :]
    w = jnp.concatenate([w, jnp.zeros((rows, 128 - rank), f32)], axis=1).T[:rank, :]
    w_hi, w_lo = split2(w)
    irms_hi = irms.astype(bf16).astype(f32)
    row = lax.broadcasted_iota(jnp.int32, (rank, tokens), 0)
    last = jnp.where(row == 0, irms_hi, jnp.where(row == 1, irms - irms_hi, 0.0)).astype(bf16)
    out_ref[:rows, :] = (total[:, :tokens] * irms).astype(bf16)
    out_ref[rows : rows + rank, :] = lrt_in[1][...]
    out_ref[rows + rank : rows + 2 * rank, :] = w_hi
    out_ref[rows + 2 * rank : rows + 3 * rank, :] = w_lo
    out_ref[rows + 3 * rank :, :] = last


def up_scratch(mine):
    rank, half = mine[0].shape
    return (pltpu.VMEM((2, len(mine) * rank, half), bf16), pltpu.SemaphoreType.DMA((2,)))


def side_of(meta, stream, dg, lrt, irms, mine, other):
    layers = len(mine)
    rank = lrt.shape[0]
    (side,) = call(
        functools.partial(side_kernel, layers),
        "side",
        (jax.ShapeDtypeStruct(((layers + 4) * rank, stream.shape[0]), bf16),),
        (meta,),
        (stream, dg, lrt, irms, *mine, *other),
        (1, 1, 1, 1) + (0,) * (2 * layers),
        up_scratch(mine),
    )
    return side


def own_kernel(count, meta_ref, refs_in, stream_in, up_in, lrt_in, *refs):
    mine, other = refs[:count], refs[count : 2 * count]
    own_ref, proj_ref, output_ref, ups_ref, up_sem = refs[2 * count :]
    core, flag, valid = meta_ref[0], meta_ref[1], meta_ref[2]
    refs_ref, stream_ref, up_ref = refs_in[1], stream_in[1], up_in[1]
    tiles, padded, chunk = refs_ref.shape
    tokens = padded - INFO
    half = mine[0].shape[1]
    per_half = half // chunk
    per_piece = tiles // PIECES
    width = per_piece * chunk

    whole(lrt_in).start()
    whole(up_in).start()
    stream_loads = [columns_piece(stream_in, i, i * width, width) for i in range(PIECES)]
    ref_loads = [leading_piece(refs_in, i, i * per_piece, per_piece) for i in range(PIECES)]
    for i in range(PIECES):
        stream_loads[i].start()
        ref_loads[i].start()
    ready = [gather_into(blocks, ups_ref.at[i], up_sem.at[i]) for i, blocks in enumerate((mine, other))]
    whole(lrt_in).wait()
    whole(up_in).wait()
    low_rank = lrt_in[1][...].astype(f32).T.astype(bf16)
    is_valid = lax.broadcasted_iota(jnp.int32, (tokens, 1), 0) < valid

    def weight(row):
        info = refs_ref[0, tokens:, :128].astype(f32)
        for i in range(1, tiles):
            info = info + refs_ref[i, tokens:, :128].astype(f32)
        return loss_scale / info[row : row + 1, 0:1]

    def stats(terms, number):
        acc = [jnp.zeros((tokens, 128), f32) for _ in range(number)]
        for i in range(PIECES):
            stream_loads[i].wait()
            ref_loads[i].wait()
            for j in range(i * per_piece, (i + 1) * per_piece):
                columns = slice(j * chunk, (j + 1) * chunk)
                out = stream_ref[:, columns].astype(f32) + nn(low_rank, up_ref[:, columns])
                output_ref[:, columns] = out
                ref = refs_ref[j, :tokens, :].astype(f32)
                acc = [a + fold(v) for a, v in zip(acc, terms(out, ref))]
        return [jnp.sum(a, axis=1, keepdims=True) for a in acc]

    group = min(4, per_half)

    def finish(make):
        for wait in ready:
            wait.wait()
        total = jnp.zeros(proj_ref.shape[1:], f32)
        for which, base in enumerate((core, 1 - core)):

            def step(i, acc, which=which, base=base):
                parts = []
                for g in range(group):
                    j = base * per_half + i * group + g
                    columns = pl.ds(pl.multiple_of(j * chunk, chunk), chunk)
                    own = make(output_ref[:, columns], refs_ref[j, :tokens, :].astype(f32)).astype(bf16)
                    own_ref[:, columns] = own
                    parts.append(own)
                local = pl.ds(pl.multiple_of(i * group * chunk, group * chunk), group * chunk)
                return acc + nt(ups_ref[which, :, local], jnp.concatenate(parts, axis=1))

            total = lax.fori_loop(0, per_half // group, step, total, unroll=2)
        total = total.astype(bf16)
        for i in range(proj_ref.shape[0]):
            proj_ref[i] = total

    @pl.when(flag == 1)
    def _():
        out_sq, ref_sq, cross = stats(lambda o, r: (o * o, r * r, o * r), 3)
        out_norm = jnp.sqrt(out_sq + stat_eps)
        ref_norm = jnp.sqrt(ref_sq + stat_eps)
        cosine = cross / (out_norm * ref_norm)
        on = jnp.where(is_valid & (cosine > 0), coef_reroute * weight(0), 0.0)
        coef_ref = on / (out_norm * ref_norm)
        coef_out = on * cosine / (out_sq + stat_eps)
        finish(lambda o, r: coef_ref * r - coef_out * o)

    @pl.when(flag != 1)
    def _():
        (diff_sq,) = stats(lambda o, r: ((o - r) * (o - r),), 1)
        coef = jnp.where(is_valid, coef_retain * weight(1), 0.0) / jnp.sqrt(diff_sq + stat_eps)
        finish(lambda o, r: coef * (o - r))


def own_gradient(meta, refs, stream, up, lrt, mine, other):
    layers = len(mine)
    return call(
        functools.partial(own_kernel, layers),
        "own",
        (
            jax.ShapeDtypeStruct(stream.shape, bf16),
            jax.ShapeDtypeStruct((layers, layers * up.shape[0], stream.shape[0]), bf16),
        ),
        (meta,),
        (refs, stream, up, lrt, *mine, *other),
        (PIECES, PIECES, 1, 1) + (0,) * (2 * layers),
        (pltpu.VMEM(stream.shape, f32),) + up_scratch(mine),
    )


def solve(width, rank, me, own_ref, side_ref, low_ref, lrt_ref, coef_ref, k_ref, acc, lrt_all):
    layers, rows, _ = own_ref.shape
    acc[...] = jnp.zeros_like(acc)
    for j in range(layers):

        @pl.when(me + j < layers)
        def _(j=j):
            low = rank * (layers - 1 - j)
            acc[0 : rank * (j + 1), :] += own_ref[me + j, low:rows, :].astype(f32)

    def inverse_rms(j):
        hi = side_ref[j, rows + 3 * rank : rows + 3 * rank + 1, :].astype(f32)
        return hi + side_ref[j, rows + 3 * rank + 1 : rows + 3 * rank + 2, :].astype(f32)

    def mean_of(grad, j):
        lrt = side_ref[j, rows : rows + rank, :].astype(f32)
        return jnp.sum(grad.astype(f32) * lrt, axis=0, keepdims=True) * (1.0 / width)

    for j in range(layers - 1, 0, -1):

        @pl.when(me + j < layers)
        def _(j=j):
            low = rank * (layers - 1 - j)
            grad = acc[rank * j : rank * (j + 1), :].astype(bf16)
            mean = mean_of(grad, j)
            w_hi = side_ref[j, rows + rank : rows + 2 * rank, :]
            w_lo = side_ref[j, rows + 2 * rank : rows + 3 * rank, :]
            term = tn(w_hi, grad) + tn(w_lo, grad)
            scaled_up = side_ref[j, low : rows - rank, :].astype(f32)
            acc[0 : rank * j, :] += inverse_rms(j) * (term[low : rows - rank, :] - mean * scaled_up)

    grad = acc[0:rank, :].astype(bf16)
    low_ref[...] = grad
    irms = inverse_rms(0)
    mean = mean_of(grad, 0)
    for j in range(layers):
        where = lax.rem(me + j, layers) * rank
        lrt_all[pl.ds(pl.multiple_of(where, rank), rank), :] = side_ref[j, rows : rows + rank, :]
    lrt_f = lrt_all[...].astype(f32)
    layer = lax.broadcasted_iota(jnp.int32, lrt_f.shape, 0) // rank
    lrt_ref[...] = jnp.where(layer <= me, lrt_f, 0.0).astype(bf16)
    below = jnp.where(layer < me, lrt_f, 0.0)
    coef_ref[...] = (below * (-irms * irms * mean)).astype(bf16)
    k_hi, k_lo = split2(nt(below.astype(bf16), (grad.astype(f32) * irms).astype(bf16)))
    k_ref[0] = k_hi
    k_ref[1] = k_lo


def part(start, loads, low, lrt, coef, k, own_in, stream_in, normed_in, dg_in, out_ref, buffer, out_sem):
    chunks, _, chunk = buffer.shape
    rows = lrt.shape[0]
    group = chunks // len(loads)
    width = group * chunk
    left = jnp.concatenate([lrt, coef], axis=1)
    k_hi, k_lo = k[0].astype(f32), k[1].astype(f32)
    k = jnp.concatenate([k_hi, k_hi, k_lo], axis=1).astype(bf16)
    stores = []
    for i, piece in enumerate(loads):
        for load in piece:
            load.wait()
        columns = pl.ds(pl.multiple_of(start + i * width, width), width)
        right = jnp.concatenate([own_in[1][:, columns], stream_in[1][:, columns]], axis=0)
        dg_hi = dg_in[1][0, :, columns]
        dg = jnp.concatenate([dg_hi, dg_in[1][1, :, columns], dg_hi], axis=0)
        up = nn(left, right) + nn(k, dg)
        down = nn(low, normed_in[1][:, columns])
        for j in range(group):
            buffer[i * group + j, :rows, :] = up[:, j * chunk : (j + 1) * chunk]
            buffer[i * group + j, rows:, :] = down[:, j * chunk : (j + 1) * chunk]
        here = pl.ds(i * group, group)
        stores.append(pltpu.make_async_copy(buffer.at[here], out_ref.at[here], out_sem.at[i]))
        stores[-1].start()
    for store in stores:
        store.wait()


def part_loads(start, large, chunks, chunk):
    pieces = min(4, chunks)
    width = chunks // pieces * chunk
    return [
        [columns_piece(item, i, pl.multiple_of(start + i * width, width), width) for item in large]
        for i in range(pieces)
    ]


def given_kernel(rank, count, meta_ref, own_up_in, *refs):
    sides, large = refs[:count], refs[count : count + 4]
    out_ref, low_ref, lrt_ref, coef_ref, k_ref, acc, lrt_all, side_ref, side_sem, buffer, out_sem = refs[count + 4 :]
    start, me = meta_ref[0], meta_ref[1]
    loads = part_loads(start, large, buffer.shape[0], buffer.shape[2])
    whole(own_up_in).start()
    for i, side in enumerate(sides):
        pltpu.make_async_copy(side, side_ref.at[i], side_sem).start()
    for load in loads:
        for item in load:
            item.start()
    whole(own_up_in).wait()
    pltpu.make_async_copy(side_ref, side_ref, side_sem).wait()
    solve(large[0][0].shape[1], rank, me, own_up_in[1], side_ref, low_ref, lrt_ref, coef_ref, k_ref, acc, lrt_all)
    part(start, loads, low_ref[...], lrt_ref[...], coef_ref[...], k_ref, *large, out_ref, buffer, out_sem)


def kept_kernel(meta_ref, low_in, lrt_in, coef_in, k_in, *refs):
    large, (out_ref, buffer, out_sem) = refs[:4], refs[4:]
    start = meta_ref[0]
    loads = part_loads(start, large, buffer.shape[0], buffer.shape[2])
    for item in (low_in, lrt_in, coef_in, k_in):
        whole(item).start()
    for load in loads:
        for item in load:
            item.start()
    for item in (low_in, lrt_in, coef_in, k_in):
        whole(item).wait()
    part(start, loads, low_in[1][...], lrt_in[1][...], coef_in[1][...], k_in[1], *large, out_ref, buffer, out_sem)


def part_shapes(chunks, chunk, rows, rank):
    shape = (chunks, rows + rank, chunk)
    return jax.ShapeDtypeStruct(shape, f32), (pltpu.VMEM(shape, f32), pltpu.SemaphoreType.DMA((4,)))


def given_part(meta, chunks, chunk, rank, own_up, sides, *large):
    layers, rows, tokens = own_up.shape
    shape, scratch = part_shapes(chunks, chunk, rows, rank)
    return call(
        functools.partial(given_kernel, rank, layers),
        "given",
        (
            shape,
            jax.ShapeDtypeStruct((rank, tokens), bf16),
            jax.ShapeDtypeStruct((rows, tokens), bf16),
            jax.ShapeDtypeStruct((rows, tokens), bf16),
            jax.ShapeDtypeStruct((2, rows, rank), bf16),
        ),
        (meta,),
        (own_up, *sides, *large),
        (1,) + (0,) * layers + (4,) * 4,
        (
            pltpu.VMEM((rows, tokens), f32),
            pltpu.VMEM((rows, tokens), bf16),
            pltpu.VMEM((layers,) + sides[0].shape, bf16),
            pltpu.SemaphoreType.DMA,
        )
        + scratch,
        in_place_outs=1,
    )


def kept_part(meta, chunks, chunk, low, lrt, coef, k, *large):
    shape, scratch = part_shapes(chunks, chunk, lrt.shape[0], low.shape[0])
    (found,) = call(
        kept_kernel,
        "kept",
        (shape,),
        (meta,),
        (low, lrt, coef, k, *large),
        (1,) * 4 + (4,) * 4,
        scratch,
        in_place_outs=1,
    )
    return found


def shards(
    layer_input_states,
    frozen_reference_states,
    adapter_down_weight,
    adapter_up_weight,
    layer_norm_gain,
    tile_reference_position,
    tile_harmful_flag,
    tile_valid_count,
):
    tokens, width = layer_input_states.shape[2:]
    rank = adapter_up_weight.shape[1]
    layers = lax.axis_size(SEC)
    me = lax.axis_index(SEC)
    core = lax.axis_index("core")
    cores = lax.axis_size("core")
    chips = lax.axis_size("y") * lax.axis_size("x")
    half = width // cores
    chunk = half // chips
    swap = [(i, (i + 1) % cores) for i in range(cores)]

    meta = jnp.stack([core, tile_harmful_flag[0], tile_valid_count[0]]).astype(jnp.int32)
    up_half = lax.dynamic_slice_in_dim(adapter_up_weight[0], core * half, half, axis=1)
    up_half, position = lax.optimization_barrier((up_half, tile_reference_position))
    ordered = order(position, meta, frozen_reference_states[0])
    refs = lax.all_to_all(ordered, DP, split_axis=0, concat_axis=0, tiled=True)
    _, stream, down, up, gains = lax.optimization_barrier(
        (ordered, layer_input_states[0, 0], adapter_down_weight[0], adapter_up_weight[0], layer_norm_gain)
    )

    normed, lrt, irms, dg = forward(stream, down, gains)
    mine = ring_gather(up_half, SEC, lrt)[::-1]
    other = [lax.ppermute(block, "core", swap) for block in mine]

    side = side_of(meta, stream, dg, lrt, irms, mine, other)
    sides = [side]
    for j in range(1, layers):
        sides.append(lax.ppermute(side, SEC, [(t, (t - j) % layers) for t in range(layers)]))

    refs, _ = lax.optimization_barrier((refs, side))

    own, own_up = own_gradient(meta, refs, stream, up, lrt, mine, other)
    own_up = lax.all_to_all(own_up, SEC, 0, 0, tiled=True)

    large = (own, stream, normed, dg)
    away = jnp.stack([(1 - core) * half, me]).astype(jnp.int32)
    here = (core * half)[None].astype(jnp.int32)
    given, *coefs = given_part(away, chips, chunk, rank, own_up, sides, *large)
    received = lax.ppermute(given, "core", swap)
    kept = kept_part(here, chips, chunk, *coefs, *large)
    blocks = lax.all_to_all((kept + received).astype(bf16), CHIPS, 0, 0, tiled=True)
    grad_up = jnp.sum(blocks[:, : layers * rank].astype(f32), axis=0)
    grad_down = jnp.sum(blocks[:, layers * rank :].astype(f32), axis=0)

    by_layer = lax.all_to_all(grad_up.reshape(layers, rank, chunk), SEC, 0, 0, tiled=True)
    final = jnp.concatenate([grad_down, jnp.sum(by_layer, axis=0)], axis=0)
    wide = lax.all_to_all(jnp.broadcast_to(final, (chips,) + final.shape), CHIPS, 0, 0, tiled=True)
    mine = wide.transpose(1, 0, 2).reshape(2 * rank, half)
    other = lax.ppermute(mine, "core", swap)
    full = jnp.concatenate([jnp.where(core == 0, mine, other), jnp.where(core == 0, other, mine)], axis=1)
    return (full[None, :rank], full[None, rank:])


def solution(mesh):
    layers, dp = mesh.devices.shape
    cores = 2
    side = round((dp // cores) ** 0.5)
    mesh4 = Mesh(mesh.devices.reshape(layers, side, side, cores), (SEC,) + DP)
    return jax.shard_map(
        shards,
        mesh=mesh4,
        in_specs=(
            P(SEC, DP, None, None),
            P(SEC, None, None, DP),
            P(SEC, None, None),
            P(SEC, None, None),
            P(SEC, None),
            P(),
            P(DP),
            P(DP),
        ),
        out_specs=(P(SEC, None, None), P(SEC, None, None)),
        check_vma=False,
    )
```

```python
import functools

import jax
import jax.numpy as jnp
from jax import lax
from jax.experimental import pallas as pl
from jax.experimental.pallas import tpu as pltpu
from jax.sharding import Mesh
from jax.sharding import PartitionSpec as P

norm_eps = 1e-05
stat_eps = 1e-06
coef_reroute = 64.0
coef_retain = 1.0
loss_scale = 2048.0

SEC = "section"
CHIPS = ("y", "x")
DP = ("y", "x", "core")
f32 = jnp.float32
bf16 = jnp.bfloat16


def nt(left, right):
    return lax.dot_general(left, right, (((1,), (1,)), ((), ())), preferred_element_type=f32)


def tn(left, right):
    return lax.dot_general(left, right, (((0,), (0,)), ((), ())), preferred_element_type=f32)


def nn(left, right):
    return lax.dot_general(left, right, (((1,), (0,)), ((), ())), preferred_element_type=f32)


def split2(value):
    hi = value.astype(bf16)
    lo = (value - hi.astype(f32)).astype(bf16)
    return hi, lo


def ring_first(block, axis):
    n = lax.axis_size(axis)
    up = [(i, (i + 1) % n) for i in range(n)]
    down = [(i, (i - 1) % n) for i in range(n)]
    return lax.ppermute(block, axis, up), lax.ppermute(block, axis, down)


def ring_gather(block, fwd, bwd, axis, gate):
    n = lax.axis_size(axis)
    up = [(i, (i + 1) % n) for i in range(n)]
    down = [(i, (i - 1) % n) for i in range(n)]
    found = [None] * n
    found[0], found[1], found[n - 1] = block, fwd, bwd
    for k in range(2, n // 2 + 1):
        fwd = lax.ppermute(fwd, axis, up)
        found[k] = fwd
        if k < n - n // 2:
            bwd = lax.ppermute(bwd, axis, down)
            found[n - k] = bwd
        if k == 2:
            fwd, bwd, _ = lax.optimization_barrier((fwd, bwd, gate))
            found[2], found[n - 2] = fwd, bwd
    return found


def params(mib=63):
    return pltpu.CompilerParams(vmem_limit_bytes=mib << 20)


def smem():
    return pl.BlockSpec(memory_space=pltpu.SMEM)


def in_place():
    return pl.BlockSpec(memory_space=pl.ANY)


def vmem():
    return pl.BlockSpec(memory_space=pltpu.VMEM)


def call(kernel, name, out_shape, scalars, arrays, pieces, scratch=(), in_place_outs=0):
    count, total = len(scalars), len(arrays)
    outs = len(out_shape)
    buffered = [(a, n) for a, n in zip(arrays, pieces, strict=True) if n]

    def body(*refs):
        held = refs[count : count + total]
        first = count + total + outs
        buffers = iter(refs[first : first + len(buffered)])
        sems = iter(refs[first + len(buffered) : first + 2 * len(buffered)])
        inputs = [(h, next(buffers), next(sems)) if n else h for h, n in zip(held, pieces)]
        kernel(*refs[:count], *inputs, *refs[count + total : first], *refs[first + 2 * len(buffered) :])

    return pl.pallas_call(
        body,
        out_shape=out_shape,
        in_specs=[smem()] * count + [in_place()] * total,
        out_specs=[in_place()] * in_place_outs + [vmem()] * (outs - in_place_outs),
        scratch_shapes=[pltpu.VMEM(a.shape, a.dtype) for a, _ in buffered]
        + [pltpu.SemaphoreType.DMA((n,)) for _, n in buffered]
        + list(scratch),
        compiler_params=params(),
        cost_estimate=pl.CostEstimate(flops=COST[name] * 10**9, bytes_accessed=COST[name] * 3 * 10**6, transcendentals=0),
        name=name,
    )(*scalars, *arrays)


PIECES = 8
COST = dict(forward=4, side=5, own=8, given=5, kept=4)


def gather_into(blocks, buffer, sem):
    rows = blocks[0].shape[0]
    for i, block in enumerate(blocks):
        pltpu.make_async_copy(block, buffer.at[pl.ds(i * rows, rows)], sem).start()
    return pltpu.make_async_copy(buffer, buffer, sem)


def whole(item):
    held, buffer, sem = item
    return pltpu.make_async_copy(held, buffer, sem.at[0])


def columns_piece(item, i, start, width):
    held, buffer, sem = item
    where = (slice(None),) * (len(held.shape) - 1) + (pl.ds(start, width),)
    return pltpu.make_async_copy(held.at[where], buffer.at[where], sem.at[i])


def leading_piece(item, i, start, count):
    held, buffer, sem = item
    return pltpu.make_async_copy(held.at[pl.ds(start, count)], buffer.at[pl.ds(start, count)], sem.at[i])


INFO = 8


def order_kernel(position_ref, meta_ref, held_ref, out_ref, buffer, in_sem, out_sem):
    tiles, tokens, width = held_ref.shape
    groups = in_sem.shape[0]
    group = tiles // groups
    for i in range(tiles):
        pltpu.make_async_copy(
            held_ref.at[position_ref[i]], buffer.at[i, pl.ds(0, tokens)], in_sem.at[i // group]
        ).start()
    flag, valid = meta_ref[1], meta_ref[2]
    row = lax.broadcasted_iota(jnp.int32, (INFO, width), 0)
    here = ((row == 0) & (flag == 1)) | ((row == 1) & (flag != 1))
    info = jnp.where(here, valid, 0).astype(f32).astype(bf16)
    for i in range(tiles):
        buffer[i, tokens:, :] = info
    stores = []
    for i in range(groups):
        part = pl.ds(i * group, group)
        landed = buffer.at[part, pl.ds(0, tokens)]
        pltpu.make_async_copy(landed, landed, in_sem.at[i]).wait()
        stores.append(pltpu.make_async_copy(buffer.at[part], out_ref.at[part], out_sem.at[i]))
        stores[-1].start()
    for store in stores:
        store.wait()


def order(position, meta, held):
    tiles, tokens, width = held.shape
    shape = (tiles, tokens + INFO, width)
    return pl.pallas_call(
        order_kernel,
        out_shape=jax.ShapeDtypeStruct(shape, held.dtype),
        in_specs=[smem(), smem(), in_place()],
        out_specs=in_place(),
        scratch_shapes=[
            pltpu.VMEM(shape, held.dtype),
            pltpu.SemaphoreType.DMA((4,)),
            pltpu.SemaphoreType.DMA((4,)),
        ],
        compiler_params=params(),
        name="order",
    )(position, meta, held)


def fold(value):
    lanes = 128
    total = value[:, :lanes]
    for i in range(1, value.shape[1] // lanes):
        total = total + value[:, i * lanes : (i + 1) * lanes]
    return total


def forward_kernel(stream_in, down_in, gain_in, normed_ref, lrt_ref, irms_ref, dg_ref):
    stream_ref, down_ref, gain_ref = stream_in[1], down_in[1], gain_in[1]
    tokens, width = stream_ref.shape
    piece = width // PIECES
    loads = [columns_piece(stream_in, i, i * piece, piece) for i in range(PIECES)]
    for load in loads:
        load.start()
    whole(down_in).start()
    whole(gain_in).start()
    total = jnp.zeros((tokens, 128), f32)
    for i in range(PIECES):
        loads[i].wait()
        for low in range(i * piece, (i + 1) * piece, 256):
            x = stream_ref[:, low : low + 256].astype(f32)
            total = total + fold(x * x)
    irms = lax.rsqrt(jnp.sum(total, axis=1, keepdims=True) * (1.0 / width) + norm_eps)
    irms_ref[...] = jnp.broadcast_to(irms, (tokens, 128)).T[:8, :]
    whole(down_in).wait()
    whole(gain_in).wait()
    chunk = min(512, piece)

    def norm(i, acc):
        columns = pl.ds(pl.multiple_of(i * chunk, chunk), chunk)
        gain = gain_ref[:, columns]
        normed = (stream_ref[:, columns].astype(f32) * irms * gain).astype(bf16)
        normed_ref[:, columns] = normed
        down = down_ref[:, columns]
        hi, lo = split2(down.astype(f32) * gain)
        dg_ref[0, :, columns] = hi
        dg_ref[1, :, columns] = lo
        return acc + nt(down, normed)

    rank = down_ref.shape[0]
    low_rank = lax.fori_loop(0, width // chunk, norm, jnp.zeros((rank, tokens), f32), unroll=2)
    lrt_ref[...] = low_rank.astype(bf16)


def forward(stream, down, gain):
    rank = down.shape[0]
    tokens, width = stream.shape
    return call(
        forward_kernel,
        "forward",
        (
            jax.ShapeDtypeStruct((tokens, width), bf16),
            jax.ShapeDtypeStruct((rank, tokens), bf16),
            jax.ShapeDtypeStruct((8, tokens), f32),
            jax.ShapeDtypeStruct((2, rank, width), bf16),
        ),
        (),
        (stream, down, gain),
        (PIECES, 1, 1),
    )


def side_kernel(count, meta_ref, stream_in, dg_in, lrt_in, irms_in, *refs):
    mine, other, (out_ref, up_ref, up_sem) = refs[:count], refs[count : 2 * count], refs[2 * count :]
    core = meta_ref[0]
    rank, half = mine[0].shape
    tokens = stream_in[1].shape[0]
    rows = count * rank
    chunk = min(1024, half)
    ready = [gather_into(mine, up_ref.at[0], up_sem.at[0])]
    for item in (stream_in, dg_in):
        whole(item).start()
    ready.append(gather_into(other, up_ref.at[1], up_sem.at[1]))
    for item in (lrt_in, irms_in):
        whole(item).start()
    for item in (stream_in, dg_in):
        whole(item).wait()
    stream_ref, dg_ref = stream_in[1], dg_in[1]
    total = jnp.zeros((rows, tokens + 2 * rank), f32)
    for which, base in enumerate((core, 1 - core)):
        ready[which].wait()

        def step(i, acc, which=which, base=base):
            local = pl.ds(pl.multiple_of(i * chunk, chunk), chunk)
            columns = pl.ds(pl.multiple_of(base * half + i * chunk, chunk), chunk)
            right = jnp.concatenate([stream_ref[:, columns], dg_ref[0, :, columns], dg_ref[1, :, columns]], axis=0)
            return acc + nt(up_ref[which, :, local], right)

        total = lax.fori_loop(0, half // chunk, step, total, unroll=2)
    whole(lrt_in).wait()
    whole(irms_in).wait()
    irms = irms_in[1][0:1, :]
    w = total[:, tokens : tokens + rank] + total[:, tokens + rank :]
    w = jnp.concatenate([w, jnp.zeros((rows, 128 - rank), f32)], axis=1).T[:rank, :]
    w_hi, w_lo = split2(w)
    irms_hi = irms.astype(bf16).astype(f32)
    row = lax.broadcasted_iota(jnp.int32, (rank, tokens), 0)
    last = jnp.where(row == 0, irms_hi, jnp.where(row == 1, irms - irms_hi, 0.0)).astype(bf16)
    out_ref[:rows, :] = (total[:, :tokens] * irms).astype(bf16)
    out_ref[rows : rows + rank, :] = lrt_in[1][...]
    out_ref[rows + rank : rows + 2 * rank, :] = w_hi
    out_ref[rows + 2 * rank : rows + 3 * rank, :] = w_lo
    out_ref[rows + 3 * rank :, :] = last


def up_scratch(mine):
    rank, half = mine[0].shape
    return (pltpu.VMEM((2, len(mine) * rank, half), bf16), pltpu.SemaphoreType.DMA((2,)))


def side_of(meta, stream, dg, lrt, irms, mine, other):
    layers = len(mine)
    rank = lrt.shape[0]
    (side,) = call(
        functools.partial(side_kernel, layers),
        "side",
        (jax.ShapeDtypeStruct(((layers + 4) * rank, stream.shape[0]), bf16),),
        (meta,),
        (stream, dg, lrt, irms, *mine, *other),
        (1, 1, 1, 1) + (0,) * (2 * layers),
        up_scratch(mine),
    )
    return side


def own_kernel(count, meta_ref, refs_in, stream_in, up_in, lrt_in, *refs):
    mine, other = refs[:count], refs[count : 2 * count]
    own_ref, proj_ref, output_ref, ups_ref, up_sem = refs[2 * count :]
    core, flag, valid = meta_ref[0], meta_ref[1], meta_ref[2]
    refs_ref, stream_ref, up_ref = refs_in[1], stream_in[1], up_in[1]
    tiles, padded, chunk = refs_ref.shape
    tokens = padded - INFO
    half = mine[0].shape[1]
    per_half = half // chunk
    per_piece = tiles // PIECES
    width = per_piece * chunk

    whole(lrt_in).start()
    whole(up_in).start()
    stream_loads = [columns_piece(stream_in, i, i * width, width) for i in range(PIECES)]
    ref_loads = [leading_piece(refs_in, i, i * per_piece, per_piece) for i in range(PIECES)]
    for i in range(PIECES):
        stream_loads[i].start()
        ref_loads[i].start()
    ready = [gather_into(blocks, ups_ref.at[i], up_sem.at[i]) for i, blocks in enumerate((mine, other))]
    whole(lrt_in).wait()
    whole(up_in).wait()
    low_rank = lrt_in[1][...].astype(f32).T.astype(bf16)
    is_valid = lax.broadcasted_iota(jnp.int32, (tokens, 1), 0) < valid

    def weight(row):
        info = refs_ref[0, tokens:, :128].astype(f32)
        for i in range(1, tiles):
            info = info + refs_ref[i, tokens:, :128].astype(f32)
        return loss_scale / info[row : row + 1, 0:1]

    def stats(terms, number):
        acc = [jnp.zeros((tokens, 128), f32) for _ in range(number)]
        for i in range(PIECES):
            stream_loads[i].wait()
            ref_loads[i].wait()
            for j in range(i * per_piece, (i + 1) * per_piece):
                columns = slice(j * chunk, (j + 1) * chunk)
                out = stream_ref[:, columns].astype(f32) + nn(low_rank, up_ref[:, columns])
                output_ref[:, columns] = out
                ref = refs_ref[j, :tokens, :].astype(f32)
                acc = [a + fold(v) for a, v in zip(acc, terms(out, ref))]
        return [jnp.sum(a, axis=1, keepdims=True) for a in acc]

    group = min(4, per_half)

    def finish(make):
        for wait in ready:
            wait.wait()
        total = jnp.zeros(proj_ref.shape[1:], f32)
        for which, base in enumerate((core, 1 - core)):

            def step(i, acc, which=which, base=base):
                parts = []
                for g in range(group):
                    j = base * per_half + i * group + g
                    columns = pl.ds(pl.multiple_of(j * chunk, chunk), chunk)
                    own = make(output_ref[:, columns], refs_ref[j, :tokens, :].astype(f32)).astype(bf16)
                    own_ref[:, columns] = own
                    parts.append(own)
                local = pl.ds(pl.multiple_of(i * group * chunk, group * chunk), group * chunk)
                return acc + nt(ups_ref[which, :, local], jnp.concatenate(parts, axis=1))

            total = lax.fori_loop(0, per_half // group, step, total, unroll=2)
        total = total.astype(bf16)
        for i in range(proj_ref.shape[0]):
            proj_ref[i] = total

    @pl.when(flag == 1)
    def _():
        out_sq, ref_sq, cross = stats(lambda o, r: (o * o, r * r, o * r), 3)
        out_norm = jnp.sqrt(out_sq + stat_eps)
        ref_norm = jnp.sqrt(ref_sq + stat_eps)
        cosine = cross / (out_norm * ref_norm)
        on = jnp.where(is_valid & (cosine > 0), coef_reroute * weight(0), 0.0)
        coef_ref = on / (out_norm * ref_norm)
        coef_out = on * cosine / (out_sq + stat_eps)
        finish(lambda o, r: coef_ref * r - coef_out * o)

    @pl.when(flag != 1)
    def _():
        (diff_sq,) = stats(lambda o, r: ((o - r) * (o - r),), 1)
        coef = jnp.where(is_valid, coef_retain * weight(1), 0.0) / jnp.sqrt(diff_sq + stat_eps)
        finish(lambda o, r: coef * (o - r))


def own_gradient(meta, refs, stream, up, lrt, mine, other):
    layers = len(mine)
    return call(
        functools.partial(own_kernel, layers),
        "own",
        (
            jax.ShapeDtypeStruct(stream.shape, bf16),
            jax.ShapeDtypeStruct((layers, layers * up.shape[0], stream.shape[0]), bf16),
        ),
        (meta,),
        (refs, stream, up, lrt, *mine, *other),
        (PIECES, PIECES, 1, 1) + (0,) * (2 * layers),
        (pltpu.VMEM(stream.shape, f32),) + up_scratch(mine),
    )


def solve(width, rank, me, own_ref, side_ref, low_ref, lrt_ref, coef_ref, k_ref, acc, lrt_all):
    layers, rows, _ = own_ref.shape
    acc[...] = jnp.zeros_like(acc)
    for j in range(layers):

        @pl.when(me + j < layers)
        def _(j=j):
            low = rank * (layers - 1 - j)
            acc[0 : rank * (j + 1), :] += own_ref[me + j, low:rows, :].astype(f32)

    def inverse_rms(j):
        hi = side_ref[j, rows + 3 * rank : rows + 3 * rank + 1, :].astype(f32)
        return hi + side_ref[j, rows + 3 * rank + 1 : rows + 3 * rank + 2, :].astype(f32)

    def mean_of(grad, j):
        lrt = side_ref[j, rows : rows + rank, :].astype(f32)
        return jnp.sum(grad.astype(f32) * lrt, axis=0, keepdims=True) * (1.0 / width)

    for j in range(layers - 1, 0, -1):

        @pl.when(me + j < layers)
        def _(j=j):
            low = rank * (layers - 1 - j)
            grad = acc[rank * j : rank * (j + 1), :].astype(bf16)
            mean = mean_of(grad, j)
            w_hi = side_ref[j, rows + rank : rows + 2 * rank, :]
            w_lo = side_ref[j, rows + 2 * rank : rows + 3 * rank, :]
            term = tn(w_hi, grad) + tn(w_lo, grad)
            scaled_up = side_ref[j, low : rows - rank, :].astype(f32)
            acc[0 : rank * j, :] += inverse_rms(j) * (term[low : rows - rank, :] - mean * scaled_up)

    grad = acc[0:rank, :].astype(bf16)
    low_ref[...] = grad
    irms = inverse_rms(0)
    mean = mean_of(grad, 0)
    for j in range(layers):
        where = lax.rem(me + j, layers) * rank
        lrt_all[pl.ds(pl.multiple_of(where, rank), rank), :] = side_ref[j, rows : rows + rank, :]
    lrt_f = lrt_all[...].astype(f32)
    layer = lax.broadcasted_iota(jnp.int32, lrt_f.shape, 0) // rank
    lrt_ref[...] = jnp.where(layer <= me, lrt_f, 0.0).astype(bf16)
    below = jnp.where(layer < me, lrt_f, 0.0)
    coef_ref[...] = (below * (-irms * irms * mean)).astype(bf16)
    k_hi, k_lo = split2(nt(below.astype(bf16), (grad.astype(f32) * irms).astype(bf16)))
    k_ref[0] = k_hi
    k_ref[1] = k_lo


def part(start, loads, low, lrt, coef, k, own_in, stream_in, normed_in, dg_in, out_ref, buffer, out_sem):
    chunks, _, chunk = buffer.shape
    rows = lrt.shape[0]
    group = chunks // len(loads)
    width = group * chunk
    left = jnp.concatenate([lrt, coef], axis=1)
    k_hi, k_lo = k[0].astype(f32), k[1].astype(f32)
    k = jnp.concatenate([k_hi, k_hi, k_lo], axis=1).astype(bf16)
    stores = []
    for i, piece in enumerate(loads):
        for load in piece:
            load.wait()
        columns = pl.ds(pl.multiple_of(start + i * width, width), width)
        right = jnp.concatenate([own_in[1][:, columns], stream_in[1][:, columns]], axis=0)
        dg_hi = dg_in[1][0, :, columns]
        dg = jnp.concatenate([dg_hi, dg_in[1][1, :, columns], dg_hi], axis=0)
        up = nn(left, right) + nn(k, dg)
        down = nn(low, normed_in[1][:, columns])
        for j in range(group):
            buffer[i * group + j, :rows, :] = up[:, j * chunk : (j + 1) * chunk]
            buffer[i * group + j, rows:, :] = down[:, j * chunk : (j + 1) * chunk]
        here = pl.ds(i * group, group)
        stores.append(pltpu.make_async_copy(buffer.at[here], out_ref.at[here], out_sem.at[i]))
        stores[-1].start()
    for store in stores:
        store.wait()


def part_loads(start, large, chunks, chunk):
    pieces = min(4, chunks)
    width = chunks // pieces * chunk
    return [
        [columns_piece(item, i, pl.multiple_of(start + i * width, width), width) for item in large]
        for i in range(pieces)
    ]


def given_kernel(rank, count, meta_ref, own_up_in, *refs):
    sides, large = refs[:count], refs[count : count + 4]
    out_ref, low_ref, lrt_ref, coef_ref, k_ref, acc, lrt_all, side_ref, side_sem, buffer, out_sem = refs[count + 4 :]
    start, me = meta_ref[0], meta_ref[1]
    loads = part_loads(start, large, buffer.shape[0], buffer.shape[2])
    whole(own_up_in).start()
    for i, side in enumerate(sides):
        pltpu.make_async_copy(side, side_ref.at[i], side_sem).start()
    for load in loads:
        for item in load:
            item.start()
    whole(own_up_in).wait()
    pltpu.make_async_copy(side_ref, side_ref, side_sem).wait()
    solve(large[0][0].shape[1], rank, me, own_up_in[1], side_ref, low_ref, lrt_ref, coef_ref, k_ref, acc, lrt_all)
    part(start, loads, low_ref[...], lrt_ref[...], coef_ref[...], k_ref, *large, out_ref, buffer, out_sem)


def kept_kernel(meta_ref, low_in, lrt_in, coef_in, k_in, *refs):
    large, (out_ref, buffer, out_sem) = refs[:4], refs[4:]
    start = meta_ref[0]
    loads = part_loads(start, large, buffer.shape[0], buffer.shape[2])
    for item in (low_in, lrt_in, coef_in, k_in):
        whole(item).start()
    for load in loads:
        for item in load:
            item.start()
    for item in (low_in, lrt_in, coef_in, k_in):
        whole(item).wait()
    part(start, loads, low_in[1][...], lrt_in[1][...], coef_in[1][...], k_in[1], *large, out_ref, buffer, out_sem)


def part_shapes(chunks, chunk, rows, rank):
    shape = (chunks, rows + rank, chunk)
    return jax.ShapeDtypeStruct(shape, f32), (pltpu.VMEM(shape, f32), pltpu.SemaphoreType.DMA((4,)))


def given_part(meta, chunks, chunk, rank, own_up, sides, *large):
    layers, rows, tokens = own_up.shape
    shape, scratch = part_shapes(chunks, chunk, rows, rank)
    return call(
        functools.partial(given_kernel, rank, layers),
        "given",
        (
            shape,
            jax.ShapeDtypeStruct((rank, tokens), bf16),
            jax.ShapeDtypeStruct((rows, tokens), bf16),
            jax.ShapeDtypeStruct((rows, tokens), bf16),
            jax.ShapeDtypeStruct((2, rows, rank), bf16),
        ),
        (meta,),
        (own_up, *sides, *large),
        (1,) + (0,) * layers + (4,) * 4,
        (
            pltpu.VMEM((rows, tokens), f32),
            pltpu.VMEM((rows, tokens), bf16),
            pltpu.VMEM((layers,) + sides[0].shape, bf16),
            pltpu.SemaphoreType.DMA,
        )
        + scratch,
        in_place_outs=1,
    )


def kept_part(meta, chunks, chunk, low, lrt, coef, k, *large):
    shape, scratch = part_shapes(chunks, chunk, lrt.shape[0], low.shape[0])
    (found,) = call(
        kept_kernel,
        "kept",
        (shape,),
        (meta,),
        (low, lrt, coef, k, *large),
        (1,) * 4 + (4,) * 4,
        scratch,
        in_place_outs=1,
    )
    return found


def shards(
    layer_input_states,
    frozen_reference_states,
    adapter_down_weight,
    adapter_up_weight,
    layer_norm_gain,
    tile_reference_position,
    tile_harmful_flag,
    tile_valid_count,
):
    tokens, width = layer_input_states.shape[2:]
    rank = adapter_up_weight.shape[1]
    layers = lax.axis_size(SEC)
    me = lax.axis_index(SEC)
    core = lax.axis_index("core")
    cores = lax.axis_size("core")
    chips = lax.axis_size("y") * lax.axis_size("x")
    half = width // cores
    chunk = half // chips
    swap = [(i, (i + 1) % cores) for i in range(cores)]

    meta = jnp.stack([core, tile_harmful_flag[0], tile_valid_count[0]]).astype(jnp.int32)
    up_half = lax.dynamic_slice_in_dim(adapter_up_weight[0], core * half, half, axis=1)
    up_half, position = lax.optimization_barrier((up_half, tile_reference_position))
    fwd, bwd = ring_first(up_half, SEC)
    ordered = order(position, meta, frozen_reference_states[0])
    ordered, fwd, bwd = lax.optimization_barrier((ordered, fwd, bwd))
    refs = lax.all_to_all(ordered, DP, split_axis=0, concat_axis=0, tiled=True)
    _, stream, down, up, gains = lax.optimization_barrier(
        (ordered, layer_input_states[0, 0], adapter_down_weight[0], adapter_up_weight[0], layer_norm_gain)
    )

    normed, lrt, irms, dg = forward(stream, down, gains)
    mine = ring_gather(up_half, fwd, bwd, SEC, lrt)[::-1]
    other = [lax.ppermute(block, "core", swap) for block in mine]

    side = side_of(meta, stream, dg, lrt, irms, mine, other)
    sides = [side]
    for j in range(1, layers):
        sides.append(lax.ppermute(side, SEC, [(t, (t - j) % layers) for t in range(layers)]))

    refs, *sides = lax.optimization_barrier((refs, *sides))

    own, own_up = own_gradient(meta, refs, stream, up, lrt, mine, other)
    own_up = lax.all_to_all(own_up, SEC, 0, 0, tiled=True)

    large = (own, stream, normed, dg)
    away = jnp.stack([(1 - core) * half, me]).astype(jnp.int32)
    here = (core * half)[None].astype(jnp.int32)
    given, *coefs = given_part(away, chips, chunk, rank, own_up, sides, *large)
    received = lax.ppermute(given, "core", swap)
    kept = kept_part(here, chips, chunk, *coefs, *large)
    blocks = lax.all_to_all((kept + received).astype(bf16), CHIPS, 0, 0, tiled=True)
    grad_up = jnp.sum(blocks[:, : layers * rank].astype(f32), axis=0)
    grad_down = jnp.sum(blocks[:, layers * rank :].astype(f32), axis=0)

    by_layer = lax.all_to_all(grad_up.reshape(layers, rank, chunk), SEC, 0, 0, tiled=True)
    final = jnp.concatenate([grad_down, jnp.sum(by_layer, axis=0)], axis=0)
    wide = lax.all_to_all(jnp.broadcast_to(final, (chips,) + final.shape), CHIPS, 0, 0, tiled=True)
    mine = wide.transpose(1, 0, 2).reshape(2 * rank, half)
    other = lax.ppermute(mine, "core", swap)
    full = jnp.concatenate([jnp.where(core == 0, mine, other), jnp.where(core == 0, other, mine)], axis=1)
    return (full[None, :rank], full[None, rank:])


def solution(mesh):
    layers, dp = mesh.devices.shape
    cores = 2
    side = round((dp // cores) ** 0.5)
    mesh4 = Mesh(mesh.devices.reshape(layers, side, side, cores), (SEC,) + DP)
    return jax.shard_map(
        shards,
        mesh=mesh4,
        in_specs=(
            P(SEC, DP, None, None),
            P(SEC, None, None, DP),
            P(SEC, None, None),
            P(SEC, None, None),
            P(SEC, None),
            P(),
            P(DP),
            P(DP),
        ),
        out_specs=(P(SEC, None, None), P(SEC, None, None)),
        check_vma=False,
    )
```

```python
import functools

import jax
import jax.numpy as jnp
from jax import lax
from jax.experimental import pallas as pl
from jax.experimental.pallas import tpu as pltpu
from jax.sharding import Mesh
from jax.sharding import PartitionSpec as P

norm_eps = 1e-05
stat_eps = 1e-06
coef_reroute = 64.0
coef_retain = 1.0
loss_scale = 2048.0

SEC = "section"
CHIPS = ("y", "x")
DP = ("y", "x", "core")
f32 = jnp.float32
bf16 = jnp.bfloat16


def nt(left, right):
    return lax.dot_general(left, right, (((1,), (1,)), ((), ())), preferred_element_type=f32)


def tn(left, right):
    return lax.dot_general(left, right, (((0,), (0,)), ((), ())), preferred_element_type=f32)


def nn(left, right):
    return lax.dot_general(left, right, (((1,), (0,)), ((), ())), preferred_element_type=f32)


def split2(value):
    hi = value.astype(bf16)
    lo = (value - hi.astype(f32)).astype(bf16)
    return hi, lo


def ring_gather(block, axis, gate):
    n = lax.axis_size(axis)
    up = [(i, (i + 1) % n) for i in range(n)]
    down = [(i, (i - 1) % n) for i in range(n)]
    found = [None] * n
    found[0] = block
    fwd = bwd = block
    for k in range(1, n // 2 + 1):
        fwd = lax.ppermute(fwd, axis, up)
        found[k] = fwd
        if k < n - n // 2:
            bwd = lax.ppermute(bwd, axis, down)
            found[n - k] = bwd
        if k == 1:
            fwd, bwd, _ = lax.optimization_barrier((fwd, bwd, gate))
            found[1], found[n - 1] = fwd, bwd
    return found


def params(mib=63):
    return pltpu.CompilerParams(vmem_limit_bytes=mib << 20)


def smem():
    return pl.BlockSpec(memory_space=pltpu.SMEM)


def in_place():
    return pl.BlockSpec(memory_space=pl.ANY)


def vmem():
    return pl.BlockSpec(memory_space=pltpu.VMEM)


def call(kernel, name, out_shape, scalars, arrays, pieces, scratch=(), in_place_outs=0):
    count, total = len(scalars), len(arrays)
    outs = len(out_shape)
    buffered = [(a, n) for a, n in zip(arrays, pieces, strict=True) if n]

    def body(*refs):
        held = refs[count : count + total]
        first = count + total + outs
        buffers = iter(refs[first : first + len(buffered)])
        sems = iter(refs[first + len(buffered) : first + 2 * len(buffered)])
        inputs = [(h, next(buffers), next(sems)) if n else h for h, n in zip(held, pieces)]
        kernel(*refs[:count], *inputs, *refs[count + total : first], *refs[first + 2 * len(buffered) :])

    return pl.pallas_call(
        body,
        out_shape=out_shape,
        in_specs=[smem()] * count + [in_place()] * total,
        out_specs=[in_place()] * in_place_outs + [vmem()] * (outs - in_place_outs),
        scratch_shapes=[pltpu.VMEM(a.shape, a.dtype) for a, _ in buffered]
        + [pltpu.SemaphoreType.DMA((n,)) for _, n in buffered]
        + list(scratch),
        compiler_params=params(),
        cost_estimate=pl.CostEstimate(flops=COST[name] * 10**9, bytes_accessed=COST[name] * 3 * 10**6, transcendentals=0),
        name=name,
    )(*scalars, *arrays)


PIECES = 8
COST = dict(forward=4, side=5, own=8, given=5, kept=4)


def gather_into(blocks, buffer, sem):
    rows = blocks[0].shape[0]
    for i, block in enumerate(blocks):
        pltpu.make_async_copy(block, buffer.at[pl.ds(i * rows, rows)], sem).start()
    return pltpu.make_async_copy(buffer, buffer, sem)


def whole(item):
    held, buffer, sem = item
    return pltpu.make_async_copy(held, buffer, sem.at[0])


def columns_piece(item, i, start, width):
    held, buffer, sem = item
    where = (slice(None),) * (len(held.shape) - 1) + (pl.ds(start, width),)
    return pltpu.make_async_copy(held.at[where], buffer.at[where], sem.at[i])


def leading_piece(item, i, start, count):
    held, buffer, sem = item
    return pltpu.make_async_copy(held.at[pl.ds(start, count)], buffer.at[pl.ds(start, count)], sem.at[i])


INFO = 8


def order_kernel(position_ref, meta_ref, held_ref, out_ref, buffer, in_sem, out_sem):
    tiles, tokens, width = held_ref.shape
    groups = in_sem.shape[0]
    group = tiles // groups
    for i in range(tiles):
        pltpu.make_async_copy(
            held_ref.at[position_ref[i]], buffer.at[i, pl.ds(0, tokens)], in_sem.at[i // group]
        ).start()
    flag, valid = meta_ref[1], meta_ref[2]
    row = lax.broadcasted_iota(jnp.int32, (INFO, width), 0)
    here = ((row == 0) & (flag == 1)) | ((row == 1) & (flag != 1))
    info = jnp.where(here, valid, 0).astype(f32).astype(bf16)
    for i in range(tiles):
        buffer[i, tokens:, :] = info
    stores = []
    for i in range(groups):
        part = pl.ds(i * group, group)
        landed = buffer.at[part, pl.ds(0, tokens)]
        pltpu.make_async_copy(landed, landed, in_sem.at[i]).wait()
        stores.append(pltpu.make_async_copy(buffer.at[part], out_ref.at[part], out_sem.at[i]))
        stores[-1].start()
    for store in stores:
        store.wait()


def order(position, meta, held):
    tiles, tokens, width = held.shape
    shape = (tiles, tokens + INFO, width)
    return pl.pallas_call(
        order_kernel,
        out_shape=jax.ShapeDtypeStruct(shape, held.dtype),
        in_specs=[smem(), smem(), in_place()],
        out_specs=in_place(),
        scratch_shapes=[
            pltpu.VMEM(shape, held.dtype),
            pltpu.SemaphoreType.DMA((4,)),
            pltpu.SemaphoreType.DMA((4,)),
        ],
        compiler_params=params(),
        name="order",
    )(position, meta, held)


def fold(value):
    lanes = 128
    total = value[:, :lanes]
    for i in range(1, value.shape[1] // lanes):
        total = total + value[:, i * lanes : (i + 1) * lanes]
    return total


def forward_kernel(stream_in, down_in, gain_in, normed_ref, lrt_ref, irms_ref, dg_ref):
    stream_ref, down_ref, gain_ref = stream_in[1], down_in[1], gain_in[1]
    tokens, width = stream_ref.shape
    piece = width // PIECES
    loads = [columns_piece(stream_in, i, i * piece, piece) for i in range(PIECES)]
    for load in loads:
        load.start()
    whole(down_in).start()
    whole(gain_in).start()
    total = jnp.zeros((tokens, 128), f32)
    for i in range(PIECES):
        loads[i].wait()
        for low in range(i * piece, (i + 1) * piece, 256):
            x = stream_ref[:, low : low + 256].astype(f32)
            total = total + fold(x * x)
    irms = lax.rsqrt(jnp.sum(total, axis=1, keepdims=True) * (1.0 / width) + norm_eps)
    irms_ref[...] = jnp.broadcast_to(irms, (tokens, 128)).T[:8, :]
    whole(down_in).wait()
    whole(gain_in).wait()
    chunk = min(512, piece)

    def norm(i, acc):
        columns = pl.ds(pl.multiple_of(i * chunk, chunk), chunk)
        gain = gain_ref[:, columns]
        normed = (stream_ref[:, columns].astype(f32) * irms * gain).astype(bf16)
        normed_ref[:, columns] = normed
        down = down_ref[:, columns]
        hi, lo = split2(down.astype(f32) * gain)
        dg_ref[0, :, columns] = hi
        dg_ref[1, :, columns] = lo
        return acc + nt(down, normed)

    rank = down_ref.shape[0]
    low_rank = lax.fori_loop(0, width // chunk, norm, jnp.zeros((rank, tokens), f32), unroll=2)
    lrt_ref[...] = low_rank.astype(bf16)


def forward(stream, down, gain):
    rank = down.shape[0]
    tokens, width = stream.shape
    return call(
        forward_kernel,
        "forward",
        (
            jax.ShapeDtypeStruct((tokens, width), bf16),
            jax.ShapeDtypeStruct((rank, tokens), bf16),
            jax.ShapeDtypeStruct((8, tokens), f32),
            jax.ShapeDtypeStruct((2, rank, width), bf16),
        ),
        (),
        (stream, down, gain),
        (PIECES, 1, 1),
    )


def side_kernel(count, meta_ref, stream_in, dg_in, lrt_in, irms_in, *refs):
    mine, other, (out_ref, up_ref, up_sem) = refs[:count], refs[count : 2 * count], refs[2 * count :]
    core = meta_ref[0]
    rank, half = mine[0].shape
    tokens = stream_in[1].shape[0]
    rows = count * rank
    chunk = min(1024, half)
    ready = [gather_into(mine, up_ref.at[0], up_sem.at[0])]
    for item in (stream_in, dg_in):
        whole(item).start()
    ready.append(gather_into(other, up_ref.at[1], up_sem.at[1]))
    for item in (lrt_in, irms_in):
        whole(item).start()
    for item in (stream_in, dg_in):
        whole(item).wait()
    stream_ref, dg_ref = stream_in[1], dg_in[1]
    total = jnp.zeros((rows, tokens + 2 * rank), f32)
    for which, base in enumerate((core, 1 - core)):
        ready[which].wait()

        def step(i, acc, which=which, base=base):
            local = pl.ds(pl.multiple_of(i * chunk, chunk), chunk)
            columns = pl.ds(pl.multiple_of(base * half + i * chunk, chunk), chunk)
            right = jnp.concatenate([stream_ref[:, columns], dg_ref[0, :, columns], dg_ref[1, :, columns]], axis=0)
            return acc + nt(up_ref[which, :, local], right)

        total = lax.fori_loop(0, half // chunk, step, total, unroll=2)
    whole(lrt_in).wait()
    whole(irms_in).wait()
    irms = irms_in[1][0:1, :]
    w = total[:, tokens : tokens + rank] + total[:, tokens + rank :]
    w = jnp.concatenate([w, jnp.zeros((rows, 128 - rank), f32)], axis=1).T[:rank, :]
    w_hi, w_lo = split2(w)
    irms_hi = irms.astype(bf16).astype(f32)
    row = lax.broadcasted_iota(jnp.int32, (rank, tokens), 0)
    last = jnp.where(row == 0, irms_hi, jnp.where(row == 1, irms - irms_hi, 0.0)).astype(bf16)
    scaled_up = (total[:, :tokens] * irms).astype(bf16)
    for i in range(out_ref.shape[0]):
        out_ref[i, :rows, :] = scaled_up
        out_ref[i, rows : rows + rank, :] = lrt_in[1][...]
        out_ref[i, rows + rank : rows + 2 * rank, :] = w_hi
        out_ref[i, rows + 2 * rank : rows + 3 * rank, :] = w_lo
        out_ref[i, rows + 3 * rank :, :] = last


def up_scratch(mine):
    rank, half = mine[0].shape
    return (pltpu.VMEM((2, len(mine) * rank, half), bf16), pltpu.SemaphoreType.DMA((2,)))


def side_of(meta, stream, dg, lrt, irms, mine, other):
    layers = len(mine)
    rank = lrt.shape[0]
    (side,) = call(
        functools.partial(side_kernel, layers),
        "side",
        (jax.ShapeDtypeStruct((layers, (layers + 4) * rank, stream.shape[0]), bf16),),
        (meta,),
        (stream, dg, lrt, irms, *mine, *other),
        (1, 1, 1, 1) + (0,) * (2 * layers),
        up_scratch(mine),
    )
    return side


def own_kernel(count, meta_ref, refs_in, stream_in, up_in, lrt_in, *refs):
    mine, other = refs[:count], refs[count : 2 * count]
    own_ref, proj_ref, output_ref, ups_ref, up_sem = refs[2 * count :]
    core, flag, valid = meta_ref[0], meta_ref[1], meta_ref[2]
    refs_ref, stream_ref, up_ref = refs_in[1], stream_in[1], up_in[1]
    tiles, padded, chunk = refs_ref.shape
    tokens = padded - INFO
    half = mine[0].shape[1]
    per_half = half // chunk
    per_piece = tiles // PIECES
    width = per_piece * chunk

    whole(lrt_in).start()
    whole(up_in).start()
    stream_loads = [columns_piece(stream_in, i, i * width, width) for i in range(PIECES)]
    ref_loads = [leading_piece(refs_in, i, i * per_piece, per_piece) for i in range(PIECES)]
    for i in range(PIECES):
        stream_loads[i].start()
        ref_loads[i].start()
    ready = [gather_into(blocks, ups_ref.at[i], up_sem.at[i]) for i, blocks in enumerate((mine, other))]
    whole(lrt_in).wait()
    whole(up_in).wait()
    low_rank = lrt_in[1][...].astype(f32).T.astype(bf16)
    is_valid = lax.broadcasted_iota(jnp.int32, (tokens, 1), 0) < valid

    def weight(row):
        info = refs_ref[0, tokens:, :128].astype(f32)
        for i in range(1, tiles):
            info = info + refs_ref[i, tokens:, :128].astype(f32)
        return loss_scale / info[row : row + 1, 0:1]

    def stats(terms, number):
        acc = [jnp.zeros((tokens, 128), f32) for _ in range(number)]
        for i in range(PIECES):
            stream_loads[i].wait()
            ref_loads[i].wait()
            for j in range(i * per_piece, (i + 1) * per_piece):
                columns = slice(j * chunk, (j + 1) * chunk)
                out = stream_ref[:, columns].astype(f32) + nn(low_rank, up_ref[:, columns])
                output_ref[:, columns] = out
                ref = refs_ref[j, :tokens, :].astype(f32)
                acc = [a + fold(v) for a, v in zip(acc, terms(out, ref))]
        return [jnp.sum(a, axis=1, keepdims=True) for a in acc]

    group = min(4, per_half)

    def finish(make):
        for wait in ready:
            wait.wait()
        total = jnp.zeros(proj_ref.shape[1:], f32)
        for which, base in enumerate((core, 1 - core)):

            def step(i, acc, which=which, base=base):
                parts = []
                for g in range(group):
                    j = base * per_half + i * group + g
                    columns = pl.ds(pl.multiple_of(j * chunk, chunk), chunk)
                    own = make(output_ref[:, columns], refs_ref[j, :tokens, :].astype(f32)).astype(bf16)
                    own_ref[:, columns] = own
                    parts.append(own)
                local = pl.ds(pl.multiple_of(i * group * chunk, group * chunk), group * chunk)
                return acc + nt(ups_ref[which, :, local], jnp.concatenate(parts, axis=1))

            total = lax.fori_loop(0, per_half // group, step, total, unroll=2)
        total = total.astype(bf16)
        for i in range(proj_ref.shape[0]):
            proj_ref[i] = total

    @pl.when(flag == 1)
    def _():
        out_sq, ref_sq, cross = stats(lambda o, r: (o * o, r * r, o * r), 3)
        out_norm = jnp.sqrt(out_sq + stat_eps)
        ref_norm = jnp.sqrt(ref_sq + stat_eps)
        cosine = cross / (out_norm * ref_norm)
        on = jnp.where(is_valid & (cosine > 0), coef_reroute * weight(0), 0.0)
        coef_ref = on / (out_norm * ref_norm)
        coef_out = on * cosine / (out_sq + stat_eps)
        finish(lambda o, r: coef_ref * r - coef_out * o)

    @pl.when(flag != 1)
    def _():
        (diff_sq,) = stats(lambda o, r: ((o - r) * (o - r),), 1)
        coef = jnp.where(is_valid, coef_retain * weight(1), 0.0) / jnp.sqrt(diff_sq + stat_eps)
        finish(lambda o, r: coef * (o - r))


def own_gradient(meta, refs, stream, up, lrt, mine, other):
    layers = len(mine)
    return call(
        functools.partial(own_kernel, layers),
        "own",
        (
            jax.ShapeDtypeStruct(stream.shape, bf16),
            jax.ShapeDtypeStruct((layers, layers * up.shape[0], stream.shape[0]), bf16),
        ),
        (meta,),
        (refs, stream, up, lrt, *mine, *other),
        (PIECES, PIECES, 1, 1) + (0,) * (2 * layers),
        (pltpu.VMEM(stream.shape, f32),) + up_scratch(mine),
    )


def solve(width, rank, me, own_ref, side_ref, low_ref, lrt_ref, coef_ref, k_ref, acc):
    layers, rows, _ = own_ref.shape
    acc[...] = jnp.zeros_like(acc)
    for j in range(layers):

        @pl.when(me + j < layers)
        def _(j=j):
            low = rank * (layers - 1 - j)
            acc[0 : rank * (j + 1), :] += own_ref[me + j, low:rows, :].astype(f32)

    def inverse_rms(t):
        hi = side_ref[t, rows + 3 * rank : rows + 3 * rank + 1, :].astype(f32)
        return hi + side_ref[t, rows + 3 * rank + 1 : rows + 3 * rank + 2, :].astype(f32)

    def mean_of(grad, t):
        lrt = side_ref[t, rows : rows + rank, :].astype(f32)
        return jnp.sum(grad.astype(f32) * lrt, axis=0, keepdims=True) * (1.0 / width)

    for j in range(layers - 1, 0, -1):

        @pl.when(me + j < layers)
        def _(j=j):
            t = me + j
            low = rank * (layers - 1 - j)
            grad = acc[rank * j : rank * (j + 1), :].astype(bf16)
            mean = mean_of(grad, t)
            w_hi = side_ref[t, rows + rank : rows + 2 * rank, :]
            w_lo = side_ref[t, rows + 2 * rank : rows + 3 * rank, :]
            term = tn(w_hi, grad) + tn(w_lo, grad)
            scaled_up = side_ref[t, low : rows - rank, :].astype(f32)
            acc[0 : rank * j, :] += inverse_rms(t) * (term[low : rows - rank, :] - mean * scaled_up)

    grad = acc[0:rank, :].astype(bf16)
    low_ref[...] = grad
    irms = inverse_rms(me)
    mean = mean_of(grad, me)
    lrt_f = side_ref[:, rows : rows + rank, :].reshape(layers * rank, -1).astype(f32)
    layer = lax.broadcasted_iota(jnp.int32, lrt_f.shape, 0) // rank
    lrt_ref[...] = jnp.where(layer <= me, lrt_f, 0.0).astype(bf16)
    below = jnp.where(layer < me, lrt_f, 0.0)
    coef_ref[...] = (below * (-irms * irms * mean)).astype(bf16)
    k_hi, k_lo = split2(nt(below.astype(bf16), (grad.astype(f32) * irms).astype(bf16)))
    k_ref[0] = k_hi
    k_ref[1] = k_lo


def part(start, loads, low, lrt, coef, k, own_in, stream_in, normed_in, dg_in, out_ref, buffer, out_sem):
    chunks, _, chunk = buffer.shape
    rows = lrt.shape[0]
    group = chunks // len(loads)
    width = group * chunk
    left = jnp.concatenate([lrt, coef], axis=1)
    k_hi, k_lo = k[0].astype(f32), k[1].astype(f32)
    k = jnp.concatenate([k_hi, k_hi, k_lo], axis=1).astype(bf16)
    stores = []
    for i, piece in enumerate(loads):
        for load in piece:
            load.wait()
        columns = pl.ds(pl.multiple_of(start + i * width, width), width)
        right = jnp.concatenate([own_in[1][:, columns], stream_in[1][:, columns]], axis=0)
        dg_hi = dg_in[1][0, :, columns]
        dg = jnp.concatenate([dg_hi, dg_in[1][1, :, columns], dg_hi], axis=0)
        up = nn(left, right) + nn(k, dg)
        down = nn(low, normed_in[1][:, columns])
        for j in range(group):
            buffer[i * group + j, :rows, :] = up[:, j * chunk : (j + 1) * chunk]
            buffer[i * group + j, rows:, :] = down[:, j * chunk : (j + 1) * chunk]
        here = pl.ds(i * group, group)
        stores.append(pltpu.make_async_copy(buffer.at[here], out_ref.at[here], out_sem.at[i]))
        stores[-1].start()
    for store in stores:
        store.wait()


def part_loads(start, large, chunks, chunk):
    pieces = min(4, chunks)
    width = chunks // pieces * chunk
    return [
        [columns_piece(item, i, pl.multiple_of(start + i * width, width), width) for item in large]
        for i in range(pieces)
    ]


def given_kernel(rank, meta_ref, own_up_in, side_in, *refs):
    large, (out_ref, low_ref, lrt_ref, coef_ref, k_ref, acc, buffer, out_sem) = refs[:4], refs[4:]
    start, me = meta_ref[0], meta_ref[1]
    loads = part_loads(start, large, buffer.shape[0], buffer.shape[2])
    for item in (own_up_in, side_in):
        whole(item).start()
    for load in loads:
        for item in load:
            item.start()
    for item in (own_up_in, side_in):
        whole(item).wait()
    solve(large[0][0].shape[1], rank, me, own_up_in[1], side_in[1], low_ref, lrt_ref, coef_ref, k_ref, acc)
    part(start, loads, low_ref[...], lrt_ref[...], coef_ref[...], k_ref, *large, out_ref, buffer, out_sem)


def kept_kernel(meta_ref, low_in, lrt_in, coef_in, k_in, *refs):
    large, (out_ref, buffer, out_sem) = refs[:4], refs[4:]
    start = meta_ref[0]
    loads = part_loads(start, large, buffer.shape[0], buffer.shape[2])
    for item in (low_in, lrt_in, coef_in, k_in):
        whole(item).start()
    for load in loads:
        for item in load:
            item.start()
    for item in (low_in, lrt_in, coef_in, k_in):
        whole(item).wait()
    part(start, loads, low_in[1][...], lrt_in[1][...], coef_in[1][...], k_in[1], *large, out_ref, buffer, out_sem)


def part_shapes(chunks, chunk, rows, rank):
    shape = (chunks, rows + rank, chunk)
    return jax.ShapeDtypeStruct(shape, f32), (pltpu.VMEM(shape, f32), pltpu.SemaphoreType.DMA((4,)))


def given_part(meta, chunks, chunk, rank, own_up, sides, *large):
    _, rows, tokens = own_up.shape
    shape, scratch = part_shapes(chunks, chunk, rows, rank)
    return call(
        functools.partial(given_kernel, rank),
        "given",
        (
            shape,
            jax.ShapeDtypeStruct((rank, tokens), bf16),
            jax.ShapeDtypeStruct((rows, tokens), bf16),
            jax.ShapeDtypeStruct((rows, tokens), bf16),
            jax.ShapeDtypeStruct((2, rows, rank), bf16),
        ),
        (meta,),
        (own_up, sides, *large),
        (1, 1) + (4,) * 4,
        (pltpu.VMEM((rows, tokens), f32),)
        + scratch,
        in_place_outs=1,
    )


def kept_part(meta, chunks, chunk, low, lrt, coef, k, *large):
    shape, scratch = part_shapes(chunks, chunk, lrt.shape[0], low.shape[0])
    (found,) = call(
        kept_kernel,
        "kept",
        (shape,),
        (meta,),
        (low, lrt, coef, k, *large),
        (1,) * 4 + (4,) * 4,
        scratch,
        in_place_outs=1,
    )
    return found


def shards(
    layer_input_states,
    frozen_reference_states,
    adapter_down_weight,
    adapter_up_weight,
    layer_norm_gain,
    tile_reference_position,
    tile_harmful_flag,
    tile_valid_count,
):
    tokens, width = layer_input_states.shape[2:]
    rank = adapter_up_weight.shape[1]
    layers = lax.axis_size(SEC)
    me = lax.axis_index(SEC)
    core = lax.axis_index("core")
    cores = lax.axis_size("core")
    chips = lax.axis_size("y") * lax.axis_size("x")
    half = width // cores
    chunk = half // chips
    swap = [(i, (i + 1) % cores) for i in range(cores)]

    meta = jnp.stack([core, tile_harmful_flag[0], tile_valid_count[0]]).astype(jnp.int32)
    up_half = lax.dynamic_slice_in_dim(adapter_up_weight[0], core * half, half, axis=1)
    up_half, position = lax.optimization_barrier((up_half, tile_reference_position))
    ordered = order(position, meta, frozen_reference_states[0])
    refs = lax.all_to_all(ordered, DP, split_axis=0, concat_axis=0, tiled=True)
    _, stream, down, up, gains = lax.optimization_barrier(
        (ordered, layer_input_states[0, 0], adapter_down_weight[0], adapter_up_weight[0], layer_norm_gain)
    )

    normed, lrt, irms, dg = forward(stream, down, gains)
    mine = ring_gather(up_half, SEC, lrt)[::-1]
    other = [lax.ppermute(block, "core", swap) for block in mine]

    side = side_of(meta, stream, dg, lrt, irms, mine, other)
    sides = lax.all_to_all(side, SEC, 0, 0, tiled=True)

    own, own_up = own_gradient(meta, refs, stream, up, lrt, mine, other)
    own_up = lax.all_to_all(own_up, SEC, 0, 0, tiled=True)

    large = (own, stream, normed, dg)
    away = jnp.stack([(1 - core) * half, me]).astype(jnp.int32)
    here = (core * half)[None].astype(jnp.int32)
    given, *coefs = given_part(away, chips, chunk, rank, own_up, sides, *large)
    received = lax.ppermute(given, "core", swap)
    kept = kept_part(here, chips, chunk, *coefs, *large)
    blocks = lax.all_to_all((kept + received).astype(bf16), CHIPS, 0, 0, tiled=True)
    grad_up = jnp.sum(blocks[:, : layers * rank].astype(f32), axis=0)
    grad_down = jnp.sum(blocks[:, layers * rank :].astype(f32), axis=0)

    by_layer = lax.all_to_all(grad_up.reshape(layers, rank, chunk), SEC, 0, 0, tiled=True)
    final = jnp.concatenate([grad_down, jnp.sum(by_layer, axis=0)], axis=0)
    wide = lax.all_to_all(jnp.broadcast_to(final, (chips,) + final.shape), CHIPS, 0, 0, tiled=True)
    mine = wide.transpose(1, 0, 2).reshape(2 * rank, half)
    other = lax.ppermute(mine, "core", swap)
    full = jnp.concatenate([jnp.where(core == 0, mine, other), jnp.where(core == 0, other, mine)], axis=1)
    return (full[None, :rank], full[None, rank:])


def solution(mesh):
    layers, dp = mesh.devices.shape
    cores = 2
    side = round((dp // cores) ** 0.5)
    mesh4 = Mesh(mesh.devices.reshape(layers, side, side, cores), (SEC,) + DP)
    return jax.shard_map(
        shards,
        mesh=mesh4,
        in_specs=(
            P(SEC, DP, None, None),
            P(SEC, None, None, DP),
            P(SEC, None, None),
            P(SEC, None, None),
            P(SEC, None),
            P(),
            P(DP),
            P(DP),
        ),
        out_specs=(P(SEC, None, None), P(SEC, None, None)),
        check_vma=False,
    )
```

```python
import functools

import jax
import jax.numpy as jnp
from jax import lax
from jax.experimental import pallas as pl
from jax.experimental.pallas import tpu as pltpu
from jax.sharding import Mesh
from jax.sharding import PartitionSpec as P

norm_eps = 1e-05
stat_eps = 1e-06
coef_reroute = 64.0
coef_retain = 1.0
loss_scale = 2048.0

SEC = "section"
CHIPS = ("y", "x")
DP = ("y", "x", "core")
f32 = jnp.float32
bf16 = jnp.bfloat16


def nt(left, right):
    return lax.dot_general(left, right, (((1,), (1,)), ((), ())), preferred_element_type=f32)


def tn(left, right):
    return lax.dot_general(left, right, (((0,), (0,)), ((), ())), preferred_element_type=f32)


def nn(left, right):
    return lax.dot_general(left, right, (((1,), (0,)), ((), ())), preferred_element_type=f32)


def split2(value):
    hi = value.astype(bf16)
    lo = (value - hi.astype(f32)).astype(bf16)
    return hi, lo


def ring_gather(block, axis, gate):
    n = lax.axis_size(axis)
    up = [(i, (i + 1) % n) for i in range(n)]
    down = [(i, (i - 1) % n) for i in range(n)]
    found = [None] * n
    found[0] = block
    fwd = bwd = block
    for k in range(1, n // 2 + 1):
        fwd = lax.ppermute(fwd, axis, up)
        found[k] = fwd
        if k < n - n // 2:
            bwd = lax.ppermute(bwd, axis, down)
            found[n - k] = bwd
        if k == 1:
            fwd, bwd, _ = lax.optimization_barrier((fwd, bwd, gate))
            found[1], found[n - 1] = fwd, bwd
    return found


def params(mib=63):
    return pltpu.CompilerParams(vmem_limit_bytes=mib << 20)


def smem():
    return pl.BlockSpec(memory_space=pltpu.SMEM)


def in_place():
    return pl.BlockSpec(memory_space=pl.ANY)


def vmem():
    return pl.BlockSpec(memory_space=pltpu.VMEM)


def call(kernel, name, out_shape, scalars, arrays, pieces, scratch=(), in_place_outs=0):
    count, total = len(scalars), len(arrays)
    outs = len(out_shape)
    buffered = [(a, n) for a, n in zip(arrays, pieces, strict=True) if n]

    def body(*refs):
        held = refs[count : count + total]
        first = count + total + outs
        buffers = iter(refs[first : first + len(buffered)])
        sems = iter(refs[first + len(buffered) : first + 2 * len(buffered)])
        inputs = [(h, next(buffers), next(sems)) if n else h for h, n in zip(held, pieces)]
        kernel(*refs[:count], *inputs, *refs[count + total : first], *refs[first + 2 * len(buffered) :])

    return pl.pallas_call(
        body,
        out_shape=out_shape,
        in_specs=[smem()] * count + [in_place()] * total,
        out_specs=[in_place()] * in_place_outs + [vmem()] * (outs - in_place_outs),
        scratch_shapes=[pltpu.VMEM(a.shape, a.dtype) for a, _ in buffered]
        + [pltpu.SemaphoreType.DMA((n,)) for _, n in buffered]
        + list(scratch),
        compiler_params=params(),
        cost_estimate=pl.CostEstimate(flops=COST[name] * 10**9, bytes_accessed=COST[name] * 3 * 10**6, transcendentals=0),
        name=name,
    )(*scalars, *arrays)


PIECES = 8
COST = dict(forward=4, own=8, given=5, kept=4)


def gather_into(blocks, buffer, sem):
    rows = blocks[0].shape[0]
    for i, block in enumerate(blocks):
        pltpu.make_async_copy(block, buffer.at[pl.ds(i * rows, rows)], sem).start()
    return pltpu.make_async_copy(buffer, buffer, sem)


def whole(item):
    held, buffer, sem = item
    return pltpu.make_async_copy(held, buffer, sem.at[0])


def columns_piece(item, i, start, width):
    held, buffer, sem = item
    where = (slice(None),) * (len(held.shape) - 1) + (pl.ds(start, width),)
    return pltpu.make_async_copy(held.at[where], buffer.at[where], sem.at[i])


def leading_piece(item, i, start, count):
    held, buffer, sem = item
    return pltpu.make_async_copy(held.at[pl.ds(start, count)], buffer.at[pl.ds(start, count)], sem.at[i])


INFO = 8


def order_kernel(position_ref, meta_ref, held_ref, out_ref, buffer, in_sem, out_sem):
    tiles, tokens, width = held_ref.shape
    groups = in_sem.shape[0]
    group = tiles // groups
    for i in range(tiles):
        pltpu.make_async_copy(
            held_ref.at[position_ref[i]], buffer.at[i, pl.ds(0, tokens)], in_sem.at[i // group]
        ).start()
    flag, valid = meta_ref[1], meta_ref[2]
    row = lax.broadcasted_iota(jnp.int32, (INFO, width), 0)
    here = ((row == 0) & (flag == 1)) | ((row == 1) & (flag != 1))
    info = jnp.where(here, valid, 0).astype(f32).astype(bf16)
    for i in range(tiles):
        buffer[i, tokens:, :] = info
    stores = []
    for i in range(groups):
        part = pl.ds(i * group, group)
        landed = buffer.at[part, pl.ds(0, tokens)]
        pltpu.make_async_copy(landed, landed, in_sem.at[i]).wait()
        stores.append(pltpu.make_async_copy(buffer.at[part], out_ref.at[part], out_sem.at[i]))
        stores[-1].start()
    for store in stores:
        store.wait()


def order(position, meta, held):
    tiles, tokens, width = held.shape
    shape = (tiles, tokens + INFO, width)
    return pl.pallas_call(
        order_kernel,
        out_shape=jax.ShapeDtypeStruct(shape, held.dtype),
        in_specs=[smem(), smem(), in_place()],
        out_specs=in_place(),
        scratch_shapes=[
            pltpu.VMEM(shape, held.dtype),
            pltpu.SemaphoreType.DMA((4,)),
            pltpu.SemaphoreType.DMA((4,)),
        ],
        compiler_params=params(),
        name="order",
    )(position, meta, held)


def fold(value):
    lanes = 128
    total = value[:, :lanes]
    for i in range(1, value.shape[1] // lanes):
        total = total + value[:, i * lanes : (i + 1) * lanes]
    return total


def forward_kernel(stream_in, down_in, gain_in, normed_ref, lrt_ref, irms_ref, dg_ref):
    stream_ref, down_ref, gain_ref = stream_in[1], down_in[1], gain_in[1]
    tokens, width = stream_ref.shape
    piece = width // PIECES
    loads = [columns_piece(stream_in, i, i * piece, piece) for i in range(PIECES)]
    for load in loads:
        load.start()
    whole(down_in).start()
    whole(gain_in).start()
    total = jnp.zeros((tokens, 128), f32)
    for i in range(PIECES):
        loads[i].wait()
        for low in range(i * piece, (i + 1) * piece, 256):
            x = stream_ref[:, low : low + 256].astype(f32)
            total = total + fold(x * x)
    irms = lax.rsqrt(jnp.sum(total, axis=1, keepdims=True) * (1.0 / width) + norm_eps)
    irms_ref[...] = jnp.broadcast_to(irms, (tokens, 128)).T[:8, :]
    whole(down_in).wait()
    whole(gain_in).wait()
    chunk = min(512, piece)

    def norm(i, acc):
        columns = pl.ds(pl.multiple_of(i * chunk, chunk), chunk)
        gain = gain_ref[:, columns]
        normed = (stream_ref[:, columns].astype(f32) * irms * gain).astype(bf16)
        normed_ref[:, columns] = normed
        down = down_ref[:, columns]
        hi, lo = split2(down.astype(f32) * gain)
        dg_ref[0, :, columns] = hi
        dg_ref[1, :, columns] = lo
        return acc + nt(down, normed)

    rank = down_ref.shape[0]
    low_rank = lax.fori_loop(0, width // chunk, norm, jnp.zeros((rank, tokens), f32), unroll=2)
    lrt_ref[...] = low_rank.astype(bf16)


def forward(stream, down, gain):
    rank = down.shape[0]
    tokens, width = stream.shape
    return call(
        forward_kernel,
        "forward",
        (
            jax.ShapeDtypeStruct((tokens, width), bf16),
            jax.ShapeDtypeStruct((rank, tokens), bf16),
            jax.ShapeDtypeStruct((8, tokens), f32),
            jax.ShapeDtypeStruct((2, rank, width), bf16),
        ),
        (),
        (stream, down, gain),
        (PIECES, 1, 1),
    )


def up_scratch(mine):
    rank, half = mine[0].shape
    return (pltpu.VMEM((2, len(mine) * rank, half), bf16), pltpu.SemaphoreType.DMA((2,)))


def own_kernel(count, meta_ref, refs_in, stream_in, up_in, lrt_in, dg_in, irms_in, *refs):
    mine, other = refs[:count], refs[count : 2 * count]
    own_ref, out_ref, output_ref, ups_ref, up_sem = refs[2 * count :]
    rank = lrt_in[1].shape[0]
    rows = count * rank
    dg_ref = dg_in[1]
    core, flag, valid = meta_ref[0], meta_ref[1], meta_ref[2]
    refs_ref, stream_ref, up_ref = refs_in[1], stream_in[1], up_in[1]
    tiles, padded, chunk = refs_ref.shape
    tokens = padded - INFO
    half = mine[0].shape[1]
    per_half = half // chunk
    per_piece = tiles // PIECES
    width = per_piece * chunk

    whole(lrt_in).start()
    whole(up_in).start()
    stream_loads = [columns_piece(stream_in, i, i * width, width) for i in range(PIECES)]
    ref_loads = [leading_piece(refs_in, i, i * per_piece, per_piece) for i in range(PIECES)]
    for i in range(PIECES):
        stream_loads[i].start()
        ref_loads[i].start()
    ready = [gather_into(blocks, ups_ref.at[i], up_sem.at[i]) for i, blocks in enumerate((mine, other))]
    for item in (dg_in, irms_in):
        whole(item).start()
        ready.append(whole(item))
    whole(lrt_in).wait()
    whole(up_in).wait()
    low_rank = lrt_in[1][...].astype(f32).T.astype(bf16)
    is_valid = lax.broadcasted_iota(jnp.int32, (tokens, 1), 0) < valid

    def weight(row):
        info = refs_ref[0, tokens:, :128].astype(f32)
        for i in range(1, tiles):
            info = info + refs_ref[i, tokens:, :128].astype(f32)
        return loss_scale / info[row : row + 1, 0:1]

    def stats(terms, number):
        acc = [jnp.zeros((tokens, 128), f32) for _ in range(number)]
        for i in range(PIECES):
            stream_loads[i].wait()
            ref_loads[i].wait()
            for j in range(i * per_piece, (i + 1) * per_piece):
                columns = slice(j * chunk, (j + 1) * chunk)
                out = stream_ref[:, columns].astype(f32) + nn(low_rank, up_ref[:, columns])
                output_ref[:, columns] = out
                ref = refs_ref[j, :tokens, :].astype(f32)
                acc = [a + fold(v) for a, v in zip(acc, terms(out, ref))]
        return [jnp.sum(a, axis=1, keepdims=True) for a in acc]

    group = min(4, per_half)

    def finish(make):
        for wait in ready:
            wait.wait()
        total = jnp.zeros((rows, 2 * tokens + 2 * rank), f32)
        for which, base in enumerate((core, 1 - core)):

            def step(i, acc, which=which, base=base):
                parts = []
                for g in range(group):
                    j = base * per_half + i * group + g
                    columns = pl.ds(pl.multiple_of(j * chunk, chunk), chunk)
                    own = make(output_ref[:, columns], refs_ref[j, :tokens, :].astype(f32)).astype(bf16)
                    own_ref[:, columns] = own
                    parts.append(own)
                size = group * chunk
                local = pl.ds(pl.multiple_of(i * size, size), size)
                columns = pl.ds(pl.multiple_of(base * half + i * size, size), size)
                right = [jnp.concatenate(parts, axis=1), stream_ref[:, columns], dg_ref[0, :, columns], dg_ref[1, :, columns]]
                return acc + nt(ups_ref[which, :, local], jnp.concatenate(right, axis=0))

            total = lax.fori_loop(0, per_half // group, step, total, unroll=2)

        irms = irms_in[1][0:1, :]
        own_up = total[:, :tokens].astype(bf16)
        scaled_up = (total[:, tokens : 2 * tokens] * irms).astype(bf16)
        w = total[:, 2 * tokens : 2 * tokens + rank] + total[:, 2 * tokens + rank :]
        w = jnp.concatenate([w, jnp.zeros((rows, 128 - rank), f32)], axis=1).T[:rank, :]
        w_hi, w_lo = split2(w)
        irms_hi = irms.astype(bf16).astype(f32)
        row = lax.broadcasted_iota(jnp.int32, (rank, tokens), 0)
        last = jnp.where(row == 0, irms_hi, jnp.where(row == 1, irms - irms_hi, 0.0)).astype(bf16)
        for i in range(out_ref.shape[0]):
            low = 0
            for value in (scaled_up, lrt_in[1][...], w_hi, w_lo, last, own_up):
                out_ref[i, low : low + value.shape[0], :] = value
                low += value.shape[0]

    @pl.when(flag == 1)
    def _():
        out_sq, ref_sq, cross = stats(lambda o, r: (o * o, r * r, o * r), 3)
        out_norm = jnp.sqrt(out_sq + stat_eps)
        ref_norm = jnp.sqrt(ref_sq + stat_eps)
        cosine = cross / (out_norm * ref_norm)
        on = jnp.where(is_valid & (cosine > 0), coef_reroute * weight(0), 0.0)
        coef_ref = on / (out_norm * ref_norm)
        coef_out = on * cosine / (out_sq + stat_eps)
        finish(lambda o, r: coef_ref * r - coef_out * o)

    @pl.when(flag != 1)
    def _():
        (diff_sq,) = stats(lambda o, r: ((o - r) * (o - r),), 1)
        coef = jnp.where(is_valid, coef_retain * weight(1), 0.0) / jnp.sqrt(diff_sq + stat_eps)
        finish(lambda o, r: coef * (o - r))


def own_gradient(meta, refs, stream, up, lrt, dg, irms, mine, other):
    layers = len(mine)
    rank = up.shape[0]
    return call(
        functools.partial(own_kernel, layers),
        "own",
        (
            jax.ShapeDtypeStruct(stream.shape, bf16),
            jax.ShapeDtypeStruct((layers, (2 * layers + 4) * rank, stream.shape[0]), bf16),
        ),
        (meta,),
        (refs, stream, up, lrt, dg, irms, *mine, *other),
        (PIECES, PIECES, 1, 1, 1, 1) + (0,) * (2 * layers),
        (pltpu.VMEM(stream.shape, f32),) + up_scratch(mine),
    )


def solve(width, rank, me, side_ref, low_ref, lrt_ref, coef_ref, k_ref, acc):
    layers = side_ref.shape[0]
    rows = layers * rank
    first = rows + 4 * rank
    acc[...] = jnp.zeros_like(acc)
    for j in range(layers):

        @pl.when(me + j < layers)
        def _(j=j):
            low = rank * (layers - 1 - j)
            acc[0 : rank * (j + 1), :] += side_ref[me + j, first + low : first + rows, :].astype(f32)

    def inverse_rms(t):
        hi = side_ref[t, rows + 3 * rank : rows + 3 * rank + 1, :].astype(f32)
        return hi + side_ref[t, rows + 3 * rank + 1 : rows + 3 * rank + 2, :].astype(f32)

    def mean_of(grad, t):
        lrt = side_ref[t, rows : rows + rank, :].astype(f32)
        return jnp.sum(grad.astype(f32) * lrt, axis=0, keepdims=True) * (1.0 / width)

    for j in range(layers - 1, 0, -1):

        @pl.when(me + j < layers)
        def _(j=j):
            t = me + j
            low = rank * (layers - 1 - j)
            grad = acc[rank * j : rank * (j + 1), :].astype(bf16)
            mean = mean_of(grad, t)
            w_hi = side_ref[t, rows + rank : rows + 2 * rank, :]
            w_lo = side_ref[t, rows + 2 * rank : rows + 3 * rank, :]
            term = tn(w_hi, grad) + tn(w_lo, grad)
            scaled_up = side_ref[t, low : rows - rank, :].astype(f32)
            acc[0 : rank * j, :] += inverse_rms(t) * (term[low : rows - rank, :] - mean * scaled_up)

    grad = acc[0:rank, :].astype(bf16)
    low_ref[...] = grad
    irms = inverse_rms(me)
    mean = mean_of(grad, me)
    lrt_f = side_ref[:, rows : rows + rank, :].reshape(layers * rank, -1).astype(f32)
    layer = lax.broadcasted_iota(jnp.int32, lrt_f.shape, 0) // rank
    lrt_ref[...] = jnp.where(layer <= me, lrt_f, 0.0).astype(bf16)
    below = jnp.where(layer < me, lrt_f, 0.0)
    coef_ref[...] = (below * (-irms * irms * mean)).astype(bf16)
    k_hi, k_lo = split2(nt(below.astype(bf16), (grad.astype(f32) * irms).astype(bf16)))
    k_ref[0] = k_hi
    k_ref[1] = k_lo


def part(start, loads, low, lrt, coef, k, own_in, stream_in, normed_in, dg_in, out_ref, buffer, out_sem):
    chunks, _, chunk = buffer.shape
    rows = lrt.shape[0]
    group = chunks // len(loads)
    width = group * chunk
    left = jnp.concatenate([lrt, coef], axis=1)
    k_hi, k_lo = k[0].astype(f32), k[1].astype(f32)
    k = jnp.concatenate([k_hi, k_hi, k_lo], axis=1).astype(bf16)
    stores = []
    for i, piece in enumerate(loads):
        for load in piece:
            load.wait()
        columns = pl.ds(pl.multiple_of(start + i * width, width), width)
        right = jnp.concatenate([own_in[1][:, columns], stream_in[1][:, columns]], axis=0)
        dg_hi = dg_in[1][0, :, columns]
        dg = jnp.concatenate([dg_hi, dg_in[1][1, :, columns], dg_hi], axis=0)
        up = nn(left, right) + nn(k, dg)
        down = nn(low, normed_in[1][:, columns])
        for j in range(group):
            buffer[i * group + j, :rows, :] = up[:, j * chunk : (j + 1) * chunk]
            buffer[i * group + j, rows:, :] = down[:, j * chunk : (j + 1) * chunk]
        here = pl.ds(i * group, group)
        stores.append(pltpu.make_async_copy(buffer.at[here], out_ref.at[here], out_sem.at[i]))
        stores[-1].start()
    for store in stores:
        store.wait()


def part_loads(start, large, chunks, chunk):
    pieces = min(4, chunks)
    width = chunks // pieces * chunk
    return [
        [columns_piece(item, i, pl.multiple_of(start + i * width, width), width) for item in large]
        for i in range(pieces)
    ]


def given_kernel(rank, meta_ref, side_in, *refs):
    large, (out_ref, low_ref, lrt_ref, coef_ref, k_ref, acc, buffer, out_sem) = refs[:4], refs[4:]
    start, me = meta_ref[0], meta_ref[1]
    loads = part_loads(start, large, buffer.shape[0], buffer.shape[2])
    whole(side_in).start()
    for load in loads:
        for item in load:
            item.start()
    whole(side_in).wait()
    solve(large[0][0].shape[1], rank, me, side_in[1], low_ref, lrt_ref, coef_ref, k_ref, acc)
    part(start, loads, low_ref[...], lrt_ref[...], coef_ref[...], k_ref, *large, out_ref, buffer, out_sem)


def kept_kernel(meta_ref, low_in, lrt_in, coef_in, k_in, *refs):
    large, (out_ref, buffer, out_sem) = refs[:4], refs[4:]
    start = meta_ref[0]
    loads = part_loads(start, large, buffer.shape[0], buffer.shape[2])
    for item in (low_in, lrt_in, coef_in, k_in):
        whole(item).start()
    for load in loads:
        for item in load:
            item.start()
    for item in (low_in, lrt_in, coef_in, k_in):
        whole(item).wait()
    part(start, loads, low_in[1][...], lrt_in[1][...], coef_in[1][...], k_in[1], *large, out_ref, buffer, out_sem)


def part_shapes(chunks, chunk, rows, rank):
    shape = (chunks, rows + rank, chunk)
    return jax.ShapeDtypeStruct(shape, f32), (pltpu.VMEM(shape, f32), pltpu.SemaphoreType.DMA((4,)))


def given_part(meta, chunks, chunk, rank, sides, *large):
    layers, _, tokens = sides.shape
    rows = layers * rank
    shape, scratch = part_shapes(chunks, chunk, rows, rank)
    return call(
        functools.partial(given_kernel, rank),
        "given",
        (
            shape,
            jax.ShapeDtypeStruct((rank, tokens), bf16),
            jax.ShapeDtypeStruct((rows, tokens), bf16),
            jax.ShapeDtypeStruct((rows, tokens), bf16),
            jax.ShapeDtypeStruct((2, rows, rank), bf16),
        ),
        (meta,),
        (sides, *large),
        (1,) + (4,) * 4,
        (pltpu.VMEM((rows, tokens), f32),)
        + scratch,
        in_place_outs=1,
    )


def kept_part(meta, chunks, chunk, low, lrt, coef, k, *large):
    shape, scratch = part_shapes(chunks, chunk, lrt.shape[0], low.shape[0])
    (found,) = call(
        kept_kernel,
        "kept",
        (shape,),
        (meta,),
        (low, lrt, coef, k, *large),
        (1,) * 4 + (4,) * 4,
        scratch,
        in_place_outs=1,
    )
    return found


def shards(
    layer_input_states,
    frozen_reference_states,
    adapter_down_weight,
    adapter_up_weight,
    layer_norm_gain,
    tile_reference_position,
    tile_harmful_flag,
    tile_valid_count,
):
    tokens, width = layer_input_states.shape[2:]
    rank = adapter_up_weight.shape[1]
    layers = lax.axis_size(SEC)
    me = lax.axis_index(SEC)
    core = lax.axis_index("core")
    cores = lax.axis_size("core")
    chips = lax.axis_size("y") * lax.axis_size("x")
    half = width // cores
    chunk = half // chips
    swap = [(i, (i + 1) % cores) for i in range(cores)]

    meta = jnp.stack([core, tile_harmful_flag[0], tile_valid_count[0]]).astype(jnp.int32)
    up_half = lax.dynamic_slice_in_dim(adapter_up_weight[0], core * half, half, axis=1)
    up_half, position = lax.optimization_barrier((up_half, tile_reference_position))
    ordered = order(position, meta, frozen_reference_states[0])
    refs = lax.all_to_all(ordered, DP, split_axis=0, concat_axis=0, tiled=True)
    _, stream, down, up, gains = lax.optimization_barrier(
        (ordered, layer_input_states[0, 0], adapter_down_weight[0], adapter_up_weight[0], layer_norm_gain)
    )

    normed, lrt, irms, dg = forward(stream, down, gains)
    mine = ring_gather(up_half, SEC, lrt)[::-1]
    other = [lax.ppermute(block, "core", swap) for block in mine]

    own, side = own_gradient(meta, refs, stream, up, lrt, dg, irms, mine, other)
    sides = lax.all_to_all(side, SEC, 0, 0, tiled=True)

    large = (own, stream, normed, dg)
    away = jnp.stack([(1 - core) * half, me]).astype(jnp.int32)
    here = (core * half)[None].astype(jnp.int32)
    given, *coefs = given_part(away, chips, chunk, rank, sides, *large)
    received = lax.ppermute(given, "core", swap)
    kept = kept_part(here, chips, chunk, *coefs, *large)
    blocks = lax.all_to_all((kept + received).astype(bf16), CHIPS, 0, 0, tiled=True)
    grad_up = jnp.sum(blocks[:, : layers * rank].astype(f32), axis=0)
    grad_down = jnp.sum(blocks[:, layers * rank :].astype(f32), axis=0)

    by_layer = lax.all_to_all(grad_up.reshape(layers, rank, chunk), SEC, 0, 0, tiled=True)
    final = jnp.concatenate([grad_down, jnp.sum(by_layer, axis=0)], axis=0)
    wide = lax.all_to_all(jnp.broadcast_to(final, (chips,) + final.shape), CHIPS, 0, 0, tiled=True)
    mine = wide.transpose(1, 0, 2).reshape(2 * rank, half)
    other = lax.ppermute(mine, "core", swap)
    full = jnp.concatenate([jnp.where(core == 0, mine, other), jnp.where(core == 0, other, mine)], axis=1)
    return (full[None, :rank], full[None, rank:])


def solution(mesh):
    layers, dp = mesh.devices.shape
    cores = 2
    side = round((dp // cores) ** 0.5)
    mesh4 = Mesh(mesh.devices.reshape(layers, side, side, cores), (SEC,) + DP)
    return jax.shard_map(
        shards,
        mesh=mesh4,
        in_specs=(
            P(SEC, DP, None, None),
            P(SEC, None, None, DP),
            P(SEC, None, None),
            P(SEC, None, None),
            P(SEC, None),
            P(),
            P(DP),
            P(DP),
        ),
        out_specs=(P(SEC, None, None), P(SEC, None, None)),
        check_vma=False,
    )
```

```python
import functools

import jax
import jax.numpy as jnp
from jax import lax
from jax.experimental import pallas as pl
from jax.experimental.pallas import tpu as pltpu
from jax.sharding import Mesh
from jax.sharding import PartitionSpec as P

norm_eps = 1e-05
stat_eps = 1e-06
coef_reroute = 64.0
coef_retain = 1.0
loss_scale = 2048.0

SEC = "section"
CHIPS = ("y", "x")
DP = ("y", "x", "core")
f32 = jnp.float32
bf16 = jnp.bfloat16


def nt(left, right):
    return lax.dot_general(left, right, (((1,), (1,)), ((), ())), preferred_element_type=f32)


def tn(left, right):
    return lax.dot_general(left, right, (((0,), (0,)), ((), ())), preferred_element_type=f32)


def nn(left, right):
    return lax.dot_general(left, right, (((1,), (0,)), ((), ())), preferred_element_type=f32)


def split2(value):
    hi = value.astype(bf16)
    lo = (value - hi.astype(f32)).astype(bf16)
    return hi, lo


def ring_gather(block, axis, gate):
    n = lax.axis_size(axis)
    up = [(i, (i + 1) % n) for i in range(n)]
    down = [(i, (i - 1) % n) for i in range(n)]
    found = [None] * n
    found[0] = block
    fwd = bwd = block
    for k in range(1, n // 2 + 1):
        fwd = lax.ppermute(fwd, axis, up)
        found[k] = fwd
        if k < n - n // 2:
            bwd = lax.ppermute(bwd, axis, down)
            found[n - k] = bwd
        if k == 1:
            fwd, bwd, _ = lax.optimization_barrier((fwd, bwd, gate))
            found[1], found[n - 1] = fwd, bwd
    return found


def params(mib=63):
    return pltpu.CompilerParams(vmem_limit_bytes=mib << 20)


def smem():
    return pl.BlockSpec(memory_space=pltpu.SMEM)


def in_place():
    return pl.BlockSpec(memory_space=pl.ANY)


def vmem():
    return pl.BlockSpec(memory_space=pltpu.VMEM)


def call(kernel, name, out_shape, scalars, arrays, pieces, scratch=(), in_place_outs=0):
    count, total = len(scalars), len(arrays)
    outs = len(out_shape)
    buffered = [(a, n) for a, n in zip(arrays, pieces, strict=True) if n]

    def body(*refs):
        held = refs[count : count + total]
        first = count + total + outs
        buffers = iter(refs[first : first + len(buffered)])
        sems = iter(refs[first + len(buffered) : first + 2 * len(buffered)])
        inputs = [(h, next(buffers), next(sems)) if n else h for h, n in zip(held, pieces)]
        kernel(*refs[:count], *inputs, *refs[count + total : first], *refs[first + 2 * len(buffered) :])

    return pl.pallas_call(
        body,
        out_shape=out_shape,
        in_specs=[smem()] * count + [in_place()] * total,
        out_specs=[in_place()] * in_place_outs + [vmem()] * (outs - in_place_outs),
        scratch_shapes=[pltpu.VMEM(a.shape, a.dtype) for a, _ in buffered]
        + [pltpu.SemaphoreType.DMA((n,)) for _, n in buffered]
        + list(scratch),
        compiler_params=params(),
        cost_estimate=pl.CostEstimate(flops=COST[name] * 10**9, bytes_accessed=COST[name] * 3 * 10**6, transcendentals=0),
        name=name,
    )(*scalars, *arrays)


PIECES = 8
COST = dict(forward=4, own=8, given=5, kept=4)


def gather_into(blocks, buffer, sem):
    rows = blocks[0].shape[0]
    for i, block in enumerate(blocks):
        pltpu.make_async_copy(block, buffer.at[pl.ds(i * rows, rows)], sem).start()
    return pltpu.make_async_copy(buffer, buffer, sem)


def whole(item):
    held, buffer, sem = item
    return pltpu.make_async_copy(held, buffer, sem.at[0])


def columns_piece(item, i, start, width):
    held, buffer, sem = item
    where = (slice(None),) * (len(held.shape) - 1) + (pl.ds(start, width),)
    return pltpu.make_async_copy(held.at[where], buffer.at[where], sem.at[i])


def leading_piece(item, i, start, count):
    held, buffer, sem = item
    return pltpu.make_async_copy(held.at[pl.ds(start, count)], buffer.at[pl.ds(start, count)], sem.at[i])


INFO = 8


def order_kernel(position_ref, meta_ref, held_ref, out_ref, buffer, in_sem, out_sem):
    tiles, tokens, width = held_ref.shape
    groups = in_sem.shape[0]
    group = tiles // groups
    for i in range(tiles):
        pltpu.make_async_copy(
            held_ref.at[position_ref[i]], buffer.at[i, pl.ds(0, tokens)], in_sem.at[i // group]
        ).start()
    flag, valid = meta_ref[1], meta_ref[2]
    row = lax.broadcasted_iota(jnp.int32, (INFO, width), 0)
    here = ((row == 0) & (flag == 1)) | ((row == 1) & (flag != 1))
    info = jnp.where(here, valid, 0).astype(f32).astype(bf16)
    for i in range(tiles):
        buffer[i, tokens:, :] = info
    stores = []
    for i in range(groups):
        part = pl.ds(i * group, group)
        landed = buffer.at[part, pl.ds(0, tokens)]
        pltpu.make_async_copy(landed, landed, in_sem.at[i]).wait()
        stores.append(pltpu.make_async_copy(buffer.at[part], out_ref.at[part], out_sem.at[i]))
        stores[-1].start()
    for store in stores:
        store.wait()


def order(position, meta, held):
    tiles, tokens, width = held.shape
    shape = (tiles, tokens + INFO, width)
    return pl.pallas_call(
        order_kernel,
        out_shape=jax.ShapeDtypeStruct(shape, held.dtype),
        in_specs=[smem(), smem(), in_place()],
        out_specs=in_place(),
        scratch_shapes=[
            pltpu.VMEM(shape, held.dtype),
            pltpu.SemaphoreType.DMA((4,)),
            pltpu.SemaphoreType.DMA((4,)),
        ],
        compiler_params=params(),
        name="order",
    )(position, meta, held)


def fold(value):
    lanes = 128
    total = value[:, :lanes]
    for i in range(1, value.shape[1] // lanes):
        total = total + value[:, i * lanes : (i + 1) * lanes]
    return total


def forward_kernel(stream_in, down_in, gain_in, normed_ref, lrt_ref, irms_ref, dg_ref):
    stream_ref, down_ref, gain_ref = stream_in[1], down_in[1], gain_in[1]
    tokens, width = stream_ref.shape
    piece = width // PIECES
    loads = [columns_piece(stream_in, i, i * piece, piece) for i in range(PIECES)]
    for load in loads:
        load.start()
    whole(down_in).start()
    whole(gain_in).start()
    total = jnp.zeros((tokens, 128), f32)
    for i in range(PIECES):
        loads[i].wait()
        for low in range(i * piece, (i + 1) * piece, 256):
            x = stream_ref[:, low : low + 256].astype(f32)
            total = total + fold(x * x)
    irms = lax.rsqrt(jnp.sum(total, axis=1, keepdims=True) * (1.0 / width) + norm_eps)
    irms_ref[...] = jnp.broadcast_to(irms, (tokens, 128)).T[:8, :]
    whole(down_in).wait()
    whole(gain_in).wait()
    chunk = min(512, piece)

    def norm(i, acc):
        columns = pl.ds(pl.multiple_of(i * chunk, chunk), chunk)
        gain = gain_ref[:, columns]
        normed = (stream_ref[:, columns].astype(f32) * irms * gain).astype(bf16)
        normed_ref[:, columns] = normed
        down = down_ref[:, columns]
        hi, lo = split2(down.astype(f32) * gain)
        dg_ref[0, :, columns] = hi
        dg_ref[1, :, columns] = lo
        return acc + nt(down, normed)

    rank = down_ref.shape[0]
    low_rank = lax.fori_loop(0, width // chunk, norm, jnp.zeros((rank, tokens), f32), unroll=2)
    lrt_ref[...] = low_rank.astype(bf16)


def forward(stream, down, gain):
    rank = down.shape[0]
    tokens, width = stream.shape
    return call(
        forward_kernel,
        "forward",
        (
            jax.ShapeDtypeStruct((tokens, width), bf16),
            jax.ShapeDtypeStruct((rank, tokens), bf16),
            jax.ShapeDtypeStruct((8, tokens), f32),
            jax.ShapeDtypeStruct((2, rank, width), bf16),
        ),
        (),
        (stream, down, gain),
        (PIECES, 1, 1),
    )


def up_scratch(mine):
    rank, half = mine[0].shape
    return (pltpu.VMEM((2, len(mine) * rank, half), bf16), pltpu.SemaphoreType.DMA((2,)))


def own_kernel(count, meta_ref, refs_in, stream_in, up_in, lrt_in, dg_in, irms_in, *refs):
    mine, other = refs[:count], refs[count : 2 * count]
    own_ref, out_ref, output_ref, ups_ref, up_sem = refs[2 * count :]
    rank = lrt_in[1].shape[0]
    rows = count * rank
    dg_ref = dg_in[1]
    core, flag, valid = meta_ref[0], meta_ref[1], meta_ref[2]
    refs_ref, stream_ref, up_ref = refs_in[1], stream_in[1], up_in[1]
    tiles, padded, chunk = refs_ref.shape
    tokens = padded - INFO
    half = mine[0].shape[1]
    per_half = half // chunk
    per_piece = tiles // PIECES
    width = per_piece * chunk

    whole(lrt_in).start()
    whole(up_in).start()
    stream_loads = [columns_piece(stream_in, i, i * width, width) for i in range(PIECES)]
    ref_loads = [leading_piece(refs_in, i, i * per_piece, per_piece) for i in range(PIECES)]
    for i in range(PIECES):
        stream_loads[i].start()
        ref_loads[i].start()
    ready = [gather_into(blocks, ups_ref.at[i], up_sem.at[i]) for i, blocks in enumerate((mine, other))]
    for item in (dg_in, irms_in):
        whole(item).start()
        ready.append(whole(item))
    whole(lrt_in).wait()
    whole(up_in).wait()
    low_rank = lrt_in[1][...].astype(f32).T.astype(bf16)
    is_valid = lax.broadcasted_iota(jnp.int32, (tokens, 1), 0) < valid

    def weight(row):
        info = refs_ref[0, tokens:, :128].astype(f32)
        for i in range(1, tiles):
            info = info + refs_ref[i, tokens:, :128].astype(f32)
        return loss_scale / info[row : row + 1, 0:1]

    def stats(terms, number):
        acc = [jnp.zeros((tokens, 128), f32) for _ in range(number)]
        for i in range(PIECES):
            stream_loads[i].wait()
            ref_loads[i].wait()
            for j in range(i * per_piece, (i + 1) * per_piece):
                columns = slice(j * chunk, (j + 1) * chunk)
                out = stream_ref[:, columns].astype(f32) + nn(low_rank, up_ref[:, columns])
                output_ref[:, columns] = out
                ref = refs_ref[j, :tokens, :].astype(f32)
                acc = [a + fold(v) for a, v in zip(acc, terms(out, ref))]
        return [jnp.sum(a, axis=1, keepdims=True) for a in acc]

    group = min(4, per_half)

    def finish(make):
        for wait in ready:
            wait.wait()
        total = jnp.zeros((rows, 2 * tokens + 2 * rank), f32)
        for which, base in enumerate((core, 1 - core)):

            def step(i, acc, which=which, base=base):
                parts = []
                for g in range(group):
                    j = base * per_half + i * group + g
                    columns = pl.ds(pl.multiple_of(j * chunk, chunk), chunk)
                    own = make(output_ref[:, columns], refs_ref[j, :tokens, :].astype(f32)).astype(bf16)
                    own_ref[:, columns] = own
                    parts.append(own)
                size = group * chunk
                local = pl.ds(pl.multiple_of(i * size, size), size)
                columns = pl.ds(pl.multiple_of(base * half + i * size, size), size)
                right = [jnp.concatenate(parts, axis=1), stream_ref[:, columns], dg_ref[0, :, columns], dg_ref[1, :, columns]]
                return acc + nt(ups_ref[which, :, local], jnp.concatenate(right, axis=0))

            total = lax.fori_loop(0, per_half // group, step, total, unroll=2)

        irms = irms_in[1][0:1, :]
        own_up = total[:, :tokens].astype(bf16)
        scaled_up = (total[:, tokens : 2 * tokens] * irms).astype(bf16)
        w = total[:, 2 * tokens : 2 * tokens + rank] + total[:, 2 * tokens + rank :]
        w = jnp.concatenate([w, jnp.zeros((rows, 128 - rank), f32)], axis=1).T[:rank, :]
        w_hi, w_lo = split2(w)
        irms_hi = irms.astype(bf16).astype(f32)
        row = lax.broadcasted_iota(jnp.int32, (8, tokens), 0)
        last = jnp.where(row == 0, irms_hi, jnp.where(row == 1, irms - irms_hi, 0.0)).astype(bf16)
        for i in range(out_ref.shape[0]):
            low = 0
            for value in (scaled_up[: rows - rank], lrt_in[1][...], w_hi, w_lo, own_up, last):
                out_ref[i, low : low + value.shape[0], :] = value
                low += value.shape[0]

    @pl.when(flag == 1)
    def _():
        out_sq, ref_sq, cross = stats(lambda o, r: (o * o, r * r, o * r), 3)
        out_norm = jnp.sqrt(out_sq + stat_eps)
        ref_norm = jnp.sqrt(ref_sq + stat_eps)
        cosine = cross / (out_norm * ref_norm)
        on = jnp.where(is_valid & (cosine > 0), coef_reroute * weight(0), 0.0)
        coef_ref = on / (out_norm * ref_norm)
        coef_out = on * cosine / (out_sq + stat_eps)
        finish(lambda o, r: coef_ref * r - coef_out * o)

    @pl.when(flag != 1)
    def _():
        (diff_sq,) = stats(lambda o, r: ((o - r) * (o - r),), 1)
        coef = jnp.where(is_valid, coef_retain * weight(1), 0.0) / jnp.sqrt(diff_sq + stat_eps)
        finish(lambda o, r: coef * (o - r))


def own_gradient(meta, refs, stream, up, lrt, dg, irms, mine, other):
    layers = len(mine)
    rank = up.shape[0]
    return call(
        functools.partial(own_kernel, layers),
        "own",
        (
            jax.ShapeDtypeStruct(stream.shape, bf16),
            jax.ShapeDtypeStruct((layers, (2 * layers + 2) * rank + 8, stream.shape[0]), bf16),
        ),
        (meta,),
        (refs, stream, up, lrt, dg, irms, *mine, *other),
        (PIECES, PIECES, 1, 1, 1, 1) + (0,) * (2 * layers),
        (pltpu.VMEM(stream.shape, f32),) + up_scratch(mine),
    )


def solve(width, rank, me, side_ref, low_ref, lrt_ref, coef_ref, k_ref, acc):
    layers = side_ref.shape[0]
    rows = layers * rank
    side = rows - rank
    first = side + 3 * rank
    last = first + rows
    acc[...] = jnp.zeros_like(acc)
    for j in range(layers):

        @pl.when(me + j < layers)
        def _(j=j):
            low = rank * (layers - 1 - j)
            acc[0 : rank * (j + 1), :] += side_ref[me + j, first + low : first + rows, :].astype(f32)

    def inverse_rms(t):
        hi = side_ref[t, last : last + 1, :].astype(f32)
        return hi + side_ref[t, last + 1 : last + 2, :].astype(f32)

    def mean_of(grad, t):
        lrt = side_ref[t, side : side + rank, :].astype(f32)
        return jnp.sum(grad.astype(f32) * lrt, axis=0, keepdims=True) * (1.0 / width)

    for j in range(layers - 1, 0, -1):

        @pl.when(me + j < layers)
        def _(j=j):
            t = me + j
            low = rank * (layers - 1 - j)
            grad = acc[rank * j : rank * (j + 1), :].astype(bf16)
            mean = mean_of(grad, t)
            w_hi = side_ref[t, side + rank : side + 2 * rank, :]
            w_lo = side_ref[t, side + 2 * rank : side + 3 * rank, :]
            term = tn(w_hi, grad) + tn(w_lo, grad)
            scaled_up = side_ref[t, low : rows - rank, :].astype(f32)
            acc[0 : rank * j, :] += inverse_rms(t) * (term[low : rows - rank, :] - mean * scaled_up)

    grad = acc[0:rank, :].astype(bf16)
    low_ref[...] = grad
    irms = inverse_rms(me)
    mean = mean_of(grad, me)
    lrt_f = side_ref[:, side : side + rank, :].reshape(layers * rank, -1).astype(f32)
    layer = lax.broadcasted_iota(jnp.int32, lrt_f.shape, 0) // rank
    lrt_ref[...] = jnp.where(layer <= me, lrt_f, 0.0).astype(bf16)
    below = jnp.where(layer < me, lrt_f, 0.0)
    coef_ref[...] = (below * (-irms * irms * mean)).astype(bf16)
    k_hi, k_lo = split2(nt(below.astype(bf16), (grad.astype(f32) * irms).astype(bf16)))
    k_ref[0] = k_hi
    k_ref[1] = k_lo


def part(start, loads, low, lrt, coef, k, own_in, stream_in, normed_in, dg_in, out_ref, buffer, out_sem):
    chunks, _, chunk = buffer.shape
    rows = lrt.shape[0]
    group = chunks // len(loads)
    width = group * chunk
    left = jnp.concatenate([lrt, coef], axis=1)
    k_hi, k_lo = k[0].astype(f32), k[1].astype(f32)
    k = jnp.concatenate([k_hi, k_hi, k_lo], axis=1).astype(bf16)
    stores = []
    for i, piece in enumerate(loads):
        for load in piece:
            load.wait()
        columns = pl.ds(pl.multiple_of(start + i * width, width), width)
        right = jnp.concatenate([own_in[1][:, columns], stream_in[1][:, columns]], axis=0)
        dg_hi = dg_in[1][0, :, columns]
        dg = jnp.concatenate([dg_hi, dg_in[1][1, :, columns], dg_hi], axis=0)
        up = nn(left, right) + nn(k, dg)
        down = nn(low, normed_in[1][:, columns])
        for j in range(group):
            buffer[i * group + j, :rows, :] = up[:, j * chunk : (j + 1) * chunk]
            buffer[i * group + j, rows:, :] = down[:, j * chunk : (j + 1) * chunk]
        here = pl.ds(i * group, group)
        stores.append(pltpu.make_async_copy(buffer.at[here], out_ref.at[here], out_sem.at[i]))
        stores[-1].start()
    for store in stores:
        store.wait()


def part_loads(start, large, chunks, chunk):
    pieces = min(4, chunks)
    width = chunks // pieces * chunk
    return [
        [columns_piece(item, i, pl.multiple_of(start + i * width, width), width) for item in large]
        for i in range(pieces)
    ]


def given_kernel(rank, meta_ref, side_in, *refs):
    large, (out_ref, low_ref, lrt_ref, coef_ref, k_ref, acc, buffer, out_sem) = refs[:4], refs[4:]
    start, me = meta_ref[0], meta_ref[1]
    loads = part_loads(start, large, buffer.shape[0], buffer.shape[2])
    whole(side_in).start()
    for load in loads:
        for item in load:
            item.start()
    whole(side_in).wait()
    solve(large[0][0].shape[1], rank, me, side_in[1], low_ref, lrt_ref, coef_ref, k_ref, acc)
    part(start, loads, low_ref[...], lrt_ref[...], coef_ref[...], k_ref, *large, out_ref, buffer, out_sem)


def kept_kernel(meta_ref, low_in, lrt_in, coef_in, k_in, *refs):
    large, (out_ref, buffer, out_sem) = refs[:4], refs[4:]
    start = meta_ref[0]
    loads = part_loads(start, large, buffer.shape[0], buffer.shape[2])
    for item in (low_in, lrt_in, coef_in, k_in):
        whole(item).start()
    for load in loads:
        for item in load:
            item.start()
    for item in (low_in, lrt_in, coef_in, k_in):
        whole(item).wait()
    part(start, loads, low_in[1][...], lrt_in[1][...], coef_in[1][...], k_in[1], *large, out_ref, buffer, out_sem)


def part_shapes(chunks, chunk, rows, rank):
    shape = (chunks, rows + rank, chunk)
    return jax.ShapeDtypeStruct(shape, f32), (pltpu.VMEM(shape, f32), pltpu.SemaphoreType.DMA((4,)))


def given_part(meta, chunks, chunk, rank, sides, *large):
    layers, _, tokens = sides.shape
    rows = layers * rank
    shape, scratch = part_shapes(chunks, chunk, rows, rank)
    return call(
        functools.partial(given_kernel, rank),
        "given",
        (
            shape,
            jax.ShapeDtypeStruct((rank, tokens), bf16),
            jax.ShapeDtypeStruct((rows, tokens), bf16),
            jax.ShapeDtypeStruct((rows, tokens), bf16),
            jax.ShapeDtypeStruct((2, rows, rank), bf16),
        ),
        (meta,),
        (sides, *large),
        (1,) + (4,) * 4,
        (pltpu.VMEM((rows, tokens), f32),)
        + scratch,
        in_place_outs=1,
    )


def kept_part(meta, chunks, chunk, low, lrt, coef, k, *large):
    shape, scratch = part_shapes(chunks, chunk, lrt.shape[0], low.shape[0])
    (found,) = call(
        kept_kernel,
        "kept",
        (shape,),
        (meta,),
        (low, lrt, coef, k, *large),
        (1,) * 4 + (4,) * 4,
        scratch,
        in_place_outs=1,
    )
    return found


def shards(
    layer_input_states,
    frozen_reference_states,
    adapter_down_weight,
    adapter_up_weight,
    layer_norm_gain,
    tile_reference_position,
    tile_harmful_flag,
    tile_valid_count,
):
    tokens, width = layer_input_states.shape[2:]
    rank = adapter_up_weight.shape[1]
    layers = lax.axis_size(SEC)
    me = lax.axis_index(SEC)
    core = lax.axis_index("core")
    cores = lax.axis_size("core")
    chips = lax.axis_size("y") * lax.axis_size("x")
    half = width // cores
    chunk = half // chips
    swap = [(i, (i + 1) % cores) for i in range(cores)]

    meta = jnp.stack([core, tile_harmful_flag[0], tile_valid_count[0]]).astype(jnp.int32)
    up_half = lax.dynamic_slice_in_dim(adapter_up_weight[0], core * half, half, axis=1)
    up_half, position = lax.optimization_barrier((up_half, tile_reference_position))
    ordered = order(position, meta, frozen_reference_states[0])
    refs = lax.all_to_all(ordered, DP, split_axis=0, concat_axis=0, tiled=True)
    _, stream, down, up, gains = lax.optimization_barrier(
        (ordered, layer_input_states[0, 0], adapter_down_weight[0], adapter_up_weight[0], layer_norm_gain)
    )

    normed, lrt, irms, dg = forward(stream, down, gains)
    mine = ring_gather(up_half, SEC, lrt)[::-1]
    other = [lax.ppermute(block, "core", swap) for block in mine]

    own, side = own_gradient(meta, refs, stream, up, lrt, dg, irms, mine, other)
    sides = lax.all_to_all(side, SEC, 0, 0, tiled=True)

    large = (own, stream, normed, dg)
    away = jnp.stack([(1 - core) * half, me]).astype(jnp.int32)
    here = (core * half)[None].astype(jnp.int32)
    given, *coefs = given_part(away, chips, chunk, rank, sides, *large)
    received = lax.ppermute(given, "core", swap)
    kept = kept_part(here, chips, chunk, *coefs, *large)
    blocks = lax.all_to_all((kept + received).astype(bf16), CHIPS, 0, 0, tiled=True)
    grad_up = jnp.sum(blocks[:, : layers * rank].astype(f32), axis=0)
    grad_down = jnp.sum(blocks[:, layers * rank :].astype(f32), axis=0)

    by_layer = lax.all_to_all(grad_up.reshape(layers, rank, chunk), SEC, 0, 0, tiled=True)
    final = jnp.concatenate([grad_down, jnp.sum(by_layer, axis=0)], axis=0)
    wide = lax.all_to_all(jnp.broadcast_to(final, (chips,) + final.shape), CHIPS, 0, 0, tiled=True)
    mine = wide.transpose(1, 0, 2).reshape(2 * rank, half)
    other = lax.ppermute(mine, "core", swap)
    full = jnp.concatenate([jnp.where(core == 0, mine, other), jnp.where(core == 0, other, mine)], axis=1)
    return (full[None, :rank], full[None, rank:])


def solution(mesh):
    layers, dp = mesh.devices.shape
    cores = 2
    side = round((dp // cores) ** 0.5)
    mesh4 = Mesh(mesh.devices.reshape(layers, side, side, cores), (SEC,) + DP)
    return jax.shard_map(
        shards,
        mesh=mesh4,
        in_specs=(
            P(SEC, DP, None, None),
            P(SEC, None, None, DP),
            P(SEC, None, None),
            P(SEC, None, None),
            P(SEC, None),
            P(),
            P(DP),
            P(DP),
        ),
        out_specs=(P(SEC, None, None), P(SEC, None, None)),
        check_vma=False,
    )
```
